128 devices in a mesh: ctx: 64 (over y_lo, x, z, core), tp: 2 (over y_hi).
Axes of the slice: x: 4, y: 4 (y_hi: 2, y_lo: 2; y = y_hi * 2 + y_lo), z: 4, core: 2. Of those that a mesh axis runs over, the one named last changes fastest.
Arguments:
- inputs: bfloat16 [3, 8192, 4096], P(None, 'ctx', 'tp'), may hold values from -6 to 6
- short_weight: float32 [3, 3, 4096], P(None, None, 'tp'), may hold values from -3 to 3
- taps: float32 [8192, 4096], P('ctx', 'tp'), may hold values from -6 to 6
- w_out: bfloat16 [4096, 4096], P('tp'), may hold values from -0.09375 to 0.09375
- grad_out: bfloat16 [8192, 4096], P('ctx', 'tp'), may hold values from -6 to 6
Outputs:
- inputs_grad: bfloat16 [3, 8192, 4096], P(None, 'ctx', 'tp')
- taps_grad: float32 [8192, 4096], P('ctx', 'tp')
- short_grad: float32 [3, 3, 4096], P(None, None, 'tp')
The draws below stay inside these ranges and needn't reach their ends.
All inputs are finite; a program needn't handle non-finite values.
Results may differ from the reference program's by a relative error of at most 0.0015.
Values may be sent and summed in bfloat16 or wider, within the bound.
No kernel may reach another device: no remote copies, remote signals or barrier semaphores. Data moves between devices by JAX's collectives and lax.ppermute only.
A program may use at most 192 MiB of HBM per device.

```python
import math
import jax
import jax.numpy as jnp
from jax import lax

D = 4096
SHORT = 3
SEQ = 8192


def levels(own_key, shape, pieces, low, largest):
    level, own = 1.0, jax.random.fold_in(own_key, 6)
    for position, blocks in pieces:
        draws = jnp.exp(jax.random.uniform(jax.random.fold_in(own, position), (blocks,), jnp.float32, low / len(pieces), largest / len(pieces)))
        level = level * jnp.repeat(draws, shape[position] // blocks).reshape([-1 if axis == position else 1 for axis in range(len(shape))])
    return level


def gaussian(rng, shape, scale, bound, shards=(), kind=jnp.bfloat16):
    loudness = levels(rng, shape, shards, -0.22, 0.18) if shards else 1.0
    drawn = jax.random.normal(rng, shape, jnp.float32) * scale * loudness
    return jnp.minimum(jnp.maximum(drawn, -bound), bound).astype(kind)


def setup_inputs(seed: int = 0) -> dict:
    splits = jax.random.split(jax.random.key(seed), 6)
    inputs = gaussian(splits[0], (3, SEQ, D), 1.0, 6.0, ((1, 64), (2, 2)))
    short_weight = gaussian(splits[1], (3, SHORT, D), 0.6, 3.0, ((2, 2),), jnp.float32)
    taps = gaussian(splits[2], (SEQ, D), 1.0, 6.0, ((0, 64), (1, 2)), jnp.float32)
    w_out = gaussian(splits[3], (D, D), D ** -0.5, 0.09375, ((0, 2),))
    grad_out = gaussian(splits[4], (SEQ, D), 1.0, 6.0, ((0, 64), (1, 2)))
    return dict(inputs=inputs, short_weight=short_weight, taps=taps, w_out=w_out, grad_out=grad_out)


def causal_mix(streams, weight):
    length = streams.shape[1]
    span = weight.shape[1]
    padded = jnp.concatenate([jnp.zeros_like(streams[:, :span - 1]), streams], axis=1)
    total = jnp.zeros_like(streams)
    for j in range(span):
        total = total + weight[:, j][:, None, :] * padded[:, span - 1 - j:span - 1 - j + length]
    return (total, padded)

def spectral_block(block):
    length = block.shape[1]
    spec = jnp.fft.rfft(block, n=2 * length, axis=1)
    filt, prod, grad = (spec[0], spec[1], spec[2])
    joined = jnp.stack([filt * prod, jnp.conj(filt) * grad, jnp.conj(prod) * grad])
    return jnp.fft.irfft(joined, n=2 * length, axis=1)[:, :length]

def reference(inputs, short_weight, taps, w_out, grad_out):
    scale = 1.0 / math.sqrt(SEQ)
    streams = inputs.astype(jnp.float32)
    mixed, padded = causal_mix(streams, short_weight)
    query, key_s, value = (mixed[0], mixed[1], mixed[2])
    product = key_s * value
    filt = taps * scale
    gated_grad = jnp.dot(grad_out, w_out.T, preferred_element_type=jnp.float32)
    dy = gated_grad * query
    width = min(256, D)
    stacked = jnp.stack([filt, product, dy]).reshape(3, SEQ, D // width, width).transpose(2, 0, 1, 3)
    result = lax.map(spectral_block, stacked)
    result = result.transpose(1, 2, 0, 3).reshape(3, SEQ, D)
    conv_out, dz, raw = (result[0], result[1], result[2])
    dmixed = jnp.stack([gated_grad * conv_out, dz * value, dz * key_s])
    span = SHORT
    dpad = jnp.concatenate([dmixed, jnp.zeros_like(dmixed[:, :span - 1])], axis=1)
    inputs_grad = jnp.zeros_like(dmixed)
    sums = []
    for j in range(span):
        inputs_grad = inputs_grad + short_weight[:, j][:, None, :] * dpad[:, j:j + SEQ]
        sums.append(lax.optimization_barrier(jnp.sum(dmixed * padded[:, span - 1 - j:span - 1 - j + SEQ], axis=1)))
    short_grad = jnp.stack(sums, axis=1) * scale
    return (inputs_grad.astype(jnp.bfloat16), raw * scale, short_grad)
```

```python
import math

import jax
import jax.numpy as jnp
import numpy as np
from jax import lax
from jax.experimental import pallas as pl
from jax.experimental.pallas import tpu as pltpu
from jax.sharding import PartitionSpec as P

GROUP = 4


def split_np(x):
    high = x.astype(jnp.bfloat16)
    low = (x - high.astype(np.float64)).astype(jnp.bfloat16)
    return high, low


def tables(blocks, width):
    length = 2 * blocks * width
    n1 = np.arange(blocks)
    n2 = np.arange(width)
    angle = 2.0 * np.pi * np.outer(n1 + 0.5, n1) / (2 * blocks)
    first = np.concatenate([np.cos(angle), -np.sin(angle)], axis=0)
    high, low = split_np(first)
    first3 = np.concatenate([high, high, low], axis=1)
    last = first.T * (2.0 / length)
    high, low = split_np(last)
    last4 = np.concatenate(
        [
            np.concatenate([high, high], axis=1),
            np.concatenate([low, np.zeros_like(low)], axis=1),
        ],
        axis=0,
    )
    angle = 2.0 * np.pi * (np.outer(n2, n2) % width) / width
    cos, sin = np.cos(angle), np.sin(angle)
    forward = np.block([[cos, -sin], [sin, cos]])
    high, low = split_np(forward)
    forward3 = np.concatenate([high, high, low], axis=0)
    backward = np.block([[cos, sin], [-sin, cos]])
    high, low = split_np(backward)
    backward3 = np.concatenate([high, high, low], axis=0)
    angle = 2.0 * np.pi * np.outer(n1 + 0.5, n2) / length
    twiddle = np.stack([np.cos(angle), np.sin(angle)]).astype(np.float32)
    return first3, last4, forward3, backward3, twiddle


def split(x):
    high = x.astype(jnp.bfloat16)
    low = (x - high.astype(jnp.float32)).astype(jnp.bfloat16)
    return high, low


def mm(a, b):
    return jnp.dot(a, b, preferred_element_type=jnp.float32)


def conv_kernel(
    scale,
    in_ref,
    taps_ref,
    grad_ref,
    weight_ref,
    first_ref,
    last_ref,
    forward_ref,
    backward_ref,
    twiddle_ref,
    ig_ref,
    tg_ref,
    sg_ref,
    src,
    res,
    key_ref,
    val_ref,
):
    blocks, _, chans, width = in_ref.shape
    lane = lax.broadcasted_iota(jnp.int32, (chans, width), 1)
    zero = jnp.zeros((chans, width), jnp.float32)

    def load(n1, b):
        cur = in_ref[n1, b].astype(jnp.float32)
        before = in_ref[jnp.maximum(n1 - 1, 0), b].astype(jnp.float32)
        before = jnp.where(n1 > 0, before, zero)
        return [cur] + [
            pltpu.roll(jnp.where(lane >= width - j, before, cur), j, 1) for j in (1, 2)
        ]

    def prepare(n1, carry):
        mixed = []
        for b in range(3):
            parts = load(n1, b)
            mixed.append(
                weight_ref[3 * b] * parts[0]
                + weight_ref[3 * b + 1] * parts[1]
                + weight_ref[3 * b + 2] * parts[2]
            )
        at = pl.ds(pl.multiple_of(n1 * chans, chans), chans)
        src[0, at, :] = taps_ref[n1] * scale
        src[1, at, :] = mixed[1] * mixed[2]
        src[2, at, :] = grad_ref[n1] * mixed[0]
        key_ref[at, :] = mixed[1]
        val_ref[at, :] = mixed[2]
        return carry

    lax.fori_loop(0, blocks, prepare, 0)

    cos, sin = twiddle_ref[0], twiddle_ref[1]

    def convolve(step, carry):
        base = step * GROUP
        rows = []
        for s in range(3):
            for g in range(0, GROUP, 2):
                cols = []
                for h in (0, 1):
                    x = src[s, pl.ds(base + g + h, blocks, stride=chans), :]
                    high, low = split(x)
                    cols.append(jnp.concatenate([high, low, high], axis=0))
                out = mm(first_ref[...], jnp.concatenate(cols, axis=1))
                for h in (0, 1):
                    re = out[:blocks, h * width : (h + 1) * width]
                    im = out[blocks:, h * width : (h + 1) * width]
                    rows.append(
                        jnp.concatenate([re * cos + im * sin, im * cos - re * sin], axis=1)
                    )
        high, low = split(jnp.concatenate(rows, axis=0))
        spec = mm(jnp.concatenate([high, low, high], axis=1), forward_ref[...])
        part = GROUP * blocks
        fr, fi = spec[:part, :width], spec[:part, width:]
        pr, pi = spec[part : 2 * part, :width], spec[part : 2 * part, width:]
        gr, gi = spec[2 * part :, :width], spec[2 * part :, width:]
        prod = jnp.concatenate(
            [
                jnp.concatenate([fr * pr - fi * pi, fr * pi + fi * pr], axis=1),
                jnp.concatenate([fr * gr + fi * gi, fr * gi - fi * gr], axis=1),
                jnp.concatenate([pr * gr + pi * gi, pr * gi - pi * gr], axis=1),
            ],
            axis=0,
        )
        high, low = split(prod)
        back = mm(jnp.concatenate([high, low, high], axis=1), backward_ref[...])
        for s in range(3):
            for g in range(0, GROUP, 2):
                cols = []
                for h in (0, 1):
                    at = (s * GROUP + g + h) * blocks
                    re = back[at : at + blocks, :width]
                    im = back[at : at + blocks, width:]
                    both = jnp.concatenate([re * cos - im * sin, re * sin + im * cos], axis=0)
                    high, low = split(both)
                    cols.append(jnp.concatenate([high, low], axis=0))
                out = mm(last_ref[...], jnp.concatenate(cols, axis=1))
                out = out[:blocks] + out[blocks:]
                for h in (0, 1):
                    res[s, pl.ds(base + g + h, blocks, stride=chans), :] = out[
                        :, h * width : (h + 1) * width
                    ]
        return carry

    lax.fori_loop(0, chans // GROUP, convolve, 0)

    def gradients(n1):
        at = pl.ds(pl.multiple_of(n1 * chans, chans), chans)
        dz = res[1, at, :]
        return grad_ref[n1] * res[0, at, :], dz * val_ref[at, :], dz * key_ref[at, :]

    sg_ref[...] = jnp.zeros_like(sg_ref)

    def finish(n1, cur):
        at = pl.ds(pl.multiple_of(n1 * chans, chans), chans)
        follow = gradients(jnp.minimum(n1 + 1, blocks - 1))
        follow = [jnp.where(n1 + 1 < blocks, f, zero) for f in follow]
        tg_ref[n1] = res[2, at, :] * scale
        for b in range(3):
            parts = load(n1, b)
            out = weight_ref[3 * b] * cur[b]
            for j in (1, 2):
                moved = pltpu.roll(jnp.where(lane < j, follow[b], cur[b]), width - j, 1)
                out = out + weight_ref[3 * b + j] * moved
            ig_ref[n1, b] = out.astype(jnp.bfloat16)
            for j in range(3):
                sg_ref[3 * b + j] += cur[b] * parts[j]
        return tuple(follow)

    lax.fori_loop(0, blocks, finish, gradients(0))


def convolve_all(inputs, taps, grad, weight, scale):
    blocks, _, chans, width = inputs.shape
    consts = [jnp.asarray(t) for t in tables(blocks, width)]
    return pl.pallas_call(
        lambda *refs: conv_kernel(scale, *refs),
        out_shape=(
            jax.ShapeDtypeStruct((blocks, 3, chans, width), jnp.bfloat16),
            jax.ShapeDtypeStruct((blocks, chans, width), jnp.float32),
            jax.ShapeDtypeStruct((9, chans, width), jnp.float32),
        ),
        scratch_shapes=[
            pltpu.VMEM((3, blocks * chans, width), jnp.float32),
            pltpu.VMEM((3, blocks * chans, width), jnp.float32),
            pltpu.VMEM((blocks * chans, width), jnp.float32),
            pltpu.VMEM((blocks * chans, width), jnp.float32),
        ],
        compiler_params=pltpu.CompilerParams(vmem_limit_bytes=56 << 20),
    )(inputs, taps, grad, weight, *consts)


def regroup(x):
    return lax.all_to_all(x, "ctx", split_axis=0, concat_axis=0, tiled=True)


def shards(inputs, short_weight, taps, w_out, grad_out):
    rows, local = inputs.shape[1], inputs.shape[2]
    count = lax.axis_size("ctx")
    where = lax.axis_index("ctx")
    chans = local // count
    scale = 1.0 / math.sqrt(count * rows)

    streams = regroup(inputs.reshape(3, rows, count, chans).transpose(2, 0, 3, 1))
    filt = regroup(taps.reshape(rows, count, chans).transpose(1, 2, 0))

    other = lax.ppermute(grad_out, "tp", [(0, 1), (1, 0)])
    first = lax.axis_index("tp") == 0
    whole = jnp.where(
        first,
        jnp.concatenate([grad_out, other], axis=1),
        jnp.concatenate([other, grad_out], axis=1),
    )
    gated = lax.dot_general(
        w_out, whole, (((1,), (1,)), ((), ())), preferred_element_type=jnp.float32
    )
    gated = regroup(gated.reshape(count, chans, rows))

    weight = lax.dynamic_slice_in_dim(short_weight, where * chans, chans, axis=2)
    weight = jnp.broadcast_to(weight.reshape(9, chans, 1), (9, chans, rows))

    inputs_grad, taps_grad, sums = convolve_all(streams, filt, gated, weight, scale)

    inputs_grad = regroup(inputs_grad).transpose(1, 3, 0, 2).reshape(3, rows, local)
    taps_grad = regroup(taps_grad).transpose(2, 0, 1).reshape(rows, local)
    sums = jnp.sum(sums, axis=2) * scale
    short_grad = lax.all_gather(sums, "ctx", axis=1, tiled=True).reshape(3, 3, local)
    return inputs_grad, taps_grad, short_grad


def solution(mesh):
    return jax.shard_map(
        shards,
        mesh=mesh,
        in_specs=(
            P(None, "ctx", "tp"),
            P(None, None, "tp"),
            P("ctx", "tp"),
            P("tp", None),
            P("ctx", "tp"),
        ),
        out_specs=(P(None, "ctx", "tp"), P("ctx", "tp"), P(None, None, "tp")),
        check_vma=False,
    )
```

```python
import math

import jax
import jax.numpy as jnp
import numpy as np
from jax import lax
from jax.experimental import pallas as pl
from jax.experimental.pallas import tpu as pltpu
from jax.sharding import PartitionSpec as P

GROUP = 4


def split_np(x):
    high = x.astype(jnp.bfloat16)
    low = (x - high.astype(np.float64)).astype(jnp.bfloat16)
    return high, low


def tables(blocks, width):
    length = 2 * blocks * width
    n1 = np.arange(blocks)
    n2 = np.arange(width)
    angle = 2.0 * np.pi * np.outer(n1 + 0.5, n1) / (2 * blocks)
    first = np.concatenate([np.cos(angle), -np.sin(angle)], axis=0)
    high, low = split_np(first)
    first3 = np.concatenate([high, high, low], axis=1)
    last = first.T * (2.0 / length)
    high, low = split_np(last)
    last4 = np.concatenate(
        [
            np.concatenate([high, high], axis=1),
            np.concatenate([low, np.zeros_like(low)], axis=1),
        ],
        axis=0,
    )
    angle = 2.0 * np.pi * (np.outer(n2, n2) % width) / width
    cos, sin = np.cos(angle), np.sin(angle)
    forward = np.block([[cos, -sin], [sin, cos]])
    high, low = split_np(forward)
    forward3 = np.concatenate([high, high, low], axis=0)
    backward = np.block([[cos, sin], [-sin, cos]])
    high, low = split_np(backward)
    backward3 = np.concatenate([high, high, low], axis=0)
    angle = 2.0 * np.pi * np.outer(n1 + 0.5, n2) / length
    twiddle = np.stack([np.cos(angle), np.sin(angle)]).astype(np.float32)
    return first3, last4, forward3, backward3, twiddle


def split(x):
    high = x.astype(jnp.bfloat16)
    low = (x - high.astype(jnp.float32)).astype(jnp.bfloat16)
    return high, low


def mm(a, b):
    return jnp.dot(a, b, preferred_element_type=jnp.float32)


def conv_kernel(
    scale,
    in_ref,
    taps_ref,
    grad_ref,
    weight_ref,
    first_ref,
    last_ref,
    forward_ref,
    backward_ref,
    twiddle_ref,
    ig_ref,
    tg_ref,
    src,
    res,
    key_ref,
    val_ref,
    sums,
):
    blocks, _, chans, width = in_ref.shape
    lane = lax.broadcasted_iota(jnp.int32, (chans, width), 1)
    zero = jnp.zeros((chans, width), jnp.float32)

    def load(n1, b):
        cur = in_ref[n1, b].astype(jnp.float32)
        before = in_ref[jnp.maximum(n1 - 1, 0), b].astype(jnp.float32)
        before = jnp.where(n1 > 0, before, zero)
        return [cur] + [
            pltpu.roll(jnp.where(lane >= width - j, before, cur), j, 1) for j in (1, 2)
        ]

    def prepare(n1, carry):
        mixed = []
        for b in range(3):
            parts = load(n1, b)
            mixed.append(
                weight_ref[3 * b] * parts[0]
                + weight_ref[3 * b + 1] * parts[1]
                + weight_ref[3 * b + 2] * parts[2]
            )
        at = pl.ds(pl.multiple_of(n1 * chans, chans), chans)
        src[0, at, :] = taps_ref[n1] * scale
        src[1, at, :] = mixed[1] * mixed[2]
        src[2, at, :] = grad_ref[n1] * mixed[0]
        key_ref[at, :] = mixed[1]
        val_ref[at, :] = mixed[2]
        return carry

    lax.fori_loop(0, blocks, prepare, 0)

    cos, sin = twiddle_ref[0], twiddle_ref[1]

    def convolve(step, carry):
        base = step * GROUP
        rows = []
        for s in range(3):
            for g in range(0, GROUP, 2):
                cols = []
                for h in (0, 1):
                    x = src[s, pl.ds(base + g + h, blocks, stride=chans), :]
                    high, low = split(x)
                    cols.append(jnp.concatenate([high, low, high], axis=0))
                out = mm(first_ref[...], jnp.concatenate(cols, axis=1))
                for h in (0, 1):
                    re = out[:blocks, h * width : (h + 1) * width]
                    im = out[blocks:, h * width : (h + 1) * width]
                    rows.append(
                        jnp.concatenate([re * cos + im * sin, im * cos - re * sin], axis=1)
                    )
        high, low = split(jnp.concatenate(rows, axis=0))
        spec = mm(jnp.concatenate([high, low, high], axis=1), forward_ref[...])
        part = GROUP * blocks
        fr, fi = spec[:part, :width], spec[:part, width:]
        pr, pi = spec[part : 2 * part, :width], spec[part : 2 * part, width:]
        gr, gi = spec[2 * part :, :width], spec[2 * part :, width:]
        prod = jnp.concatenate(
            [
                jnp.concatenate([fr * pr - fi * pi, fr * pi + fi * pr], axis=1),
                jnp.concatenate([fr * gr + fi * gi, fr * gi - fi * gr], axis=1),
                jnp.concatenate([pr * gr + pi * gi, pr * gi - pi * gr], axis=1),
            ],
            axis=0,
        )
        high, low = split(prod)
        back = mm(jnp.concatenate([high, low, high], axis=1), backward_ref[...])
        for s in range(3):
            for g in range(0, GROUP, 2):
                cols = []
                for h in (0, 1):
                    at = (s * GROUP + g + h) * blocks
                    re = back[at : at + blocks, :width]
                    im = back[at : at + blocks, width:]
                    both = jnp.concatenate([re * cos - im * sin, re * sin + im * cos], axis=0)
                    high, low = split(both)
                    cols.append(jnp.concatenate([high, low], axis=0))
                out = mm(last_ref[...], jnp.concatenate(cols, axis=1))
                out = out[:blocks] + out[blocks:]
                for h in (0, 1):
                    res[s, pl.ds(base + g + h, blocks, stride=chans), :] = out[
                        :, h * width : (h + 1) * width
                    ]
        return carry

    lax.fori_loop(0, chans // GROUP, convolve, 0)

    def gradients(n1):
        at = pl.ds(pl.multiple_of(n1 * chans, chans), chans)
        dz = res[1, at, :]
        return grad_ref[n1] * res[0, at, :], dz * val_ref[at, :], dz * key_ref[at, :]

    sums[...] = jnp.zeros_like(sums)

    def finish(n1, cur):
        at = pl.ds(pl.multiple_of(n1 * chans, chans), chans)
        follow = gradients(jnp.minimum(n1 + 1, blocks - 1))
        follow = [jnp.where(n1 + 1 < blocks, f, zero) for f in follow]
        tg_ref[n1, :chans] = res[2, at, :] * scale
        for b in range(3):
            parts = load(n1, b)
            out = weight_ref[3 * b] * cur[b]
            for j in (1, 2):
                moved = pltpu.roll(jnp.where(lane < j, follow[b], cur[b]), width - j, 1)
                out = out + weight_ref[3 * b + j] * moved
            ig_ref[n1, b] = out.astype(jnp.bfloat16)
            for j in range(3):
                sums[3 * b + j] += cur[b] * parts[j]
        return tuple(follow)

    lax.fori_loop(0, blocks, finish, gradients(0))

    total = jnp.zeros((chans, width), jnp.float32)
    for t in range(9):
        column = jnp.sum(sums[t], axis=1, keepdims=True) * scale
        total = total + jnp.where(lane == t, column, 0.0)
    total = jnp.concatenate([total] + [zero] * (width // chans - 1), axis=0).T
    per = width // chans
    packed = []
    for r in range(8):
        row = jnp.zeros((1, width), jnp.float32)
        for a in range(per):
            if per * r + a < 9:
                line = total[per * r + a : per * r + a + 1]
                row = row + (pltpu.roll(line, a * chans, 1) if a else line)
        packed.append(row)
    packed = jnp.concatenate(packed, axis=0)

    def attach(n1, carry):
        tg_ref[n1, chans:] = packed
        return carry

    lax.fori_loop(0, blocks, attach, 0)


def convolve_all(inputs, taps, grad, weight, scale):
    blocks, _, chans, width = inputs.shape
    consts = [jnp.asarray(t) for t in tables(blocks, width)]
    return pl.pallas_call(
        lambda *refs: conv_kernel(scale, *refs),
        out_shape=(
            jax.ShapeDtypeStruct((blocks, 3, chans, width), jnp.bfloat16),
            jax.ShapeDtypeStruct((blocks, chans + 8, width), jnp.float32),
        ),
        scratch_shapes=[
            pltpu.VMEM((3, blocks * chans, width), jnp.float32),
            pltpu.VMEM((3, blocks * chans, width), jnp.float32),
            pltpu.VMEM((blocks * chans, width), jnp.float32),
            pltpu.VMEM((blocks * chans, width), jnp.float32),
            pltpu.VMEM((9, chans, width), jnp.float32),
        ],
        compiler_params=pltpu.CompilerParams(vmem_limit_bytes=56 << 20),
    )(inputs, taps, grad, weight, *consts)


def regroup(x):
    return lax.all_to_all(x, "ctx", split_axis=0, concat_axis=0, tiled=True)


def shards(inputs, short_weight, taps, w_out, grad_out):
    rows, local = inputs.shape[1], inputs.shape[2]
    count = lax.axis_size("ctx")
    where = lax.axis_index("ctx")
    chans = local // count
    scale = 1.0 / math.sqrt(count * rows)

    streams = regroup(inputs.reshape(3, rows, count, chans).transpose(2, 0, 3, 1))
    filt = regroup(taps.reshape(rows, count, chans).transpose(1, 2, 0))

    other = lax.ppermute(grad_out, "tp", [(0, 1), (1, 0)])
    first = lax.axis_index("tp") == 0
    whole = jnp.where(
        first,
        jnp.concatenate([grad_out, other], axis=1),
        jnp.concatenate([other, grad_out], axis=1),
    )
    gated = lax.dot_general(
        w_out, whole, (((1,), (1,)), ((), ())), preferred_element_type=jnp.float32
    )
    gated = regroup(gated.reshape(count, chans, rows))

    weight = lax.dynamic_slice_in_dim(short_weight, where * chans, chans, axis=2)
    weight = jnp.broadcast_to(weight.reshape(9, chans, 1), (9, chans, rows))

    inputs_grad, taps_grad = convolve_all(streams, filt, gated, weight, scale)

    inputs_grad = regroup(inputs_grad).transpose(1, 3, 0, 2).reshape(3, rows, local)
    taps_grad = regroup(taps_grad)
    sums = taps_grad[:, chans:].reshape(count, 8 * rows)[:, : 9 * chans]
    short_grad = sums.reshape(count, 9, chans).transpose(1, 0, 2).reshape(3, 3, local)
    taps_grad = taps_grad[:, :chans].transpose(2, 0, 1).reshape(rows, local)
    return inputs_grad, taps_grad, short_grad


def solution(mesh):
    return jax.shard_map(
        shards,
        mesh=mesh,
        in_specs=(
            P(None, "ctx", "tp"),
            P(None, None, "tp"),
            P("ctx", "tp"),
            P("tp", None),
            P("ctx", "tp"),
        ),
        out_specs=(P(None, "ctx", "tp"), P("ctx", "tp"), P(None, None, "tp")),
        check_vma=False,
    )
```

```python
import math

import jax
import jax.numpy as jnp
import numpy as np
from jax import lax
from jax.experimental import pallas as pl
from jax.experimental.pallas import tpu as pltpu
from jax.sharding import PartitionSpec as P

GROUP = 4
UNROLL = 4


def split_np(x):
    high = x.astype(jnp.bfloat16)
    low = (x - high.astype(np.float64)).astype(jnp.bfloat16)
    return high, low


def tables(blocks, width):
    length = 2 * blocks * width
    n1 = np.arange(blocks)
    n2 = np.arange(width)
    angle = 2.0 * np.pi * np.outer(n1 + 0.5, n1) / (2 * blocks)
    first = np.concatenate([np.cos(angle), -np.sin(angle)], axis=0)
    high, low = split_np(first)
    first3 = np.concatenate([high, high, low], axis=1)
    last = first.T * (2.0 / length)
    high, low = split_np(last)
    last4 = np.concatenate(
        [
            np.concatenate([high, high], axis=1),
            np.concatenate([low, np.zeros_like(low)], axis=1),
        ],
        axis=0,
    )
    angle = 2.0 * np.pi * (np.outer(n2, n2) % width) / width
    cos, sin = np.cos(angle), np.sin(angle)
    forward = np.block([[cos, -sin], [sin, cos]])
    high, low = split_np(forward)
    forward3 = np.concatenate([high, high, low], axis=0)
    backward = np.block([[cos, sin], [-sin, cos]])
    high, low = split_np(backward)
    backward3 = np.concatenate([high, high, low], axis=0)
    angle = 2.0 * np.pi * np.outer(n1 + 0.5, n2) / length
    twiddle = np.stack([np.cos(angle), np.sin(angle)]).astype(np.float32)
    return first3, last4, forward3, backward3, twiddle


def split(x):
    high = x.astype(jnp.bfloat16)
    low = (x - high.astype(jnp.float32)).astype(jnp.bfloat16)
    return high, low


def mm(a, b):
    return jnp.dot(a, b, preferred_element_type=jnp.float32)


def forward_rows(x_of, first_ref, cos, sin, blocks, width):
    rows = []
    for g in range(0, GROUP, 2):
        cols = []
        for h in (0, 1):
            high, low = split(x_of(g + h))
            cols.append(jnp.concatenate([high, low, high], axis=0))
        out = mm(first_ref[...], jnp.concatenate(cols, axis=1))
        for h in (0, 1):
            re = out[:blocks, h * width : (h + 1) * width]
            im = out[blocks:, h * width : (h + 1) * width]
            rows.append(jnp.concatenate([re * cos + im * sin, im * cos - re * sin], axis=1))
    return rows


def step_two(rows, table_ref):
    high, low = split(rows)
    return mm(jnp.concatenate([high, low, high], axis=1), table_ref[...])


def inverse_one(back, put, last_ref, cos, sin, blocks, width):
    for g in range(0, GROUP, 2):
        cols = []
        for h in (0, 1):
            at = (g + h) * blocks
            re = back[at : at + blocks, :width]
            im = back[at : at + blocks, width:]
            both = jnp.concatenate([re * cos - im * sin, re * sin + im * cos], axis=0)
            high, low = split(both)
            cols.append(jnp.concatenate([high, low], axis=0))
        out = mm(last_ref[...], jnp.concatenate(cols, axis=1))
        out = out[:blocks] + out[blocks:]
        for h in (0, 1):
            put(g + h, out[:, h * width : (h + 1) * width])


def times(a, b, width):
    ar, ai, br, bi = a[:, :width], a[:, width:], b[:, :width], b[:, width:]
    return jnp.concatenate([ar * br - ai * bi, ar * bi + ai * br], axis=1)


def conj_times(a, b, width):
    ar, ai, br, bi = a[:, :width], a[:, width:], b[:, :width], b[:, width:]
    return jnp.concatenate([ar * br + ai * bi, ar * bi - ai * br], axis=1)


def row_of(n1, chans):
    return pl.ds(pl.multiple_of(n1 * chans, chans), chans)


def lagged(in_ref, n1, b, chans, width):
    lane = lax.broadcasted_iota(jnp.int32, (chans, width), 1)
    at = pl.ds(b * chans, chans)
    cur = in_ref[n1, at, :].astype(jnp.float32)
    before = in_ref[jnp.maximum(n1 - 1, 0), at, :].astype(jnp.float32)
    before = jnp.where(n1 > 0, before, 0.0)
    return [cur] + [
        pltpu.roll(jnp.where(lane >= width - j, before, cur), j, 1) for j in (1, 2)
    ]


def ahead(weights, cur, follow, chans, width):
    lane = lax.broadcasted_iota(jnp.int32, (chans, width), 1)
    out = weights[0] * cur
    for j in (1, 2):
        moved = pltpu.roll(jnp.where(lane < j, follow, cur), width - j, 1)
        out = out + weights[j] * moved
    return out


def first_kernel(
    scale,
    in_ref,
    weight_ref,
    first_ref,
    last_ref,
    forward_ref,
    backward_ref,
    twiddle_ref,
    mixed_ref,
    filt_ref,
    prod_ref,
    conv_ref,
    src,
):
    blocks, width = in_ref.shape[0], in_ref.shape[2]
    chans = weight_ref.shape[1]

    def prepare(step, carry):
        for u in range(UNROLL):
            n1 = step * UNROLL + u
            at = row_of(n1, chans)
            mixed = []
            for b in range(3):
                parts = lagged(in_ref, n1, b, chans, width)
                mixed.append(
                    weight_ref[3 * b] * parts[0]
                    + weight_ref[3 * b + 1] * parts[1]
                    + weight_ref[3 * b + 2] * parts[2]
                )
                mixed_ref[b, at, :] = mixed[b]
            taps = in_ref[n1, pl.ds(3 * chans, chans), :].astype(jnp.float32)
            taps = taps + in_ref[n1, pl.ds(4 * chans, chans), :].astype(jnp.float32)
            src[0, at, :] = taps * scale
            src[1, at, :] = mixed[1] * mixed[2]
        return carry

    lax.fori_loop(0, blocks // UNROLL, prepare, 0)
    cos, sin = twiddle_ref[0], twiddle_ref[1]

    def convolve(step, carry):
        base = step * GROUP
        part = GROUP * blocks
        rows = []
        for s in range(2):
            rows += forward_rows(
                lambda g: src[s, pl.ds(base + g, blocks, stride=chans), :],
                first_ref,
                cos,
                sin,
                blocks,
                width,
            )
        spec = step_two(jnp.concatenate(rows, axis=0), forward_ref)
        at = row_of(step, part)
        filt_ref[at, :] = spec[:part]
        prod_ref[at, :] = spec[part:]
        back = step_two(times(spec[:part], spec[part:], width), backward_ref)

        def put(g, out):
            conv_ref[pl.ds(base + g, blocks, stride=chans), :] = out

        inverse_one(back, put, last_ref, cos, sin, blocks, width)
        return carry

    lax.fori_loop(0, chans // GROUP, convolve, 0)


def query_kernel(grad_ref, conv_ref, weight_ref, ig_ref):
    blocks, chans, width = grad_ref.shape
    weights = [weight_ref[j] for j in range(3)]

    def dm(n1):
        return grad_ref[n1] * conv_ref[row_of(n1, chans), :]

    def finish(step, cur):
        for u in range(UNROLL):
            n1 = step * UNROLL + u
            follow = dm(jnp.minimum(n1 + 1, blocks - 1))
            if u == UNROLL - 1:
                follow = jnp.where(n1 + 1 < blocks, follow, 0.0)
            ig_ref[n1] = ahead(weights, cur, follow, chans, width).astype(jnp.bfloat16)
            cur = follow
        return cur

    lax.fori_loop(0, blocks // UNROLL, finish, dm(0))


def last_kernel(
    scale,
    grad_ref,
    in_ref,
    mixed_ref,
    filt_ref,
    prod_ref,
    conv_ref,
    weight_ref,
    first_ref,
    last_ref,
    forward_ref,
    backward_ref,
    twiddle_ref,
    out_ref,
    src,
    res,
    sums,
):
    blocks, chans, width = grad_ref.shape
    lane = lax.broadcasted_iota(jnp.int32, (chans, width), 1)

    def prepare(step, carry):
        for u in range(UNROLL):
            n1 = step * UNROLL + u
            at = row_of(n1, chans)
            src[at, :] = grad_ref[n1] * mixed_ref[0, at, :]
        return carry

    lax.fori_loop(0, blocks // UNROLL, prepare, 0)
    cos, sin = twiddle_ref[0], twiddle_ref[1]

    def convolve(step, carry):
        base = step * GROUP
        part = GROUP * blocks
        rows = forward_rows(
            lambda g: src[pl.ds(base + g, blocks, stride=chans), :],
            first_ref,
            cos,
            sin,
            blocks,
            width,
        )
        spec = step_two(jnp.concatenate(rows, axis=0), forward_ref)
        at = row_of(step, part)
        both = [conj_times(r[at, :], spec, width) for r in (filt_ref, prod_ref)]
        back = step_two(jnp.concatenate(both, axis=0), backward_ref)
        for s in range(2):

            def put(g, out):
                res[s, pl.ds(base + g, blocks, stride=chans), :] = out

            inverse_one(
                back[s * part : (s + 1) * part], put, last_ref, cos, sin, blocks, width
            )
        return carry

    lax.fori_loop(0, chans // GROUP, convolve, 0)

    def gradients(n1):
        at = row_of(n1, chans)
        dz = res[0, at, :]
        return [dz * mixed_ref[2, at, :], dz * mixed_ref[1, at, :]]

    sums[...] = jnp.zeros_like(sums)

    def finish(step, cur):
        cur = list(cur)
        adds = [None] * 9
        for u in range(UNROLL):
            n1 = step * UNROLL + u
            at = row_of(n1, chans)
            follow = gradients(jnp.minimum(n1 + 1, blocks - 1))
            if u == UNROLL - 1:
                follow = [jnp.where(n1 + 1 < blocks, f, 0.0) for f in follow]
            for b in (1, 2):
                weights = [weight_ref[3 * b + j] for j in range(3)]
                out = ahead(weights, cur[b - 1], follow[b - 1], chans, width)
                out_ref[n1, pl.ds((b - 1) * chans, chans), :] = out.astype(jnp.bfloat16)
            high, low = split(res[1, at, :] * scale)
            out_ref[n1, pl.ds(2 * chans, chans), :] = high
            out_ref[n1, pl.ds(3 * chans, chans), :] = low
            full = [grad_ref[n1] * conv_ref[at, :]] + cur
            for b in range(3):
                parts = lagged(in_ref, n1, b, chans, width)
                for j in range(3):
                    term = full[b] * parts[j]
                    old = adds[3 * b + j]
                    adds[3 * b + j] = term if old is None else old + term
            cur = follow
        for t in range(9):
            sums[t] += adds[t]
        return tuple(cur)

    lax.fori_loop(0, blocks // UNROLL, finish, tuple(gradients(0)))

    total = jnp.zeros((chans, width), jnp.float32)
    for t in range(9):
        column = jnp.sum(sums[t], axis=1, keepdims=True) * scale
        total = total + jnp.where(lane == t, column, 0.0)
    per = width // chans
    total = jnp.concatenate([total] + [jnp.zeros_like(total)] * (per - 1), axis=0).T
    high = total.astype(jnp.bfloat16).astype(jnp.float32)
    mid = (total - high).astype(jnp.bfloat16).astype(jnp.float32)
    low = total - high - mid
    lines = [p[t : t + 1] for p in (high, mid, low) for t in range(9)]
    packed = []
    for r in range(8):
        row = jnp.zeros((1, width), jnp.float32)
        for a, line in enumerate(lines[per * r : per * r + per]):
            row = row + (pltpu.roll(line, a * chans, 1) if a else line)
        packed.append(row)
    packed = jnp.concatenate(packed, axis=0).astype(jnp.bfloat16)

    def attach(n1, carry):
        out_ref[n1, pl.ds(4 * chans, 8), :] = packed
        return carry

    lax.fori_loop(0, blocks, attach, 0)


def f32(*shape):
    return jax.ShapeDtypeStruct(shape, jnp.float32)


def bf16(*shape):
    return jax.ShapeDtypeStruct(shape, jnp.bfloat16)


def estimate(us):
    return pl.CostEstimate(flops=int(us * 1e8), bytes_accessed=int(us * 3e6), transcendentals=0)


def params(mib):
    return pltpu.CompilerParams(vmem_limit_bytes=mib << 20)


def stage_one(streams, weight, consts, scale):
    blocks, width = streams.shape[0], streams.shape[2]
    chans = weight.shape[1]
    rows = blocks * chans
    return pl.pallas_call(
        lambda *refs: first_kernel(scale, *refs),
        name="stage_one",
        out_shape=(
            f32(3, rows, width),
            f32(rows, 2 * width),
            f32(rows, 2 * width),
            f32(rows, width),
        ),
        scratch_shapes=[pltpu.VMEM((2, rows, width), jnp.float32)],
        cost_estimate=estimate(14),
        compiler_params=params(24),
    )(streams, weight, *consts)


def stage_two(grad, conv, weight):
    return pl.pallas_call(
        query_kernel,
        name="stage_two",
        out_shape=bf16(*grad.shape),
        cost_estimate=estimate(3),
        compiler_params=params(8),
    )(grad, conv, weight)


def stage_three(grad, streams, mixed, filt, prod, conv, weight, consts, scale):
    blocks, chans, width = grad.shape
    rows = blocks * chans
    return pl.pallas_call(
        lambda *refs: last_kernel(scale, *refs),
        name="stage_three",
        out_shape=bf16(blocks, 4 * chans + 8, width),
        scratch_shapes=[
            pltpu.VMEM((rows, width), jnp.float32),
            pltpu.VMEM((2, rows, width), jnp.float32),
            pltpu.VMEM((9, chans, width), jnp.float32),
        ],
        cost_estimate=estimate(14),
        compiler_params=params(32),
    )(grad, streams, mixed, filt, prod, conv, weight, *consts)


def regroup(x):
    return lax.all_to_all(x, "ctx", split_axis=0, concat_axis=0, tiled=True)


def shards(inputs, short_weight, taps, w_out, grad_out):
    rows, local = inputs.shape[1], inputs.shape[2]
    count = lax.axis_size("ctx")
    where = lax.axis_index("ctx")
    chans = local // count
    scale = 1.0 / math.sqrt(count * rows)

    high = lax.reduce_precision(taps, 8, 7)
    low = (taps - high).astype(jnp.bfloat16)
    streams = jnp.concatenate([inputs, high.astype(jnp.bfloat16)[None], low[None]], axis=0)
    streams = streams.reshape(5, rows, count, chans).transpose(2, 0, 3, 1)
    streams = regroup(streams.reshape(count, 5 * chans, rows))

    other = lax.ppermute(grad_out, "tp", [(0, 1), (1, 0)])
    first = lax.axis_index("tp") == 0
    whole = jnp.where(
        first,
        jnp.concatenate([grad_out, other], axis=1),
        jnp.concatenate([other, grad_out], axis=1),
    )
    gated = lax.dot_general(
        w_out, whole, (((1,), (1,)), ((), ())), preferred_element_type=jnp.float32
    )
    gated = regroup(gated.reshape(count, chans, rows))

    weight = lax.dynamic_slice_in_dim(short_weight, where * chans, chans, axis=2)
    weight = jnp.broadcast_to(weight.reshape(9, chans, 1), (9, chans, rows))

    consts = [jnp.asarray(t) for t in tables(count, rows)]
    mixed, filt, prod, conv = stage_one(streams, weight, consts, scale)
    query = stage_two(gated, conv, weight)
    query, gated, mixed = lax.optimization_barrier((query, gated, mixed))
    rest = stage_three(gated, streams, mixed, filt, prod, conv, weight, consts, scale)

    query = regroup(query)
    query, rest = lax.optimization_barrier((query, rest))
    rest = regroup(rest)
    grads = jnp.stack(
        [query, rest[:, :chans], rest[:, chans : 2 * chans]], axis=1
    )
    inputs_grad = grads.transpose(1, 3, 0, 2).reshape(3, rows, local)
    taps_grad = rest[:, 2 * chans : 3 * chans].astype(jnp.float32)
    taps_grad = taps_grad + rest[:, 3 * chans : 4 * chans].astype(jnp.float32)
    taps_grad = taps_grad.transpose(2, 0, 1).reshape(rows, local)
    sums = rest[:, 4 * chans :].astype(jnp.float32)
    sums = sums.reshape(count, 8 * rows)[:, : 27 * chans].reshape(count, 3, 9, chans)
    short_grad = jnp.sum(sums, axis=1).transpose(1, 0, 2).reshape(3, 3, local)
    return inputs_grad, taps_grad, short_grad


def solution(mesh):
    return jax.shard_map(
        shards,
        mesh=mesh,
        in_specs=(
            P(None, "ctx", "tp"),
            P(None, None, "tp"),
            P("ctx", "tp"),
            P("tp", None),
            P("ctx", "tp"),
        ),
        out_specs=(P(None, "ctx", "tp"), P("ctx", "tp"), P(None, None, "tp")),
        check_vma=False,
    )
```

```python
import math

import jax
import jax.numpy as jnp
import numpy as np
from jax import lax
from jax.experimental import pallas as pl
from jax.experimental.pallas import tpu as pltpu
from jax.sharding import PartitionSpec as P

GROUP = 4
UNROLL = 4


def split_np(x):
    high = x.astype(jnp.bfloat16)
    low = (x - high.astype(np.float64)).astype(jnp.bfloat16)
    return high, low


def tables(blocks, width):
    length = 2 * blocks * width
    n1 = np.arange(blocks)
    n2 = np.arange(width)
    angle = 2.0 * np.pi * np.outer(n1 + 0.5, n1) / (2 * blocks)
    first = np.concatenate([np.cos(angle), -np.sin(angle)], axis=0)
    high, low = split_np(first)
    first3 = np.concatenate([high, high, low], axis=1)
    last = first.T * (2.0 / length)
    high, low = split_np(last)
    last4 = np.concatenate(
        [
            np.concatenate([high, high], axis=1),
            np.concatenate([low, np.zeros_like(low)], axis=1),
        ],
        axis=0,
    )
    angle = 2.0 * np.pi * (np.outer(n2, n2) % width) / width
    cos, sin = np.cos(angle), np.sin(angle)
    forward = np.block([[cos, -sin], [sin, cos]])
    high, low = split_np(forward)
    forward3 = np.concatenate([high, high, low], axis=0)
    backward = np.block([[cos, sin], [-sin, cos]])
    high, low = split_np(backward)
    backward3 = np.concatenate([high, high, low], axis=0)
    angle = 2.0 * np.pi * np.outer(n1 + 0.5, n2) / length
    twiddle = np.stack([np.cos(angle), np.sin(angle)]).astype(np.float32)
    return first3, last4, forward3, backward3, twiddle


def split(x):
    high = x.astype(jnp.bfloat16)
    low = (x - high.astype(jnp.float32)).astype(jnp.bfloat16)
    return high, low


def mm(a, b):
    return jnp.dot(a, b, preferred_element_type=jnp.float32)


def forward_rows(x_of, first_ref, cos, sin, blocks, width):
    rows = []
    for g in range(0, GROUP, 2):
        cols = []
        for h in (0, 1):
            high, low = split(x_of(g + h))
            cols.append(jnp.concatenate([high, low, high], axis=0))
        out = mm(first_ref[...], jnp.concatenate(cols, axis=1))
        for h in (0, 1):
            re = out[:blocks, h * width : (h + 1) * width]
            im = out[blocks:, h * width : (h + 1) * width]
            rows.append(jnp.concatenate([re * cos + im * sin, im * cos - re * sin], axis=1))
    return rows


def step_two(rows, table_ref):
    high, low = split(rows)
    return mm(jnp.concatenate([high, low, high], axis=1), table_ref[...])


def inverse_one(back, put, last_ref, cos, sin, blocks, width):
    for g in range(0, GROUP, 2):
        cols = []
        for h in (0, 1):
            at = (g + h) * blocks
            re = back[at : at + blocks, :width]
            im = back[at : at + blocks, width:]
            both = jnp.concatenate([re * cos - im * sin, re * sin + im * cos], axis=0)
            high, low = split(both)
            cols.append(jnp.concatenate([high, low], axis=0))
        out = mm(last_ref[...], jnp.concatenate(cols, axis=1))
        out = out[:blocks] + out[blocks:]
        for h in (0, 1):
            put(g + h, out[:, h * width : (h + 1) * width])


def times(a, b, width):
    ar, ai, br, bi = a[:, :width], a[:, width:], b[:, :width], b[:, width:]
    return jnp.concatenate([ar * br - ai * bi, ar * bi + ai * br], axis=1)


def conj_times(a, b, width):
    ar, ai, br, bi = a[:, :width], a[:, width:], b[:, :width], b[:, width:]
    return jnp.concatenate([ar * br + ai * bi, ar * bi - ai * br], axis=1)


def row_of(n1, chans):
    return pl.ds(pl.multiple_of(n1 * chans, chans), chans)


def lagged(in_ref, n1, b, chans, width):
    lane = lax.broadcasted_iota(jnp.int32, (chans, width), 1)
    at = pl.ds(b * chans, chans)
    cur = in_ref[n1, at, :].astype(jnp.float32)
    before = in_ref[jnp.maximum(n1 - 1, 0), at, :].astype(jnp.float32)
    before = jnp.where(n1 > 0, before, 0.0)
    return [cur] + [
        pltpu.roll(jnp.where(lane >= width - j, before, cur), j, 1) for j in (1, 2)
    ]


def ahead(weights, cur, follow, chans, width):
    lane = lax.broadcasted_iota(jnp.int32, (chans, width), 1)
    out = weights[0] * cur
    for j in (1, 2):
        moved = pltpu.roll(jnp.where(lane < j, follow, cur), width - j, 1)
        out = out + weights[j] * moved
    return out


def first_kernel(
    scale,
    in_ref,
    weight_ref,
    first_ref,
    last_ref,
    forward_ref,
    backward_ref,
    twiddle_ref,
    mixed_out,
    filt_out,
    prod_out,
    conv_out,
    src,
    mixed_ref,
    filt_ref,
    prod_ref,
    conv_ref,
    sems,
):
    blocks, width = in_ref.shape[0], in_ref.shape[2]
    chans = weight_ref.shape[1]
    copies = [
        pltpu.make_async_copy(a, b, sems.at[i])
        for i, (a, b) in enumerate(
            (
                (mixed_ref, mixed_out),
                (filt_ref, filt_out),
                (prod_ref, prod_out),
                (conv_ref, conv_out),
            )
        )
    ]

    def prepare(step, carry):
        for u in range(UNROLL):
            n1 = step * UNROLL + u
            at = row_of(n1, chans)
            mixed = []
            for b in range(3):
                parts = lagged(in_ref, n1, b, chans, width)
                mixed.append(
                    weight_ref[3 * b] * parts[0]
                    + weight_ref[3 * b + 1] * parts[1]
                    + weight_ref[3 * b + 2] * parts[2]
                )
                mixed_ref[b, at, :] = mixed[b]
            taps = in_ref[n1, pl.ds(3 * chans, chans), :].astype(jnp.float32)
            taps = taps + in_ref[n1, pl.ds(4 * chans, chans), :].astype(jnp.float32)
            src[0, at, :] = taps * scale
            src[1, at, :] = mixed[1] * mixed[2]
        return carry

    lax.fori_loop(0, blocks // UNROLL, prepare, 0)
    copies[0].start()
    cos, sin = twiddle_ref[0], twiddle_ref[1]

    def convolve(step, carry):
        base = step * GROUP
        part = GROUP * blocks
        rows = []
        for s in range(2):
            rows += forward_rows(
                lambda g: src[s, pl.ds(base + g, blocks, stride=chans), :],
                first_ref,
                cos,
                sin,
                blocks,
                width,
            )
        spec = step_two(jnp.concatenate(rows, axis=0), forward_ref)
        at = row_of(step, part)
        filt_ref[at, :] = spec[:part]
        prod_ref[at, :] = spec[part:]
        back = step_two(times(spec[:part], spec[part:], width), backward_ref)

        def put(g, out):
            conv_ref[pl.ds(base + g, blocks, stride=chans), :] = out

        inverse_one(back, put, last_ref, cos, sin, blocks, width)
        return carry

    lax.fori_loop(0, chans // GROUP, convolve, 0)
    for copy in copies[1:]:
        copy.start()
    for copy in copies:
        copy.wait()


def last_kernel(
    scale,
    grad_in,
    streams_in,
    mixed_in,
    filt_in,
    prod_in,
    conv_in,
    weight_ref,
    first_ref,
    last_ref,
    forward_ref,
    backward_ref,
    twiddle_ref,
    out_hbm,
    grad_ref,
    in_ref,
    mixed_ref,
    filt_ref,
    prod_ref,
    conv_ref,
    res,
    sums,
    out_ref,
    tail_ref,
    sems,
    out_sems,
):
    blocks, width = in_ref.shape[0], in_ref.shape[2]
    chans = weight_ref.shape[1]
    lane = lax.broadcasted_iota(jnp.int32, (chans, width), 1)
    copies = [
        pltpu.make_async_copy(a, b, sems.at[i])
        for i, (a, b) in enumerate(
            (
                (grad_in, grad_ref),
                (mixed_in.at[0], mixed_ref.at[0]),
                (filt_in, filt_ref),
                (prod_in, prod_ref),
                (mixed_in.at[pl.ds(1, 2)], mixed_ref.at[pl.ds(1, 2)]),
                (conv_in, conv_ref),
                (streams_in, in_ref),
            )
        )
    ]
    for copy in copies:
        copy.start()
    for copy in copies[:4]:
        copy.wait()
    cos, sin = twiddle_ref[0], twiddle_ref[1]

    def convolve(step, carry):
        base = step * GROUP
        part = GROUP * blocks

        def dy(g):
            at = pl.ds(base + g, blocks, stride=chans)
            return grad_ref[at, :] * mixed_ref[0, at, :]

        rows = forward_rows(dy, first_ref, cos, sin, blocks, width)
        spec = step_two(jnp.concatenate(rows, axis=0), forward_ref)
        at = row_of(step, part)
        both = [conj_times(r[at, :], spec, width) for r in (filt_ref, prod_ref)]
        back = step_two(jnp.concatenate(both, axis=0), backward_ref)
        for s in range(2):

            def put(g, out):
                res[s, pl.ds(base + g, blocks, stride=chans), :] = out

            inverse_one(
                back[s * part : (s + 1) * part], put, last_ref, cos, sin, blocks, width
            )
        return carry

    lax.fori_loop(0, chans // GROUP, convolve, 0)
    for copy in copies[4:]:
        copy.wait()

    def gradients(n1):
        at = row_of(n1, chans)
        dz = res[0, at, :]
        return [
            grad_ref[at, :] * conv_ref[at, :],
            dz * mixed_ref[2, at, :],
            dz * mixed_ref[1, at, :],
        ]

    sums[...] = jnp.zeros_like(sums)

    def finish(step, cur):
        cur = list(cur)
        adds = [None] * 9
        for u in range(UNROLL):
            n1 = step * UNROLL + u
            at = row_of(n1, chans)
            follow = gradients(jnp.minimum(n1 + 1, blocks - 1))
            if u == UNROLL - 1:
                follow = [jnp.where(n1 + 1 < blocks, f, 0.0) for f in follow]
            for b in range(3):
                weights = [weight_ref[3 * b + j] for j in range(3)]
                out = ahead(weights, cur[b], follow[b], chans, width)
                out_ref[n1, pl.ds(b * chans, chans), :] = out.astype(jnp.bfloat16)
            high, low = split(res[1, at, :] * scale)
            out_ref[n1, pl.ds(3 * chans, chans), :] = high
            out_ref[n1, pl.ds(4 * chans, chans), :] = low
            for b in range(3):
                parts = lagged(in_ref, n1, b, chans, width)
                for j in range(3):
                    term = cur[b] * parts[j]
                    old = adds[3 * b + j]
                    adds[3 * b + j] = term if old is None else old + term
            cur = follow
        for t in range(9):
            sums[t] += adds[t]
        some = pl.ds(step * UNROLL, UNROLL)
        pltpu.make_async_copy(
            out_ref.at[some], out_hbm.at[some, pl.ds(0, 5 * chans)], out_sems.at[0]
        ).start()
        return tuple(cur)

    lax.fori_loop(0, blocks // UNROLL, finish, tuple(gradients(0)))

    total = jnp.zeros((chans, width), jnp.float32)
    for t in range(9):
        column = jnp.sum(sums[t], axis=1, keepdims=True) * scale
        total = total + jnp.where(lane == t, column, 0.0)
    per = width // chans
    total = jnp.concatenate([total] + [jnp.zeros_like(total)] * (per - 1), axis=0).T
    high = total.astype(jnp.bfloat16).astype(jnp.float32)
    mid = (total - high).astype(jnp.bfloat16).astype(jnp.float32)
    low = total - high - mid
    lines = [p[t : t + 1] for p in (high, mid, low) for t in range(9)]
    packed = []
    for r in range(8):
        row = jnp.zeros((1, width), jnp.float32)
        for a, line in enumerate(lines[per * r : per * r + per]):
            row = row + (pltpu.roll(line, a * chans, 1) if a else line)
        packed.append(row)
    packed = jnp.concatenate(packed, axis=0).astype(jnp.bfloat16)

    def attach(n1, carry):
        tail_ref[n1] = packed
        return carry

    lax.fori_loop(0, blocks, attach, 0)
    tail = pltpu.make_async_copy(
        tail_ref, out_hbm.at[:, pl.ds(5 * chans, 8)], out_sems.at[1]
    )
    tail.start()
    tail.wait()
    pltpu.make_async_copy(
        out_ref, out_hbm.at[:, pl.ds(0, 5 * chans)], out_sems.at[0]
    ).wait()


def f32(*shape):
    return jax.ShapeDtypeStruct(shape, jnp.float32)


def bf16(*shape):
    return jax.ShapeDtypeStruct(shape, jnp.bfloat16)


def estimate(us):
    return pl.CostEstimate(flops=int(us * 1e8), bytes_accessed=int(us * 3e6), transcendentals=0)


def params(mib):
    return pltpu.CompilerParams(vmem_limit_bytes=mib << 20)


def hbm():
    return pl.BlockSpec(memory_space=pltpu.HBM)


def vmem():
    return pl.BlockSpec(memory_space=pltpu.VMEM)


def stage_one(streams, weight, consts, scale):
    blocks, width = streams.shape[0], streams.shape[2]
    chans = weight.shape[1]
    rows = blocks * chans
    shapes = [(3, rows, width), (rows, 2 * width), (rows, 2 * width), (rows, width)]
    return pl.pallas_call(
        lambda *refs: first_kernel(scale, *refs),
        name="stage_one",
        out_shape=tuple(f32(*shape) for shape in shapes),
        in_specs=[vmem()] * 7,
        out_specs=(hbm(),) * 4,
        scratch_shapes=[pltpu.VMEM((2, rows, width), jnp.float32)]
        + [pltpu.VMEM(shape, jnp.float32) for shape in shapes]
        + [pltpu.SemaphoreType.DMA((4,))],
        cost_estimate=estimate(14),
        compiler_params=params(60),
    )(streams, weight, *consts)


def stage_two(grad, streams, mixed, filt, prod, conv, weight, consts, scale):
    blocks, width = streams.shape[0], streams.shape[2]
    chans = weight.shape[1]
    rows = blocks * chans
    return pl.pallas_call(
        lambda *refs: last_kernel(scale, *refs),
        name="stage_two",
        out_shape=bf16(blocks, 5 * chans + 8, width),
        in_specs=[hbm()] * 6 + [vmem()] * 6,
        out_specs=hbm(),
        scratch_shapes=[
            pltpu.VMEM((rows, width), jnp.float32),
            pltpu.VMEM(streams.shape, jnp.bfloat16),
            pltpu.VMEM((3, rows, width), jnp.float32),
            pltpu.VMEM((rows, 2 * width), jnp.float32),
            pltpu.VMEM((rows, 2 * width), jnp.float32),
            pltpu.VMEM((rows, width), jnp.float32),
            pltpu.VMEM((2, rows, width), jnp.float32),
            pltpu.VMEM((9, chans, width), jnp.float32),
            pltpu.VMEM((blocks, 5 * chans, width), jnp.bfloat16),
            pltpu.VMEM((blocks, 8, width), jnp.bfloat16),
            pltpu.SemaphoreType.DMA((7,)),
            pltpu.SemaphoreType.DMA((2,)),
        ],
        cost_estimate=estimate(14),
        compiler_params=params(60),
    )(grad, streams, mixed, filt, prod, conv, weight, *consts)


def regroup(x):
    return lax.all_to_all(x, "ctx", split_axis=0, concat_axis=0, tiled=True)


def shards(inputs, short_weight, taps, w_out, grad_out):
    rows, local = inputs.shape[1], inputs.shape[2]
    count = lax.axis_size("ctx")
    where = lax.axis_index("ctx")
    chans = local // count
    scale = 1.0 / math.sqrt(count * rows)

    high = lax.reduce_precision(taps, 8, 7)
    low = (taps - high).astype(jnp.bfloat16)
    streams = jnp.concatenate([inputs, high.astype(jnp.bfloat16)[None], low[None]], axis=0)
    streams = streams.reshape(5, rows, count, chans).transpose(2, 0, 3, 1)
    streams = streams.reshape(count, 5 * chans, rows)
    other = lax.ppermute(grad_out, "tp", [(0, 1), (1, 0)])
    streams, other = lax.optimization_barrier((streams, other))
    streams = regroup(streams)

    first = lax.axis_index("tp") == 0
    whole = jnp.where(
        first,
        jnp.concatenate([grad_out, other], axis=1),
        jnp.concatenate([other, grad_out], axis=1),
    )
    gated = lax.dot_general(
        w_out, whole, (((1,), (1,)), ((), ())), preferred_element_type=jnp.float32
    )
    gated = regroup(gated.reshape(count, chans, rows)).reshape(count * chans, rows)

    weight = lax.dynamic_slice_in_dim(short_weight, where * chans, chans, axis=2)
    weight = jnp.broadcast_to(weight.reshape(9, chans, 1), (9, chans, rows))

    consts = [jnp.asarray(t) for t in tables(count, rows)]
    mixed, filt, prod, conv = stage_one(streams, weight, consts, scale)
    back = stage_two(gated, streams, mixed, filt, prod, conv, weight, consts, scale)

    back = regroup(back)
    grads = back[:, : 3 * chans].reshape(count, 3, chans, rows)
    inputs_grad = grads.transpose(1, 3, 0, 2).reshape(3, rows, local)
    taps_grad = back[:, 3 * chans : 4 * chans].astype(jnp.float32)
    taps_grad = taps_grad + back[:, 4 * chans : 5 * chans].astype(jnp.float32)
    taps_grad = taps_grad.transpose(2, 0, 1).reshape(rows, local)
    sums = back[:, 5 * chans :].astype(jnp.float32)
    sums = sums.reshape(count, 8 * rows)[:, : 27 * chans].reshape(count, 3, 9, chans)
    short_grad = jnp.sum(sums, axis=1).transpose(1, 0, 2).reshape(3, 3, local)
    return inputs_grad, taps_grad, short_grad


def solution(mesh):
    return jax.shard_map(
        shards,
        mesh=mesh,
        in_specs=(
            P(None, "ctx", "tp"),
            P(None, None, "tp"),
            P("ctx", "tp"),
            P("tp", None),
            P("ctx", "tp"),
        ),
        out_specs=(P(None, "ctx", "tp"), P("ctx", "tp"), P(None, None, "tp")),
        check_vma=False,
    )
```

```python
import math

import jax
import jax.numpy as jnp
import numpy as np
from jax import lax
from jax.experimental import pallas as pl
from jax.experimental.pallas import tpu as pltpu
from jax.sharding import PartitionSpec as P

GROUP = 16
UNROLL = 8


def split_np(x):
    high = x.astype(jnp.bfloat16)
    low = (x - high.astype(np.float64)).astype(jnp.bfloat16)
    return high, low


def tables(blocks, width):
    length = 2 * blocks * width
    n1 = np.arange(blocks)
    n2 = np.arange(width)
    angle = 2.0 * np.pi * np.outer(n1 + 0.5, n1) / (2 * blocks)
    first = np.concatenate([np.cos(angle), -np.sin(angle)], axis=0)
    high, low = split_np(first)
    first3 = np.concatenate([high, high, low], axis=1)
    last = first.T * (2.0 / length)
    high, low = split_np(last)
    last4 = np.concatenate(
        [
            np.concatenate([high, high], axis=1),
            np.concatenate([low, np.zeros_like(low)], axis=1),
        ],
        axis=0,
    )
    angle = 2.0 * np.pi * (np.outer(n2, n2) % width) / width
    cos, sin = np.cos(angle), np.sin(angle)
    forward = np.block([[cos, -sin], [sin, cos]])
    high, low = split_np(forward)
    forward2 = np.stack([high, low])
    backward = np.block([[cos, sin], [-sin, cos]])
    high, low = split_np(backward)
    backward2 = np.stack([high, low])
    angle = 2.0 * np.pi * np.outer(n1 + 0.5, n2) / length
    twiddle = np.stack([np.cos(angle), np.sin(angle)]).astype(np.float32)
    return first3, last4, forward2, backward2, twiddle


def split(x):
    high = x.astype(jnp.bfloat16)
    low = (x - high.astype(jnp.float32)).astype(jnp.bfloat16)
    return high, low


def mm(a, b):
    return jnp.dot(a, b, preferred_element_type=jnp.float32)


def forward_rows(x_of, first_ref, cos, sin, blocks, width):
    rows = []
    for g in range(0, GROUP, 2):
        cols = []
        for h in (0, 1):
            high, low = split(x_of(g + h))
            cols.append(jnp.concatenate([high, low, high], axis=0))
        out = mm(first_ref[...], jnp.concatenate(cols, axis=1))
        for h in (0, 1):
            re = out[:blocks, h * width : (h + 1) * width]
            im = out[blocks:, h * width : (h + 1) * width]
            rows.append(jnp.concatenate([re * cos + im * sin, im * cos - re * sin], axis=1))
    return rows


def step_two(rows, table_ref):
    high, low = split(rows)
    return mm(high, table_ref[0]) + mm(low, table_ref[0]) + mm(high, table_ref[1])


def inverse_one(back, put, last_ref, cos, sin, blocks, width):
    for g in range(0, GROUP, 2):
        cols = []
        for h in (0, 1):
            at = (g + h) * blocks
            re = back[at : at + blocks, :width]
            im = back[at : at + blocks, width:]
            both = jnp.concatenate([re * cos - im * sin, re * sin + im * cos], axis=0)
            high, low = split(both)
            cols.append(jnp.concatenate([high, low], axis=0))
        out = mm(last_ref[...], jnp.concatenate(cols, axis=1))
        out = out[:blocks] + out[blocks:]
        for h in (0, 1):
            put(g + h, out[:, h * width : (h + 1) * width])


def times(a, b, width):
    ar, ai, br, bi = a[:, :width], a[:, width:], b[:, :width], b[:, width:]
    return jnp.concatenate([ar * br - ai * bi, ar * bi + ai * br], axis=1)


def conj_times(a, b, width):
    ar, ai, br, bi = a[:, :width], a[:, width:], b[:, :width], b[:, width:]
    return jnp.concatenate([ar * br + ai * bi, ar * bi - ai * br], axis=1)


def row_of(n1, chans):
    return pl.ds(pl.multiple_of(n1 * chans, chans), chans)


def lagged(in_ref, n1, b, chans, width):
    lane = lax.broadcasted_iota(jnp.int32, (chans, width), 1)
    at = pl.ds(b * chans, chans)
    cur = in_ref[n1, at, :].astype(jnp.float32)
    before = in_ref[jnp.maximum(n1 - 1, 0), at, :].astype(jnp.float32)
    before = jnp.where(n1 > 0, before, 0.0)
    return [cur] + [
        pltpu.roll(jnp.where(lane >= width - j, before, cur), j, 1) for j in (1, 2)
    ]


def ahead(weights, cur, follow, chans, width):
    lane = lax.broadcasted_iota(jnp.int32, (chans, width), 1)
    out = weights[0] * cur
    for j in (1, 2):
        moved = pltpu.roll(jnp.where(lane < j, follow, cur), width - j, 1)
        out = out + weights[j] * moved
    return out


def load_consts(sources, targets, sems):
    copies = [pltpu.make_async_copy(a, b, sems.at[i]) for i, (a, b) in enumerate(zip(sources, targets))]
    for copy in copies:
        copy.start()
    return copies


def first_kernel(scale, in_hbm, weight_ref, *refs):
    const_in, (mixed_out, filt_out, prod_out, conv_out) = refs[:5], refs[5:9]
    in_ref, src, mixed_ref, filt_ref, prod_ref, conv_ref = refs[9:15]
    consts, const_sems, in_sems, out_sems = refs[15:20], refs[20], refs[21], refs[22]
    first_ref, last_ref, forward_ref, backward_ref, twiddle_ref = consts
    blocks, width = in_ref.shape[0], in_ref.shape[2]
    chans = weight_ref.shape[1]

    def fetch(step):
        some = pl.ds(step * UNROLL, UNROLL)
        return pltpu.make_async_copy(in_hbm.at[some], in_ref.at[some], in_sems.at[step])

    for step in range(blocks // UNROLL):
        fetch(step).start()
    const_copies = load_consts(const_in, consts, const_sems)

    def prepare(step, carry):
        fetch(step).wait()
        for u in range(UNROLL):
            n1 = step * UNROLL + u
            at = row_of(n1, chans)
            mixed = []
            for b in range(3):
                parts = lagged(in_ref, n1, b, chans, width)
                mixed.append(
                    weight_ref[3 * b] * parts[0]
                    + weight_ref[3 * b + 1] * parts[1]
                    + weight_ref[3 * b + 2] * parts[2]
                )
                mixed_ref[b, at, :] = mixed[b]
            taps = in_ref[n1, pl.ds(3 * chans, chans), :].astype(jnp.float32)
            taps = taps + in_ref[n1, pl.ds(4 * chans, chans), :].astype(jnp.float32)
            src[0, at, :] = taps * scale
            src[1, at, :] = mixed[1] * mixed[2]
        return carry

    lax.fori_loop(0, blocks // UNROLL, prepare, 0)
    mixed_copy = pltpu.make_async_copy(mixed_ref, mixed_out, out_sems.at[0])
    mixed_copy.start()
    for copy in const_copies:
        copy.wait()
    cos, sin = twiddle_ref[0], twiddle_ref[1]

    def convolve(step, carry):
        base = step * GROUP
        part = GROUP * blocks
        rows = []
        for s in range(2):
            rows += forward_rows(
                lambda g: src[s, pl.ds(base + g, blocks, stride=chans), :],
                first_ref,
                cos,
                sin,
                blocks,
                width,
            )
        spec = step_two(jnp.concatenate(rows, axis=0), forward_ref)
        at = row_of(step, part)
        filt_ref[at, :] = spec[:part]
        prod_ref[at, :] = spec[part:]
        pltpu.make_async_copy(filt_ref.at[at], filt_out.at[at], out_sems.at[1]).start()
        pltpu.make_async_copy(prod_ref.at[at], prod_out.at[at], out_sems.at[2]).start()
        back = step_two(times(spec[:part], spec[part:], width), backward_ref)

        def put(g, out):
            conv_ref[pl.ds(base + g, blocks, stride=chans), :] = out

        inverse_one(back, put, last_ref, cos, sin, blocks, width)
        return carry

    lax.fori_loop(0, chans // GROUP, convolve, 0)
    conv_copy = pltpu.make_async_copy(conv_ref, conv_out, out_sems.at[3])
    conv_copy.start()
    mixed_copy.wait()
    pltpu.make_async_copy(filt_ref, filt_out, out_sems.at[1]).wait()
    pltpu.make_async_copy(prod_ref, prod_out, out_sems.at[2]).wait()
    conv_copy.wait()


def last_kernel(scale, grad_in, streams_in, mixed_in, filt_in, prod_in, conv_in, weight_ref, *refs):
    const_in, out_hbm = refs[:5], refs[5]
    grad_ref, in_ref, mixed_ref, filt_ref, prod_ref, conv_ref = refs[6:12]
    res, sums, out_ref, tail_ref = refs[12:16]
    consts, const_sems, sems, spec_sems, out_sems = refs[16:21], *refs[21:25]
    first_ref, last_ref, forward_ref, backward_ref, twiddle_ref = consts
    blocks, width = in_ref.shape[0], in_ref.shape[2]
    chans = weight_ref.shape[1]
    lane = lax.broadcasted_iota(jnp.int32, (chans, width), 1)
    copies = [
        pltpu.make_async_copy(a, b, sems.at[i])
        for i, (a, b) in enumerate(
            (
                (grad_in, grad_ref),
                (mixed_in.at[0], mixed_ref.at[0]),
                (mixed_in.at[pl.ds(1, 2)], mixed_ref.at[pl.ds(1, 2)]),
                (conv_in, conv_ref),
                (streams_in, in_ref),
            )
        )
    ]

    def fetch(step):
        at = row_of(step, GROUP * blocks)
        return [
            pltpu.make_async_copy(a.at[at], b.at[at], spec_sems.at[i, step])
            for i, (a, b) in enumerate(((filt_in, filt_ref), (prod_in, prod_ref)))
        ]

    for copy in copies[:2]:
        copy.start()
    const_copies = load_consts(const_in, consts, const_sems)
    for copy in copies[:2] + const_copies:
        copy.wait()
    for copy in fetch(0):
        copy.start()
    cos, sin = twiddle_ref[0], twiddle_ref[1]
    steps = chans // GROUP

    def convolve(step, carry):
        base = step * GROUP
        part = GROUP * blocks

        def dy(g):
            at = pl.ds(base + g, blocks, stride=chans)
            return grad_ref[at, :] * mixed_ref[0, at, :]

        @pl.when(step + 1 < steps)
        def _():
            for copy in fetch(step + 1):
                copy.start()

        @pl.when(step + 1 == steps)
        def _():
            for copy in copies[2:]:
                copy.start()

        rows = forward_rows(dy, first_ref, cos, sin, blocks, width)
        spec = step_two(jnp.concatenate(rows, axis=0), forward_ref)
        at = row_of(step, part)
        for copy in fetch(step):
            copy.wait()
        both = [conj_times(r[at, :], spec, width) for r in (filt_ref, prod_ref)]
        back = step_two(jnp.concatenate(both, axis=0), backward_ref)
        for s in range(2):

            def put(g, out):
                res[s, pl.ds(base + g, blocks, stride=chans), :] = out

            inverse_one(
                back[s * part : (s + 1) * part], put, last_ref, cos, sin, blocks, width
            )
        return carry

    lax.fori_loop(0, steps, convolve, 0)
    for copy in copies[2:]:
        copy.wait()

    def gradients(n1):
        at = row_of(n1, chans)
        dz = res[0, at, :]
        return [
            grad_ref[at, :] * conv_ref[at, :],
            dz * mixed_ref[2, at, :],
            dz * mixed_ref[1, at, :],
        ]

    sums[...] = jnp.zeros_like(sums)

    def finish(step, cur):
        cur = list(cur)
        adds = [None] * 9
        for u in range(UNROLL):
            n1 = step * UNROLL + u
            at = row_of(n1, chans)
            follow = gradients(jnp.minimum(n1 + 1, blocks - 1))
            if u == UNROLL - 1:
                follow = [jnp.where(n1 + 1 < blocks, f, 0.0) for f in follow]
            for b in range(3):
                weights = [weight_ref[3 * b + j] for j in range(3)]
                out = ahead(weights, cur[b], follow[b], chans, width)
                out_ref[n1, pl.ds(b * chans, chans), :] = out.astype(jnp.bfloat16)
            high, low = split(res[1, at, :] * scale)
            out_ref[n1, pl.ds(3 * chans, chans), :] = high
            out_ref[n1, pl.ds(4 * chans, chans), :] = low
            for b in range(3):
                parts = lagged(in_ref, n1, b, chans, width)
                for j in range(3):
                    term = cur[b] * parts[j]
                    old = adds[3 * b + j]
                    adds[3 * b + j] = term if old is None else old + term
            cur = follow
        for t in range(9):
            sums[t] += adds[t]
        some = pl.ds(step * UNROLL, UNROLL)
        pltpu.make_async_copy(
            out_ref.at[some], out_hbm.at[some, pl.ds(0, 5 * chans)], out_sems.at[0]
        ).start()
        return tuple(cur)

    lax.fori_loop(0, blocks // UNROLL, finish, tuple(gradients(0)))

    total = jnp.zeros((chans, width), jnp.float32)
    for t in range(9):
        column = jnp.sum(sums[t], axis=1, keepdims=True) * scale
        total = total + jnp.where(lane == t, column, 0.0)
    per = width // chans
    total = jnp.concatenate([total] + [jnp.zeros_like(total)] * (per - 1), axis=0).T
    high = total.astype(jnp.bfloat16).astype(jnp.float32)
    mid = (total - high).astype(jnp.bfloat16).astype(jnp.float32)
    low = total - high - mid
    lines = [p[t : t + 1] for p in (high, mid, low) for t in range(9)]
    packed = []
    for r in range(8):
        row = jnp.zeros((1, width), jnp.float32)
        for a, line in enumerate(lines[per * r : per * r + per]):
            row = row + (pltpu.roll(line, a * chans, 1) if a else line)
        packed.append(row)
    packed = jnp.concatenate(packed, axis=0).astype(jnp.bfloat16)

    def attach(n1, carry):
        tail_ref[n1] = packed
        return carry

    lax.fori_loop(0, blocks, attach, 0)
    tail = pltpu.make_async_copy(
        tail_ref, out_hbm.at[:, pl.ds(5 * chans, 8)], out_sems.at[1]
    )
    tail.start()
    tail.wait()
    pltpu.make_async_copy(
        out_ref, out_hbm.at[:, pl.ds(0, 5 * chans)], out_sems.at[0]
    ).wait()


def f32(*shape):
    return jax.ShapeDtypeStruct(shape, jnp.float32)


def bf16(*shape):
    return jax.ShapeDtypeStruct(shape, jnp.bfloat16)


def estimate(us):
    return pl.CostEstimate(flops=int(us * 1e8), bytes_accessed=int(us * 3e6), transcendentals=0)


def params(mib):
    return pltpu.CompilerParams(vmem_limit_bytes=mib << 20)


def hbm():
    return pl.BlockSpec(memory_space=pltpu.HBM)


def vmem():
    return pl.BlockSpec(memory_space=pltpu.VMEM)


def hbm():
    return pl.BlockSpec(memory_space=pltpu.HBM)


def vmem():
    return pl.BlockSpec(memory_space=pltpu.VMEM)


def room(*arrays):
    return [pltpu.VMEM(a.shape, a.dtype) for a in arrays]


def stage_one(streams, weight, consts, scale):
    blocks, width = streams.shape[0], streams.shape[2]
    chans = weight.shape[1]
    rows = blocks * chans
    shapes = [f32(3, rows, width), f32(rows, 2 * width), f32(rows, 2 * width), f32(rows, width)]
    return pl.pallas_call(
        lambda *refs: first_kernel(scale, *refs),
        name="stage_one",
        out_shape=tuple(shapes),
        in_specs=[hbm(), vmem()] + [hbm()] * 5,
        out_specs=(hbm(),) * 4,
        scratch_shapes=room(streams, f32(2, rows, width), *shapes, *consts)
        + [
            pltpu.SemaphoreType.DMA((5,)),
            pltpu.SemaphoreType.DMA((blocks // UNROLL,)),
            pltpu.SemaphoreType.DMA((4,)),
        ],
        cost_estimate=estimate(14),
        compiler_params=params(60),
    )(streams, weight, *consts)


def stage_two(grad, streams, mixed, filt, prod, conv, weight, consts, scale):
    blocks, width = streams.shape[0], streams.shape[2]
    chans = weight.shape[1]
    rows = blocks * chans
    return pl.pallas_call(
        lambda *refs: last_kernel(scale, *refs),
        name="stage_two",
        out_shape=bf16(blocks, 5 * chans + 8, width),
        in_specs=[hbm()] * 6 + [vmem()] + [hbm()] * 5,
        out_specs=hbm(),
        scratch_shapes=room(
            grad,
            streams,
            mixed,
            filt,
            prod,
            conv,
            f32(2, rows, width),
            f32(9, chans, width),
            bf16(blocks, 5 * chans, width),
            bf16(blocks, 8, width),
            *consts,
        )
        + [
            pltpu.SemaphoreType.DMA((5,)),
            pltpu.SemaphoreType.DMA((5,)),
            pltpu.SemaphoreType.DMA((2, chans // GROUP)),
            pltpu.SemaphoreType.DMA((2,)),
        ],
        cost_estimate=estimate(14),
        compiler_params=params(60),
    )(grad, streams, mixed, filt, prod, conv, weight, *consts)


def spread_kernel(back_ref, ig_ref, tg_ref):
    some, _, width = back_ref.shape
    chans = width // some

    def part(i):
        rows = [back_ref[d, pl.ds(i * chans, chans), :].astype(jnp.float32) for d in range(some)]
        return jnp.concatenate(rows, axis=0)

    for b in range(3):
        ig_ref[b] = part(b).T.astype(jnp.bfloat16)
    tg_ref[...] = (part(3) + part(4)).T


def spread(back, chans):
    count, height, width = back.shape
    some = width // chans
    return pl.pallas_call(
        spread_kernel,
        name="spread",
        grid=(count // some,),
        out_shape=(bf16(3, width, count * chans), f32(width, count * chans)),
        in_specs=[pl.BlockSpec((some, height, width), lambda i: (i, 0, 0))],
        out_specs=(
            pl.BlockSpec((3, width, width), lambda i: (0, 0, i)),
            pl.BlockSpec((width, width), lambda i: (0, i)),
        ),
        cost_estimate=estimate(4),
        compiler_params=params(16),
    )(back)


def regroup(x):
    return lax.all_to_all(x, "ctx", split_axis=0, concat_axis=0, tiled=True)


def shards(inputs, short_weight, taps, w_out, grad_out):
    rows, local = inputs.shape[1], inputs.shape[2]
    count = lax.axis_size("ctx")
    where = lax.axis_index("ctx")
    chans = local // count
    scale = 1.0 / math.sqrt(count * rows)

    high = lax.reduce_precision(taps, 8, 7)
    low = (taps - high).astype(jnp.bfloat16)
    streams = jnp.concatenate([inputs, high.astype(jnp.bfloat16)[None], low[None]], axis=0)
    streams = streams.reshape(5, rows, count, chans).transpose(2, 0, 3, 1)
    streams = streams.reshape(count, 5 * chans, rows)
    other = lax.ppermute(grad_out, "tp", [(0, 1), (1, 0)])
    streams, other = lax.optimization_barrier((streams, other))
    streams = regroup(streams)

    first = lax.axis_index("tp") == 0
    whole = jnp.where(
        first,
        jnp.concatenate([grad_out, other], axis=1),
        jnp.concatenate([other, grad_out], axis=1),
    )
    gated = lax.dot_general(
        w_out, whole, (((1,), (1,)), ((), ())), preferred_element_type=jnp.float32
    )
    gated = regroup(gated.reshape(count, chans, rows)).reshape(count * chans, rows)

    weight = lax.dynamic_slice_in_dim(short_weight, where * chans, chans, axis=2)
    weight = jnp.broadcast_to(weight.reshape(9, chans, 1), (9, chans, rows))

    consts = [jnp.asarray(t) for t in tables(count, rows)]
    mixed, filt, prod, conv = stage_one(streams, weight, consts, scale)
    back = stage_two(gated, streams, mixed, filt, prod, conv, weight, consts, scale)

    back = regroup(back)
    inputs_grad, taps_grad = spread(back, chans)
    sums = back[:, 5 * chans :].astype(jnp.float32)
    sums = sums.reshape(count, 8 * rows)[:, : 27 * chans].reshape(count, 3, 9, chans)
    short_grad = jnp.sum(sums, axis=1).transpose(1, 0, 2).reshape(3, 3, local)
    return inputs_grad, taps_grad, short_grad


def solution(mesh):
    return jax.shard_map(
        shards,
        mesh=mesh,
        in_specs=(
            P(None, "ctx", "tp"),
            P(None, None, "tp"),
            P("ctx", "tp"),
            P("tp", None),
            P("ctx", "tp"),
        ),
        out_specs=(P(None, "ctx", "tp"), P("ctx", "tp"), P(None, None, "tp")),
        check_vma=False,
    )
```

```python
import math

import jax
import jax.numpy as jnp
import numpy as np
from jax import lax
from jax.experimental import pallas as pl
from jax.experimental.pallas import tpu as pltpu
from jax.sharding import PartitionSpec as P

GROUP = 16
UNROLL = 8
STEPS = 240


def split_np(x):
    high = x.astype(jnp.bfloat16)
    low = (x - high.astype(np.float64)).astype(jnp.bfloat16)
    return high, low


def tables(blocks, width):
    length = 2 * blocks * width
    n1 = np.arange(blocks)
    n2 = np.arange(width)
    angle = 2.0 * np.pi * np.outer(n1 + 0.5, n1) / (2 * blocks)
    first = np.concatenate([np.cos(angle), -np.sin(angle)], axis=0)
    high, low = split_np(first)
    first3 = np.concatenate([high, high, low], axis=1)
    last = first.T * (2.0 / length)
    high, low = split_np(last)
    last4 = np.concatenate(
        [
            np.concatenate([high, high], axis=1),
            np.concatenate([low, np.zeros_like(low)], axis=1),
        ],
        axis=0,
    )
    angle = 2.0 * np.pi * (np.outer(n2, n2) % width) / width
    cos, sin = np.cos(angle), np.sin(angle)
    forward = np.block([[cos, -sin], [sin, cos]])
    high, low = split_np(forward)
    forward2 = np.stack([high, low])
    backward = np.block([[cos, sin], [-sin, cos]])
    high, low = split_np(backward)
    backward2 = np.stack([high, low])
    angle = 2.0 * np.pi * np.outer(n1 + 0.5, n2) / length
    twiddle = np.stack([np.cos(angle), np.sin(angle)]).astype(np.float32)
    return first3, last4, forward2, backward2, twiddle


def split(x):
    high = x.astype(jnp.bfloat16)
    low = (x - high.astype(jnp.float32)).astype(jnp.bfloat16)
    return high, low


def limit(peak):
    return jnp.maximum(lax.reduce_precision(peak * (1.0 + 2.0**-7), 8, 7), 2.0**-100)


def encode(x, bound):
    root = jnp.minimum(jnp.sqrt(jnp.abs(x) * (1.0 / bound)), 1.0)
    n = jnp.floor(root * (STEPS * 128.0) + 0.5)
    high = jnp.floor(n * (1.0 / 128.0))
    code = jnp.exp2(high - STEPS / 2) * (1.0 + (n - 128.0 * high) * (1.0 / 128.0))
    return jnp.where(x < 0, -code, code).astype(jnp.bfloat16)


def decode(code, bound):
    code = code.astype(jnp.float32)
    size = jnp.abs(code)
    high = jnp.floor(jnp.log2(size))
    root = (high + size * jnp.exp2(-high) + (STEPS / 2 - 1.0)) * (1.0 / STEPS)
    size = root * root * bound
    return jnp.where(code < 0, -size, size)


def mm(a, b):
    return jnp.dot(a, b, preferred_element_type=jnp.float32)


def forward_rows(x_of, first_ref, cos, sin, blocks, width):
    rows = []
    for g in range(0, GROUP, 2):
        cols = []
        for h in (0, 1):
            high, low = split(x_of(g + h))
            cols.append(jnp.concatenate([high, low, high], axis=0))
        out = mm(first_ref[...], jnp.concatenate(cols, axis=1))
        for h in (0, 1):
            re = out[:blocks, h * width : (h + 1) * width]
            im = out[blocks:, h * width : (h + 1) * width]
            rows.append(jnp.concatenate([re * cos + im * sin, im * cos - re * sin], axis=1))
    return rows


def step_two(rows, table_ref):
    high, low = split(rows)
    return mm(high, table_ref[0]) + mm(low, table_ref[0]) + mm(high, table_ref[1])


def inverse_one(back, put, last_ref, cos, sin, blocks, width):
    for g in range(0, GROUP, 2):
        cols = []
        for h in (0, 1):
            at = (g + h) * blocks
            re = back[at : at + blocks, :width]
            im = back[at : at + blocks, width:]
            both = jnp.concatenate([re * cos - im * sin, re * sin + im * cos], axis=0)
            high, low = split(both)
            cols.append(jnp.concatenate([high, low], axis=0))
        out = mm(last_ref[...], jnp.concatenate(cols, axis=1))
        out = out[:blocks] + out[blocks:]
        for h in (0, 1):
            put(g + h, out[:, h * width : (h + 1) * width])


def times(a, b, width):
    ar, ai, br, bi = a[:, :width], a[:, width:], b[:, :width], b[:, width:]
    return jnp.concatenate([ar * br - ai * bi, ar * bi + ai * br], axis=1)


def conj_times(a, b, width):
    ar, ai, br, bi = a[:, :width], a[:, width:], b[:, :width], b[:, width:]
    return jnp.concatenate([ar * br + ai * bi, ar * bi - ai * br], axis=1)


def row_of(n1, chans):
    return pl.ds(pl.multiple_of(n1 * chans, chans), chans)


def lagged(in_ref, n1, b, chans, width):
    lane = lax.broadcasted_iota(jnp.int32, (chans, width), 1)
    at = pl.ds(b * chans, chans)
    cur = in_ref[n1, at, :].astype(jnp.float32)
    before = in_ref[jnp.maximum(n1 - 1, 0), at, :].astype(jnp.float32)
    before = jnp.where(n1 > 0, before, 0.0)
    return [cur] + [
        pltpu.roll(jnp.where(lane >= width - j, before, cur), j, 1) for j in (1, 2)
    ]


def mix(weight_ref, b, parts):
    return (
        weight_ref[3 * b] * parts[0]
        + weight_ref[3 * b + 1] * parts[1]
        + weight_ref[3 * b + 2] * parts[2]
    )


def coded(in_ref, n1, b, chans):
    bound = in_ref[n1, pl.ds((b + 1) * chans, 8), :].astype(jnp.float32)
    bound = jnp.concatenate([bound] * (chans // 8), axis=0)
    return decode(in_ref[n1, pl.ds(b * chans, chans), :], bound)


def ahead(weights, cur, follow, chans, width):
    lane = lax.broadcasted_iota(jnp.int32, (chans, width), 1)
    out = weights[0] * cur
    for j in (1, 2):
        moved = pltpu.roll(jnp.where(lane < j, follow, cur), width - j, 1)
        out = out + weights[j] * moved
    return out


def load_consts(sources, targets, sems):
    copies = [pltpu.make_async_copy(a, b, sems.at[i]) for i, (a, b) in enumerate(zip(sources, targets))]
    for copy in copies:
        copy.start()
    return copies


def first_kernel(scale, in_hbm, weight_ref, *refs):
    const_in, (mixed_out, filt_out, prod_out, conv_out) = refs[:5], refs[5:9]
    in_ref, src, mixed_ref, filt_ref, prod_ref, conv_ref = refs[9:15]
    consts, const_sems, in_sems, out_sems = refs[15:20], refs[20], refs[21], refs[22]
    first_ref, last_ref, forward_ref, backward_ref, twiddle_ref = consts
    blocks, width = in_ref.shape[0], in_ref.shape[2]
    chans = weight_ref.shape[1]

    def fetch(step):
        some = pl.ds(step * UNROLL, UNROLL)
        return pltpu.make_async_copy(in_hbm.at[some], in_ref.at[some], in_sems.at[step])

    for step in range(blocks // UNROLL):
        fetch(step).start()
    const_copies = load_consts(const_in, consts, const_sems)

    def prepare(step, carry):
        fetch(step).wait()
        for u in range(UNROLL):
            n1 = step * UNROLL + u
            at = row_of(n1, chans)
            mixed = []
            for b in range(2):
                mixed.append(mix(weight_ref, b + 1, lagged(in_ref, n1, b, chans, width)))
                mixed_ref[b, at, :] = mixed[b]
            src[0, at, :] = coded(in_ref, n1, 2, chans) * scale
            src[1, at, :] = mixed[0] * mixed[1]
        return carry

    lax.fori_loop(0, blocks // UNROLL, prepare, 0)
    mixed_copy = pltpu.make_async_copy(mixed_ref, mixed_out, out_sems.at[0])
    mixed_copy.start()
    for copy in const_copies:
        copy.wait()
    cos, sin = twiddle_ref[0], twiddle_ref[1]

    def convolve(step, carry):
        base = step * GROUP
        part = GROUP * blocks
        rows = []
        for s in range(2):
            rows += forward_rows(
                lambda g: src[s, pl.ds(base + g, blocks, stride=chans), :],
                first_ref,
                cos,
                sin,
                blocks,
                width,
            )
        spec = step_two(jnp.concatenate(rows, axis=0), forward_ref)
        at = row_of(step, part)
        filt_ref[at, :] = spec[:part]
        prod_ref[at, :] = spec[part:]
        pltpu.make_async_copy(filt_ref.at[at], filt_out.at[at], out_sems.at[1]).start()
        pltpu.make_async_copy(prod_ref.at[at], prod_out.at[at], out_sems.at[2]).start()
        back = step_two(times(spec[:part], spec[part:], width), backward_ref)

        def put(g, out):
            conv_ref[pl.ds(base + g, blocks, stride=chans), :] = out

        inverse_one(back, put, last_ref, cos, sin, blocks, width)
        return carry

    lax.fori_loop(0, chans // GROUP, convolve, 0)
    conv_copy = pltpu.make_async_copy(conv_ref, conv_out, out_sems.at[3])
    conv_copy.start()
    mixed_copy.wait()
    pltpu.make_async_copy(filt_ref, filt_out, out_sems.at[1]).wait()
    pltpu.make_async_copy(prod_ref, prod_out, out_sems.at[2]).wait()
    conv_copy.wait()


def last_kernel(scale, grad_in, streams_in, mixed_in, filt_in, prod_in, conv_in, weight_ref, *refs):
    const_in, out_hbm = refs[:5], refs[5]
    query_ref, in_ref, mixed_ref, filt_ref, prod_ref, conv_ref = refs[6:12]
    grad_ref, src, res, sums, peak, out_ref, tail_ref = refs[12:19]
    consts, const_sems, grad_sems, sems, spec_sems, out_sems = refs[19:24], *refs[24:29]
    first_ref, last_ref, forward_ref, backward_ref, twiddle_ref = consts
    blocks, width = in_ref.shape[0], in_ref.shape[2]
    chans = weight_ref.shape[1]
    lane = lax.broadcasted_iota(jnp.int32, (chans, width), 1)
    copies = [
        pltpu.make_async_copy(a, b, sems.at[i])
        for i, (a, b) in enumerate(
            ((mixed_in, mixed_ref), (conv_in, conv_ref), (streams_in, in_ref))
        )
    ]

    def fetch_grad(step):
        some = pl.ds(step * UNROLL, UNROLL)
        return pltpu.make_async_copy(grad_in.at[some], query_ref.at[some], grad_sems.at[step])

    def fetch(step):
        at = row_of(step, GROUP * blocks)
        return [
            pltpu.make_async_copy(a.at[at], b.at[at], spec_sems.at[i, step])
            for i, (a, b) in enumerate(((filt_in, filt_ref), (prod_in, prod_ref)))
        ]

    for step in range(blocks // UNROLL):
        fetch_grad(step).start()
    const_copies = load_consts(const_in, consts, const_sems)
    for copy in fetch(0):
        copy.start()

    def prepare(step, carry):
        fetch_grad(step).wait()
        for u in range(UNROLL):
            n1 = step * UNROLL + u
            at = row_of(n1, chans)
            grad = coded(query_ref, n1, 1, chans)
            grad_ref[at, :] = grad
            src[at, :] = grad * mix(weight_ref, 0, lagged(query_ref, n1, 0, chans, width))
        return carry

    lax.fori_loop(0, blocks // UNROLL, prepare, 0)
    peak[...] = jnp.zeros_like(peak)
    for copy in const_copies:
        copy.wait()
    cos, sin = twiddle_ref[0], twiddle_ref[1]
    steps = chans // GROUP

    def convolve(step, carry):
        base = step * GROUP
        part = GROUP * blocks

        def dy(g):
            return src[pl.ds(base + g, blocks, stride=chans), :]

        @pl.when(step + 1 < steps)
        def _():
            for copy in fetch(step + 1):
                copy.start()

        @pl.when(step + 1 == steps)
        def _():
            for copy in copies:
                copy.start()

        rows = forward_rows(dy, first_ref, cos, sin, blocks, width)
        spec = step_two(jnp.concatenate(rows, axis=0), forward_ref)
        at = row_of(step, part)
        for copy in fetch(step):
            copy.wait()
        both = [conj_times(r[at, :], spec, width) for r in (filt_ref, prod_ref)]
        back = step_two(jnp.concatenate(both, axis=0), backward_ref)
        for s in range(2):

            def put(g, out):
                res[s, pl.ds(base + g, blocks, stride=chans), :] = out
                if s == 1:
                    peak[...] = jnp.maximum(peak[...], jnp.abs(out))

            inverse_one(
                back[s * part : (s + 1) * part], put, last_ref, cos, sin, blocks, width
            )
        return carry

    lax.fori_loop(0, steps, convolve, 0)
    for copy in copies:
        copy.wait()

    def gradients(n1):
        at = row_of(n1, chans)
        dz = res[0, at, :]
        return [
            grad_ref[at, :] * conv_ref[at, :],
            dz * mixed_ref[1, at, :],
            dz * mixed_ref[0, at, :],
        ]

    sums[...] = jnp.zeros_like(sums)
    most = jnp.max(jnp.max(peak[...], axis=0, keepdims=True), axis=1, keepdims=True)
    most = jnp.maximum(most * scale * (1.0 + 2.0**-7), 2.0**-100)
    bound = jnp.broadcast_to(most.astype(jnp.bfloat16).astype(jnp.float32), (chans, width))

    def finish(step, cur):
        cur = list(cur)
        adds = [None] * 9
        for u in range(UNROLL):
            n1 = step * UNROLL + u
            at = row_of(n1, chans)
            follow = gradients(jnp.minimum(n1 + 1, blocks - 1))
            if u == UNROLL - 1:
                follow = [jnp.where(n1 + 1 < blocks, f, 0.0) for f in follow]
            for b in range(3):
                weights = [weight_ref[3 * b + j] for j in range(3)]
                out = ahead(weights, cur[b], follow[b], chans, width)
                out_ref[n1, pl.ds(b * chans, chans), :] = out.astype(jnp.bfloat16)
            out_ref[n1, pl.ds(3 * chans, chans), :] = encode(res[1, at, :] * scale, bound)
            for b in range(3):
                ref, place = (in_ref, b - 1) if b else (query_ref, 0)
                parts = lagged(ref, n1, place, chans, width)
                for j in range(3):
                    term = cur[b] * parts[j]
                    old = adds[3 * b + j]
                    adds[3 * b + j] = term if old is None else old + term
            cur = follow
        for t in range(9):
            sums[t] += adds[t]
        some = pl.ds(step * UNROLL, UNROLL)
        pltpu.make_async_copy(
            out_ref.at[some], out_hbm.at[some, pl.ds(0, 4 * chans)], out_sems.at[0]
        ).start()
        return tuple(cur)

    lax.fori_loop(0, blocks // UNROLL, finish, tuple(gradients(0)))

    total = jnp.zeros((chans, width), jnp.float32)
    for t in range(9):
        column = jnp.sum(sums[t], axis=1, keepdims=True) * scale
        total = total + jnp.where(lane == t, column, 0.0)
    per = width // chans
    total = jnp.concatenate([total] + [jnp.zeros_like(total)] * (per - 1), axis=0).T
    high = total.astype(jnp.bfloat16).astype(jnp.float32)
    mid = (total - high).astype(jnp.bfloat16).astype(jnp.float32)
    low = total - high - mid
    lines = [p[t : t + 1] for p in (high, mid, low) for t in range(9)]
    lines += [jnp.where(lane[:1] < chans, bound[:1], 0.0)] * (8 * per - 27)
    packed = []
    for r in range(8):
        row = jnp.zeros((1, width), jnp.float32)
        for a, line in enumerate(lines[per * r : per * r + per]):
            row = row + (pltpu.roll(line, a * chans, 1) if a else line)
        packed.append(row)
    packed = jnp.concatenate(packed, axis=0).astype(jnp.bfloat16)

    def attach(n1, carry):
        tail_ref[n1] = packed
        return carry

    lax.fori_loop(0, blocks, attach, 0)
    tail = pltpu.make_async_copy(
        tail_ref, out_hbm.at[:, pl.ds(4 * chans, 8)], out_sems.at[1]
    )
    tail.start()
    tail.wait()
    pltpu.make_async_copy(
        out_ref, out_hbm.at[:, pl.ds(0, 4 * chans)], out_sems.at[0]
    ).wait()


def f32(*shape):
    return jax.ShapeDtypeStruct(shape, jnp.float32)


def bf16(*shape):
    return jax.ShapeDtypeStruct(shape, jnp.bfloat16)


def estimate(us):
    return pl.CostEstimate(flops=int(us * 1e8), bytes_accessed=int(us * 3e6), transcendentals=0)


def params(mib):
    return pltpu.CompilerParams(vmem_limit_bytes=mib << 20)


def hbm():
    return pl.BlockSpec(memory_space=pltpu.HBM)


def vmem():
    return pl.BlockSpec(memory_space=pltpu.VMEM)


def hbm():
    return pl.BlockSpec(memory_space=pltpu.HBM)


def vmem():
    return pl.BlockSpec(memory_space=pltpu.VMEM)


def room(*arrays):
    return [pltpu.VMEM(a.shape, a.dtype) for a in arrays]


def stage_one(streams, weight, consts, scale):
    blocks, width = streams.shape[0], streams.shape[2]
    chans = weight.shape[1]
    rows = blocks * chans
    shapes = [f32(2, rows, width), f32(rows, 2 * width), f32(rows, 2 * width), f32(rows, width)]
    return pl.pallas_call(
        lambda *refs: first_kernel(scale, *refs),
        name="stage_one",
        out_shape=tuple(shapes),
        in_specs=[hbm(), vmem()] + [hbm()] * 5,
        out_specs=(hbm(),) * 4,
        scratch_shapes=room(streams, f32(2, rows, width), *shapes, *consts)
        + [
            pltpu.SemaphoreType.DMA((5,)),
            pltpu.SemaphoreType.DMA((blocks // UNROLL,)),
            pltpu.SemaphoreType.DMA((4,)),
        ],
        cost_estimate=estimate(14),
        compiler_params=params(60),
    )(streams, weight, *consts)


def stage_two(grad, streams, mixed, filt, prod, conv, weight, consts, scale):
    blocks, width = streams.shape[0], streams.shape[2]
    chans = weight.shape[1]
    rows = blocks * chans
    return pl.pallas_call(
        lambda *refs: last_kernel(scale, *refs),
        name="stage_two",
        out_shape=bf16(blocks, 4 * chans + 8, width),
        in_specs=[hbm()] * 6 + [vmem()] + [hbm()] * 5,
        out_specs=hbm(),
        scratch_shapes=room(
            grad,
            streams,
            mixed,
            filt,
            prod,
            conv,
            f32(rows, width),
            f32(rows, width),
            f32(2, rows, width),
            f32(9, chans, width),
            f32(blocks, width),
            bf16(blocks, 4 * chans, width),
            bf16(blocks, 8, width),
            *consts,
        )
        + [
            pltpu.SemaphoreType.DMA((5,)),
            pltpu.SemaphoreType.DMA((blocks // UNROLL,)),
            pltpu.SemaphoreType.DMA((3,)),
            pltpu.SemaphoreType.DMA((2, chans // GROUP)),
            pltpu.SemaphoreType.DMA((2,)),
        ],
        cost_estimate=estimate(14),
        compiler_params=params(60),
    )(grad, streams, mixed, filt, prod, conv, weight, *consts)


def spread_kernel(back_ref, ig_ref, tg_ref):
    some, _, width = back_ref.shape
    chans = width // some

    def part(i):
        rows = [back_ref[d, pl.ds(i * chans, chans), :].astype(jnp.float32) for d in range(some)]
        return jnp.concatenate(rows, axis=0)

    for b in range(3):
        ig_ref[b] = part(b).T.astype(jnp.bfloat16)
    rows = []
    for d in range(some):
        bound = back_ref[d, pl.ds(4 * chans, 8), :].astype(jnp.float32)[7:8]
        bound = jnp.broadcast_to(bound, (chans, width))
        rows.append(decode(back_ref[d, pl.ds(3 * chans, chans), :], bound))
    tg_ref[...] = jnp.concatenate(rows, axis=0).T


def spread(back, chans):
    count, height, width = back.shape
    some = width // chans
    return pl.pallas_call(
        spread_kernel,
        name="spread",
        grid=(count // some,),
        out_shape=(bf16(3, width, count * chans), f32(width, count * chans)),
        in_specs=[pl.BlockSpec((some, height, width), lambda i: (i, 0, 0))],
        out_specs=(
            pl.BlockSpec((3, width, width), lambda i: (0, 0, i)),
            pl.BlockSpec((width, width), lambda i: (0, i)),
        ),
        cost_estimate=estimate(4),
        compiler_params=params(16),
    )(back)


def regroup(x):
    return lax.all_to_all(x, "ctx", split_axis=0, concat_axis=0, tiled=True)


def shards(inputs, short_weight, taps, w_out, grad_out):
    rows, local = inputs.shape[1], inputs.shape[2]
    count = lax.axis_size("ctx")
    where = lax.axis_index("ctx")
    chans = local // count
    scale = 1.0 / math.sqrt(count * rows)

    def by_owner(x):
        return x.reshape(-1, rows, count, chans).transpose(2, 0, 3, 1).reshape(count, -1, rows)

    def with_bound(x, bound):
        bound = jnp.broadcast_to(bound.astype(jnp.bfloat16), (count, 8, rows))
        return jnp.concatenate([x, bound], axis=1)

    bound = limit(jnp.max(jnp.abs(taps)))
    streams = jnp.concatenate([inputs[1:], encode(taps, bound)[None]], axis=0)
    streams = with_bound(by_owner(streams), bound)
    other = lax.ppermute(grad_out, "tp", [(0, 1), (1, 0)])
    streams, other = lax.optimization_barrier((streams, other))
    streams = regroup(streams)

    first = lax.axis_index("tp") == 0
    whole = jnp.where(
        first,
        jnp.concatenate([grad_out, other], axis=1),
        jnp.concatenate([other, grad_out], axis=1),
    )
    gated = lax.dot_general(
        w_out, whole, (((1,), (1,)), ((), ())), preferred_element_type=jnp.float32
    )
    bound = limit(jnp.max(jnp.abs(gated)))
    gated = encode(gated, bound).reshape(count, chans, rows)
    gated = regroup(with_bound(jnp.concatenate([by_owner(inputs[:1]), gated], axis=1), bound))

    weight = lax.dynamic_slice_in_dim(short_weight, where * chans, chans, axis=2)
    weight = jnp.broadcast_to(weight.reshape(9, chans, 1), (9, chans, rows))

    consts = [jnp.asarray(t) for t in tables(count, rows)]
    mixed, filt, prod, conv = stage_one(streams, weight, consts, scale)
    back = stage_two(gated, streams, mixed, filt, prod, conv, weight, consts, scale)

    back = regroup(back)
    inputs_grad, taps_grad = spread(back, chans)
    sums = back[:, 4 * chans :].astype(jnp.float32)
    sums = sums.reshape(count, 8 * rows)[:, : 27 * chans].reshape(count, 3, 9, chans)
    short_grad = jnp.sum(sums, axis=1).transpose(1, 0, 2).reshape(3, 3, local)
    return inputs_grad, taps_grad, short_grad


def solution(mesh):
    return jax.shard_map(
        shards,
        mesh=mesh,
        in_specs=(
            P(None, "ctx", "tp"),
            P(None, None, "tp"),
            P("ctx", "tp"),
            P("tp", None),
            P("ctx", "tp"),
        ),
        out_specs=(P(None, "ctx", "tp"), P("ctx", "tp"), P(None, None, "tp")),
        check_vma=False,
    )
```

```python
import math

import jax
import jax.numpy as jnp
import numpy as np
from jax import lax
from jax.experimental import pallas as pl
from jax.experimental.pallas import tpu as pltpu
from jax.sharding import PartitionSpec as P

GROUP = 16
UNROLL = 8
STEPS = 240
CHUNKS = 4
PROJECT_US = 200


def split_np(x):
    high = x.astype(jnp.bfloat16)
    low = (x - high.astype(np.float64)).astype(jnp.bfloat16)
    return high, low


def tables(blocks, width):
    length = 2 * blocks * width
    n1 = np.arange(blocks)
    n2 = np.arange(width)
    angle = 2.0 * np.pi * np.outer(n1 + 0.5, n1) / (2 * blocks)
    first = np.concatenate([np.cos(angle), -np.sin(angle)], axis=0)
    high, low = split_np(first)
    first3 = np.concatenate([high, high, low], axis=1)
    last = first.T * (2.0 / length)
    high, low = split_np(last)
    last4 = np.concatenate(
        [
            np.concatenate([high, high], axis=1),
            np.concatenate([low, np.zeros_like(low)], axis=1),
        ],
        axis=0,
    )
    angle = 2.0 * np.pi * (np.outer(n2, n2) % width) / width
    cos, sin = np.cos(angle), np.sin(angle)
    forward = np.block([[cos, -sin], [sin, cos]])
    high, low = split_np(forward)
    forward2 = np.stack([high, low])
    backward = np.block([[cos, sin], [-sin, cos]])
    high, low = split_np(backward)
    backward2 = np.stack([high, low])
    angle = 2.0 * np.pi * np.outer(n1 + 0.5, n2) / length
    twiddle = np.stack([np.cos(angle), np.sin(angle)]).astype(np.float32)
    return first3, last4, forward2, backward2, twiddle


def split(x):
    high = x.astype(jnp.bfloat16)
    low = (x - high.astype(jnp.float32)).astype(jnp.bfloat16)
    return high, low


def encode(x, bound):
    root = jnp.minimum(jnp.sqrt(jnp.abs(x) * (1.0 / bound)), 1.0)
    n = jnp.floor(root * (STEPS * 128.0) + 0.5)
    high = jnp.floor(n * (1.0 / 128.0))
    code = jnp.exp2(high - STEPS / 2) * (1.0 + (n - 128.0 * high) * (1.0 / 128.0))
    return jnp.where(x < 0, -code, code).astype(jnp.bfloat16)


def decode(code, bound):
    code = code.astype(jnp.float32)
    size = jnp.abs(code)
    high = jnp.floor(jnp.log2(size))
    root = (high + size * jnp.exp2(-high) + (STEPS / 2 - 1.0)) * (1.0 / STEPS)
    size = root * root * bound
    return jnp.where(code < 0, -size, size)


def mm(a, b):
    return jnp.dot(a, b, preferred_element_type=jnp.float32)


def forward_rows(x_of, first_ref, cos, sin, blocks, width):
    rows = []
    for g in range(0, GROUP, 2):
        cols = []
        for h in (0, 1):
            high, low = split(x_of(g + h))
            cols.append(jnp.concatenate([high, low, high], axis=0))
        out = mm(first_ref[...], jnp.concatenate(cols, axis=1))
        for h in (0, 1):
            re = out[:blocks, h * width : (h + 1) * width]
            im = out[blocks:, h * width : (h + 1) * width]
            rows.append(jnp.concatenate([re * cos + im * sin, im * cos - re * sin], axis=1))
    return rows


def step_two(rows, table_ref):
    high, low = split(rows)
    return mm(high, table_ref[0]) + mm(low, table_ref[0]) + mm(high, table_ref[1])


def inverse_one(back, put, last_ref, cos, sin, blocks, width):
    for g in range(0, GROUP, 2):
        cols = []
        for h in (0, 1):
            at = (g + h) * blocks
            re = back[at : at + blocks, :width]
            im = back[at : at + blocks, width:]
            both = jnp.concatenate([re * cos - im * sin, re * sin + im * cos], axis=0)
            high, low = split(both)
            cols.append(jnp.concatenate([high, low], axis=0))
        out = mm(last_ref[...], jnp.concatenate(cols, axis=1))
        out = out[:blocks] + out[blocks:]
        for h in (0, 1):
            put(g + h, out[:, h * width : (h + 1) * width])


def times(a, b, width):
    ar, ai, br, bi = a[:, :width], a[:, width:], b[:, :width], b[:, width:]
    return jnp.concatenate([ar * br - ai * bi, ar * bi + ai * br], axis=1)


def conj_times(a, b, width):
    ar, ai, br, bi = a[:, :width], a[:, width:], b[:, :width], b[:, width:]
    return jnp.concatenate([ar * br + ai * bi, ar * bi - ai * br], axis=1)


def row_of(n1, chans):
    return pl.ds(pl.multiple_of(n1 * chans, chans), chans)


def lagged(in_ref, n1, b, chans, width):
    lane = lax.broadcasted_iota(jnp.int32, (chans, width), 1)
    at = pl.ds(b * chans, chans)
    cur = in_ref[n1, at, :].astype(jnp.float32)
    before = in_ref[jnp.maximum(n1 - 1, 0), at, :].astype(jnp.float32)
    before = jnp.where(n1 > 0, before, 0.0)
    return [cur] + [
        pltpu.roll(jnp.where(lane >= width - j, before, cur), j, 1) for j in (1, 2)
    ]


def mix(weight_ref, b, parts):
    return (
        weight_ref[3 * b] * parts[0]
        + weight_ref[3 * b + 1] * parts[1]
        + weight_ref[3 * b + 2] * parts[2]
    )


def coded(in_ref, n1, b, chans):
    bound = in_ref[n1, pl.ds((b + 1) * chans, 8), :].astype(jnp.float32)
    bound = jnp.concatenate([bound] * (chans // 8), axis=0)
    return decode(in_ref[n1, pl.ds(b * chans, chans), :], bound)


def ahead(weights, cur, follow, chans, width):
    lane = lax.broadcasted_iota(jnp.int32, (chans, width), 1)
    out = weights[0] * cur
    for j in (1, 2):
        moved = pltpu.roll(jnp.where(lane < j, follow, cur), width - j, 1)
        out = out + weights[j] * moved
    return out


def load_consts(sources, targets, sems):
    copies = [pltpu.make_async_copy(a, b, sems.at[i]) for i, (a, b) in enumerate(zip(sources, targets))]
    for copy in copies:
        copy.start()
    return copies


def first_kernel(scale, in_hbm, weight_ref, *refs):
    const_in, (mixed_out, filt_out, prod_out, conv_out) = refs[:5], refs[5:9]
    in_ref, src, mixed_ref, filt_ref, prod_ref, conv_ref = refs[9:15]
    consts, const_sems, in_sems, out_sems = refs[15:20], refs[20], refs[21], refs[22]
    first_ref, last_ref, forward_ref, backward_ref, twiddle_ref = consts
    blocks, width = in_ref.shape[0], in_ref.shape[2]
    chans = weight_ref.shape[1]

    def fetch(step):
        some = pl.ds(step * UNROLL, UNROLL)
        return pltpu.make_async_copy(in_hbm.at[some], in_ref.at[some], in_sems.at[step])

    for step in range(blocks // UNROLL):
        fetch(step).start()
    const_copies = load_consts(const_in, consts, const_sems)

    def prepare(step, carry):
        fetch(step).wait()
        for u in range(UNROLL):
            n1 = step * UNROLL + u
            at = row_of(n1, chans)
            mixed = []
            for b in range(2):
                mixed.append(mix(weight_ref, b + 1, lagged(in_ref, n1, b, chans, width)))
                mixed_ref[b, at, :] = mixed[b]
            src[0, at, :] = coded(in_ref, n1, 2, chans) * scale
            src[1, at, :] = mixed[0] * mixed[1]
        return carry

    lax.fori_loop(0, blocks // UNROLL, prepare, 0)
    mixed_copy = pltpu.make_async_copy(mixed_ref, mixed_out, out_sems.at[0])
    mixed_copy.start()
    for copy in const_copies:
        copy.wait()
    cos, sin = twiddle_ref[0], twiddle_ref[1]

    def convolve(step, carry):
        base = step * GROUP
        part = GROUP * blocks
        rows = []
        for s in range(2):
            rows += forward_rows(
                lambda g: src[s, pl.ds(base + g, blocks, stride=chans), :],
                first_ref,
                cos,
                sin,
                blocks,
                width,
            )
        spec = step_two(jnp.concatenate(rows, axis=0), forward_ref)
        at = row_of(step, part)
        filt_ref[at, :] = spec[:part]
        prod_ref[at, :] = spec[part:]
        pltpu.make_async_copy(filt_ref.at[at], filt_out.at[at], out_sems.at[1]).start()
        pltpu.make_async_copy(prod_ref.at[at], prod_out.at[at], out_sems.at[2]).start()
        back = step_two(times(spec[:part], spec[part:], width), backward_ref)

        def put(g, out):
            conv_ref[pl.ds(base + g, blocks, stride=chans), :] = out

        inverse_one(back, put, last_ref, cos, sin, blocks, width)
        return carry

    lax.fori_loop(0, chans // GROUP, convolve, 0)
    conv_copy = pltpu.make_async_copy(conv_ref, conv_out, out_sems.at[3])
    conv_copy.start()
    mixed_copy.wait()
    pltpu.make_async_copy(filt_ref, filt_out, out_sems.at[1]).wait()
    pltpu.make_async_copy(prod_ref, prod_out, out_sems.at[2]).wait()
    conv_copy.wait()


def last_kernel(scale, grad_in, streams_in, mixed_in, filt_in, prod_in, conv_in, weight_ref, *refs):
    const_in, out_hbm = refs[:5], refs[5]
    query_ref, in_ref, mixed_ref, filt_ref, prod_ref, conv_ref = refs[6:12]
    grad_ref, src, res, sums, peak, out_ref, tail_ref = refs[12:19]
    consts, const_sems, grad_sems, sems, spec_sems, out_sems = refs[19:24], *refs[24:29]
    first_ref, last_ref, forward_ref, backward_ref, twiddle_ref = consts
    blocks, width = in_ref.shape[0], in_ref.shape[2]
    chans = weight_ref.shape[1]
    lane = lax.broadcasted_iota(jnp.int32, (chans, width), 1)
    copies = [
        pltpu.make_async_copy(a, b, sems.at[i])
        for i, (a, b) in enumerate(
            ((mixed_in, mixed_ref), (conv_in, conv_ref), (streams_in, in_ref))
        )
    ]

    def fetch_grad(step):
        some = pl.ds(step * UNROLL, UNROLL)
        return pltpu.make_async_copy(grad_in.at[some], query_ref.at[some], grad_sems.at[step])

    def fetch(step):
        at = row_of(step, GROUP * blocks)
        return [
            pltpu.make_async_copy(a.at[at], b.at[at], spec_sems.at[i, step])
            for i, (a, b) in enumerate(((filt_in, filt_ref), (prod_in, prod_ref)))
        ]

    for step in range(blocks // UNROLL):
        fetch_grad(step).start()
    const_copies = load_consts(const_in, consts, const_sems)
    for copy in fetch(0):
        copy.start()

    def prepare(step, carry):
        fetch_grad(step).wait()
        for u in range(UNROLL):
            n1 = step * UNROLL + u
            at = row_of(n1, chans)
            grad = coded(query_ref, n1, 1, chans)
            grad_ref[at, :] = grad
            src[at, :] = grad * mix(weight_ref, 0, lagged(query_ref, n1, 0, chans, width))
        return carry

    lax.fori_loop(0, blocks // UNROLL, prepare, 0)
    peak[...] = jnp.zeros_like(peak)
    for copy in const_copies:
        copy.wait()
    cos, sin = twiddle_ref[0], twiddle_ref[1]
    steps = chans // GROUP

    def convolve(step, carry):
        base = step * GROUP
        part = GROUP * blocks

        def dy(g):
            return src[pl.ds(base + g, blocks, stride=chans), :]

        @pl.when(step + 1 < steps)
        def _():
            for copy in fetch(step + 1):
                copy.start()

        @pl.when(step + 1 == steps)
        def _():
            for copy in copies:
                copy.start()

        rows = forward_rows(dy, first_ref, cos, sin, blocks, width)
        spec = step_two(jnp.concatenate(rows, axis=0), forward_ref)
        at = row_of(step, part)
        for copy in fetch(step):
            copy.wait()
        both = [conj_times(r[at, :], spec, width) for r in (filt_ref, prod_ref)]
        back = step_two(jnp.concatenate(both, axis=0), backward_ref)
        for s in range(2):

            def put(g, out):
                res[s, pl.ds(base + g, blocks, stride=chans), :] = out
                if s == 1:
                    peak[...] = jnp.maximum(peak[...], jnp.abs(out))

            inverse_one(
                back[s * part : (s + 1) * part], put, last_ref, cos, sin, blocks, width
            )
        return carry

    lax.fori_loop(0, steps, convolve, 0)
    for copy in copies:
        copy.wait()

    def gradients(n1):
        at = row_of(n1, chans)
        dz = res[0, at, :]
        return [
            grad_ref[at, :] * conv_ref[at, :],
            dz * mixed_ref[1, at, :],
            dz * mixed_ref[0, at, :],
        ]

    sums[...] = jnp.zeros_like(sums)
    most = jnp.max(jnp.max(peak[...], axis=0, keepdims=True), axis=1, keepdims=True)
    most = jnp.maximum(most * scale * (1.0 + 2.0**-7), 2.0**-100)
    bound = jnp.broadcast_to(most.astype(jnp.bfloat16).astype(jnp.float32), (chans, width))

    def finish(step, cur):
        cur = list(cur)
        adds = [None] * 9
        for u in range(UNROLL):
            n1 = step * UNROLL + u
            at = row_of(n1, chans)
            follow = gradients(jnp.minimum(n1 + 1, blocks - 1))
            if u == UNROLL - 1:
                follow = [jnp.where(n1 + 1 < blocks, f, 0.0) for f in follow]
            for b in range(3):
                weights = [weight_ref[3 * b + j] for j in range(3)]
                out = ahead(weights, cur[b], follow[b], chans, width)
                out_ref[n1, pl.ds(b * chans, chans), :] = out.astype(jnp.bfloat16)
            out_ref[n1, pl.ds(3 * chans, chans), :] = encode(res[1, at, :] * scale, bound)
            for b in range(3):
                ref, place = (in_ref, b - 1) if b else (query_ref, 0)
                parts = lagged(ref, n1, place, chans, width)
                for j in range(3):
                    term = cur[b] * parts[j]
                    old = adds[3 * b + j]
                    adds[3 * b + j] = term if old is None else old + term
            cur = follow
        for t in range(9):
            sums[t] += adds[t]
        some = pl.ds(step * UNROLL, UNROLL)
        pltpu.make_async_copy(
            out_ref.at[some], out_hbm.at[some, pl.ds(0, 4 * chans)], out_sems.at[0]
        ).start()
        return tuple(cur)

    lax.fori_loop(0, blocks // UNROLL, finish, tuple(gradients(0)))

    total = jnp.zeros((chans, width), jnp.float32)
    for t in range(9):
        column = jnp.sum(sums[t], axis=1, keepdims=True) * scale
        total = total + jnp.where(lane == t, column, 0.0)
    per = width // chans
    total = jnp.concatenate([total] + [jnp.zeros_like(total)] * (per - 1), axis=0).T
    high = total.astype(jnp.bfloat16).astype(jnp.float32)
    mid = (total - high).astype(jnp.bfloat16).astype(jnp.float32)
    low = total - high - mid
    lines = [p[t : t + 1] for p in (high, mid, low) for t in range(9)]
    lines += [jnp.where(lane[:1] < chans, bound[:1], 0.0)] * (8 * per - 27)
    packed = []
    for r in range(8):
        row = jnp.zeros((1, width), jnp.float32)
        for a, line in enumerate(lines[per * r : per * r + per]):
            row = row + (pltpu.roll(line, a * chans, 1) if a else line)
        packed.append(row)
    packed = jnp.concatenate(packed, axis=0).astype(jnp.bfloat16)

    def attach(n1, carry):
        tail_ref[n1] = packed
        return carry

    lax.fori_loop(0, blocks, attach, 0)
    tail = pltpu.make_async_copy(
        tail_ref, out_hbm.at[:, pl.ds(4 * chans, 8)], out_sems.at[1]
    )
    tail.start()
    tail.wait()
    pltpu.make_async_copy(
        out_ref, out_hbm.at[:, pl.ds(0, 4 * chans)], out_sems.at[0]
    ).wait()


def f32(*shape):
    return jax.ShapeDtypeStruct(shape, jnp.float32)


def bf16(*shape):
    return jax.ShapeDtypeStruct(shape, jnp.bfloat16)


def estimate(us):
    return pl.CostEstimate(flops=int(us * 1e8), bytes_accessed=int(us * 3e6), transcendentals=0)


def params(mib):
    return pltpu.CompilerParams(vmem_limit_bytes=mib << 20)


def hbm():
    return pl.BlockSpec(memory_space=pltpu.HBM)


def vmem():
    return pl.BlockSpec(memory_space=pltpu.VMEM)


def hbm():
    return pl.BlockSpec(memory_space=pltpu.HBM)


def vmem():
    return pl.BlockSpec(memory_space=pltpu.VMEM)


def room(*arrays):
    return [pltpu.VMEM(a.shape, a.dtype) for a in arrays]


def stage_one(streams, weight, consts, scale):
    blocks, width = streams.shape[0], streams.shape[2]
    chans = weight.shape[1]
    rows = blocks * chans
    shapes = [f32(2, rows, width), f32(rows, 2 * width), f32(rows, 2 * width), f32(rows, width)]
    return pl.pallas_call(
        lambda *refs: first_kernel(scale, *refs),
        name="stage_one",
        out_shape=tuple(shapes),
        in_specs=[hbm(), vmem()] + [hbm()] * 5,
        out_specs=(hbm(),) * 4,
        scratch_shapes=room(streams, f32(2, rows, width), *shapes, *consts)
        + [
            pltpu.SemaphoreType.DMA((5,)),
            pltpu.SemaphoreType.DMA((blocks // UNROLL,)),
            pltpu.SemaphoreType.DMA((4,)),
        ],
        cost_estimate=estimate(14),
        compiler_params=params(60),
    )(streams, weight, *consts)


def stage_two(grad, streams, mixed, filt, prod, conv, weight, consts, scale):
    blocks, width = streams.shape[0], streams.shape[2]
    chans = weight.shape[1]
    rows = blocks * chans
    return pl.pallas_call(
        lambda *refs: last_kernel(scale, *refs),
        name="stage_two",
        out_shape=bf16(blocks, 4 * chans + 8, width),
        in_specs=[hbm()] * 6 + [vmem()] + [hbm()] * 5,
        out_specs=hbm(),
        scratch_shapes=room(
            grad,
            streams,
            mixed,
            filt,
            prod,
            conv,
            f32(rows, width),
            f32(rows, width),
            f32(2, rows, width),
            f32(9, chans, width),
            f32(blocks, width),
            bf16(blocks, 4 * chans, width),
            bf16(blocks, 8, width),
            *consts,
        )
        + [
            pltpu.SemaphoreType.DMA((5,)),
            pltpu.SemaphoreType.DMA((blocks // UNROLL,)),
            pltpu.SemaphoreType.DMA((3,)),
            pltpu.SemaphoreType.DMA((2, chans // GROUP)),
            pltpu.SemaphoreType.DMA((2,)),
        ],
        cost_estimate=estimate(14),
        compiler_params=params(61),
    )(grad, streams, mixed, filt, prod, conv, weight, *consts)


def spread_kernel(back_ref, ig_hbm, tg_hbm, ig_ref, tg_ref, sems):
    count, _, width = back_ref.shape
    total = tg_ref.shape[1]
    chans = total // count
    some = width // chans
    wide = total // CHUNKS

    def copies(part):
        cols = pl.ds(part * wide, wide)
        return [
            pltpu.make_async_copy(a.at[..., cols], b.at[..., cols], sems.at[i, part])
            for i, (a, b) in enumerate(((ig_ref, ig_hbm), (tg_ref, tg_hbm)))
        ]

    for part in range(CHUNKS):
        for m in range(part * wide // width, (part + 1) * wide // width):
            cols = pl.ds(m * width, width)
            owners = range(m * some, (m + 1) * some)
            for b in range(3):
                rows = [back_ref[d, pl.ds(b * chans, chans), :] for d in owners]
                rows = jnp.concatenate(rows, axis=0).astype(jnp.float32)
                ig_ref[b, :, cols] = rows.T.astype(jnp.bfloat16)
            rows = []
            for d in owners:
                bound = back_ref[d, pl.ds(4 * chans, 8), :].astype(jnp.float32)[7:8]
                bound = jnp.broadcast_to(bound, (chans, width))
                rows.append(decode(back_ref[d, pl.ds(3 * chans, chans), :], bound))
            tg_ref[:, cols] = jnp.concatenate(rows, axis=0).T
        for copy in copies(part):
            copy.start()
    for part in range(CHUNKS):
        for copy in copies(part):
            copy.wait()


def spread(back, chans):
    count, _, width = back.shape
    outs = (bf16(3, width, count * chans), f32(width, count * chans))
    return pl.pallas_call(
        spread_kernel,
        name="spread",
        out_shape=outs,
        in_specs=[vmem()],
        out_specs=(hbm(), hbm()),
        scratch_shapes=room(*outs) + [pltpu.SemaphoreType.DMA((2, CHUNKS))],
        cost_estimate=estimate(4),
        compiler_params=params(24),
    )(back)


def collect_kernel(in_hbm, taps_hbm, out_hbm, query_hbm, in_ref, taps_ref, out_ref, query_ref, sems):
    total = taps_ref.shape[1]
    count, chans, width = query_ref.shape
    some = width // chans
    wide = total // CHUNKS
    owners = count // CHUNKS
    taps_copy = pltpu.make_async_copy(taps_hbm, taps_ref, sems.at[3, 0])
    taps_copy.start()

    def fetch(part):
        cols = pl.ds(part * wide, wide)
        return pltpu.make_async_copy(in_hbm.at[..., cols], in_ref.at[..., cols], sems.at[0, part])

    def puts(part):
        these = pl.ds(part * owners, owners)
        return [
            pltpu.make_async_copy(a.at[these], b.at[these], sems.at[1 + i, part])
            for i, (a, b) in enumerate(((out_ref, out_hbm), (query_ref, query_hbm)))
        ]

    for part in range(CHUNKS):
        fetch(part).start()
    taps_copy.wait()
    most = jnp.max(jnp.abs(taps_ref[...]), axis=0, keepdims=True)
    most = jnp.max(most, axis=1, keepdims=True)
    most = jnp.maximum(most * (1.0 + 2.0**-7), 2.0**-100).astype(jnp.bfloat16)
    mark = jnp.broadcast_to(most, (8, width))
    bound = jnp.broadcast_to(most.astype(jnp.float32), (width, width))
    for part in range(CHUNKS):
        fetch(part).wait()
        for m in range(part * wide // width, (part + 1) * wide // width):
            cols = pl.ds(m * width, width)
            blocks = [in_ref[b, :, cols].astype(jnp.float32).T.astype(jnp.bfloat16) for b in range(3)]
            blocks.append(encode(taps_ref[:, cols].T, bound))
            for h in range(some):
                d = m * some + h
                at = slice(h * chans, (h + 1) * chans)
                query_ref[d] = blocks[0][at]
                for b in range(3):
                    out_ref[d, pl.ds(b * chans, chans), :] = blocks[b + 1][at]
                out_ref[d, pl.ds(3 * chans, 8), :] = mark
        for copy in puts(part):
            copy.start()
    for part in range(CHUNKS):
        for copy in puts(part):
            copy.wait()


def collect(inputs, taps, count):
    rows, total = taps.shape
    chans = total // count
    outs = (bf16(count, 3 * chans + 8, rows), bf16(count, chans, rows))
    return pl.pallas_call(
        collect_kernel,
        name="collect",
        out_shape=outs,
        in_specs=[hbm(), hbm()],
        out_specs=(hbm(), hbm()),
        scratch_shapes=room(inputs, taps, *outs) + [pltpu.SemaphoreType.DMA((4, CHUNKS))],
        cost_estimate=estimate(5),
        compiler_params=params(60),
    )(inputs, taps)


def project_kernel(which_ref, own_w, other_w, own_ref, other_ref, query_ref, out_ref, grad, peak):
    step = pl.program_id(0)
    rows, width = own_w.shape[0], own_ref.shape[0]
    count, chans, _ = query_ref.shape

    def part(a, b):
        return lax.dot_general(
            a[...], b[...], (((1,), (1,)), ((), ())), preferred_element_type=jnp.float32
        )

    block = part(own_w, own_ref) + part(other_w, other_ref)
    grad[pl.ds(pl.multiple_of(step * rows, rows), rows), :] = block
    most = jnp.max(jnp.abs(block), axis=0, keepdims=True)

    @pl.when(step == 0)
    def _():
        peak[...] = jnp.broadcast_to(most, peak.shape)

    @pl.when(step > 0)
    def _():
        peak[...] = jnp.maximum(peak[...], most)

    @pl.when(step == pl.num_programs(0) - 1)
    def _():
        most = jnp.max(peak[...], axis=1, keepdims=True)
        most = jnp.maximum(most * (1.0 + 2.0**-7), 2.0**-100).astype(jnp.bfloat16)
        mark = jnp.broadcast_to(most, (8, width))
        bound = jnp.broadcast_to(most[:1].astype(jnp.float32), (chans, width))

        def fill(i, carry):
            for u in range(UNROLL):
                d = i * UNROLL + u
                out_ref[d, pl.ds(0, chans), :] = query_ref[d]
                out_ref[d, pl.ds(chans, chans), :] = encode(grad[row_of(d, chans), :], bound)
                out_ref[d, pl.ds(2 * chans, 8), :] = mark
            return carry

        lax.fori_loop(0, count // UNROLL, fill, 0)


def project(which, w_out, own, other, query):
    count, chans, rows = query.shape
    depth = own.shape[1]
    tile = 256
    whole = lambda shape: pl.BlockSpec(shape, lambda i, which: (0,) * len(shape))
    return pl.pallas_call(
        project_kernel,
        name="project",
        grid_spec=pltpu.PrefetchScalarGridSpec(
            num_scalar_prefetch=1,
            grid=(w_out.shape[0] // tile,),
            in_specs=[
                pl.BlockSpec((tile, depth), lambda i, which: (i, which[0])),
                pl.BlockSpec((tile, depth), lambda i, which: (i, 1 - which[0])),
                whole(own.shape),
                whole(other.shape),
                whole(query.shape),
            ],
            out_specs=whole((count, 2 * chans + 8, rows)),
            scratch_shapes=[
                pltpu.VMEM((count * chans, rows), jnp.float32),
                pltpu.VMEM((8, rows), jnp.float32),
            ],
        ),
        out_shape=bf16(count, 2 * chans + 8, rows),
        cost_estimate=estimate(PROJECT_US),
        compiler_params=params(40),
    )(which, w_out, w_out, own, other, query)


def regroup(x):
    return lax.all_to_all(x, "ctx", split_axis=0, concat_axis=0, tiled=True)


def shards(inputs, short_weight, taps, w_out, grad_out):
    rows, local = inputs.shape[1], inputs.shape[2]
    count = lax.axis_size("ctx")
    where = lax.axis_index("ctx")
    chans = local // count
    scale = 1.0 / math.sqrt(count * rows)

    streams, query = collect(inputs, taps, count)
    other = lax.ppermute(grad_out, "tp", [(0, 1), (1, 0)])
    streams = regroup(streams)
    which = lax.axis_index("tp").astype(jnp.int32).reshape(1)
    gated = regroup(project(which, w_out, grad_out, other, query))

    weight = lax.dynamic_slice_in_dim(short_weight, where * chans, chans, axis=2)
    weight = jnp.broadcast_to(weight.reshape(9, chans, 1), (9, chans, rows))

    consts = [jnp.asarray(t) for t in tables(count, rows)]
    mixed, filt, prod, conv = stage_one(streams, weight, consts, scale)
    back = stage_two(gated, streams, mixed, filt, prod, conv, weight, consts, scale)

    back = regroup(back)
    inputs_grad, taps_grad = spread(back, chans)
    sums = back[:, 4 * chans :].astype(jnp.float32)
    sums = sums.reshape(count, 8 * rows)[:, : 27 * chans].reshape(count, 3, 9, chans)
    short_grad = jnp.sum(sums, axis=1).transpose(1, 0, 2).reshape(3, 3, local)
    return inputs_grad, taps_grad, short_grad


def solution(mesh):
    return jax.shard_map(
        shards,
        mesh=mesh,
        in_specs=(
            P(None, "ctx", "tp"),
            P(None, None, "tp"),
            P("ctx", "tp"),
            P("tp", None),
            P("ctx", "tp"),
        ),
        out_specs=(P(None, "ctx", "tp"), P("ctx", "tp"), P(None, None, "tp")),
        check_vma=False,
    )
```

```python
import math

import jax
import jax.numpy as jnp
import numpy as np
from jax import lax
from jax.experimental import pallas as pl
from jax.experimental.pallas import tpu as pltpu
from jax.sharding import PartitionSpec as P

GROUP = 16
UNROLL = 8
STEPS = 240
CHUNKS = 4
PROJECT_US = 200


def split_np(x):
    high = x.astype(jnp.bfloat16)
    low = (x - high.astype(np.float64)).astype(jnp.bfloat16)
    return high, low


def tables(blocks, width):
    length = 2 * blocks * width
    n1 = np.arange(blocks)
    n2 = np.arange(width)
    angle = 2.0 * np.pi * np.outer(n1 + 0.5, n1) / (2 * blocks)
    first = np.concatenate([np.cos(angle), -np.sin(angle)], axis=0)
    high, low = split_np(first)
    first3 = np.concatenate([high, high, low], axis=1)
    last = first.T * (2.0 / length)
    high, low = split_np(last)
    last4 = np.concatenate(
        [
            np.concatenate([high, high], axis=1),
            np.concatenate([low, np.zeros_like(low)], axis=1),
        ],
        axis=0,
    )
    angle = 2.0 * np.pi * (np.outer(n2, n2) % width) / width
    cos, sin = np.cos(angle), np.sin(angle)
    forward = np.block([[cos, -sin], [sin, cos]])
    high, low = split_np(forward)
    forward2 = np.stack([high, low])
    backward = np.block([[cos, sin], [-sin, cos]])
    high, low = split_np(backward)
    backward2 = np.stack([high, low])
    angle = 2.0 * np.pi * np.outer(n1 + 0.5, n2) / length
    twiddle = np.stack([np.cos(angle), np.sin(angle)]).astype(np.float32)
    return first3, last4, forward2, backward2, twiddle


def split(x):
    high = x.astype(jnp.bfloat16)
    low = (x - high.astype(jnp.float32)).astype(jnp.bfloat16)
    return high, low


def encode(x, bound):
    root = jnp.minimum(jnp.sqrt(jnp.abs(x) * (1.0 / bound)), 1.0)
    n = jnp.floor(root * (STEPS * 128.0) + 0.5)
    high = jnp.floor(n * (1.0 / 128.0))
    code = jnp.exp2(high - STEPS / 2) * (1.0 + (n - 128.0 * high) * (1.0 / 128.0))
    return jnp.where(x < 0, -code, code).astype(jnp.bfloat16)


def decode(code, bound):
    code = code.astype(jnp.float32)
    size = jnp.abs(code)
    high = jnp.floor(jnp.log2(size))
    root = (high + size * jnp.exp2(-high) + (STEPS / 2 - 1.0)) * (1.0 / STEPS)
    size = root * root * bound
    return jnp.where(code < 0, -size, size)


def mm(a, b):
    return jnp.dot(a, b, preferred_element_type=jnp.float32)


def forward_rows(x_of, first_ref, cos, sin, blocks, width):
    rows = []
    for g in range(0, GROUP, 2):
        cols = []
        for h in (0, 1):
            high, low = split(x_of(g + h))
            cols.append(jnp.concatenate([high, low, high], axis=0))
        out = mm(first_ref[...], jnp.concatenate(cols, axis=1))
        for h in (0, 1):
            re = out[:blocks, h * width : (h + 1) * width]
            im = out[blocks:, h * width : (h + 1) * width]
            rows.append(jnp.concatenate([re * cos + im * sin, im * cos - re * sin], axis=1))
    return rows


def step_two(rows, table_ref):
    high, low = split(rows)
    return mm(high, table_ref[0]) + mm(low, table_ref[0]) + mm(high, table_ref[1])


def inverse_one(back, put, last_ref, cos, sin, blocks, width):
    for g in range(0, GROUP, 2):
        cols = []
        for h in (0, 1):
            at = (g + h) * blocks
            re = back[at : at + blocks, :width]
            im = back[at : at + blocks, width:]
            both = jnp.concatenate([re * cos - im * sin, re * sin + im * cos], axis=0)
            high, low = split(both)
            cols.append(jnp.concatenate([high, low], axis=0))
        out = mm(last_ref[...], jnp.concatenate(cols, axis=1))
        out = out[:blocks] + out[blocks:]
        for h in (0, 1):
            put(g + h, out[:, h * width : (h + 1) * width])


def times(a, b, width):
    ar, ai, br, bi = a[:, :width], a[:, width:], b[:, :width], b[:, width:]
    return jnp.concatenate([ar * br - ai * bi, ar * bi + ai * br], axis=1)


def conj_times(a, b, width):
    ar, ai, br, bi = a[:, :width], a[:, width:], b[:, :width], b[:, width:]
    return jnp.concatenate([ar * br + ai * bi, ar * bi - ai * br], axis=1)


def row_of(n1, chans):
    return pl.ds(pl.multiple_of(n1 * chans, chans), chans)


def lagged(in_ref, n1, b, chans, width):
    lane = lax.broadcasted_iota(jnp.int32, (chans, width), 1)
    at = pl.ds(b * chans, chans)
    cur = in_ref[n1, at, :].astype(jnp.float32)
    before = in_ref[jnp.maximum(n1 - 1, 0), at, :].astype(jnp.float32)
    before = jnp.where(n1 > 0, before, 0.0)
    return [cur] + [
        pltpu.roll(jnp.where(lane >= width - j, before, cur), j, 1) for j in (1, 2)
    ]


def mix(weight_ref, b, parts):
    return (
        weight_ref[3 * b] * parts[0]
        + weight_ref[3 * b + 1] * parts[1]
        + weight_ref[3 * b + 2] * parts[2]
    )


def coded(in_ref, n1, b, chans):
    bound = in_ref[n1, pl.ds((b + 1) * chans, 8), :].astype(jnp.float32)
    bound = jnp.concatenate([bound] * (chans // 8), axis=0)
    return decode(in_ref[n1, pl.ds(b * chans, chans), :], bound)


def ahead(weights, cur, follow, chans, width):
    lane = lax.broadcasted_iota(jnp.int32, (chans, width), 1)
    out = weights[0] * cur
    for j in (1, 2):
        moved = pltpu.roll(jnp.where(lane < j, follow, cur), width - j, 1)
        out = out + weights[j] * moved
    return out


def load_consts(sources, targets, sems):
    copies = [pltpu.make_async_copy(a, b, sems.at[i]) for i, (a, b) in enumerate(zip(sources, targets))]
    for copy in copies:
        copy.start()
    return copies


def first_kernel(scale, in_hbm, weight_ref, *refs):
    const_in, (mixed_out, filt_out, prod_out, conv_out, edge_out) = refs[:5], refs[5:10]
    in_ref, src, mixed_ref, filt_ref, prod_ref, conv_ref, edge_ref = refs[10:17]
    consts, const_sems, in_sems, out_sems = refs[17:22], refs[22], refs[23], refs[24]
    first_ref, last_ref, forward_ref, backward_ref, twiddle_ref = consts
    blocks, width = in_ref.shape[0], in_ref.shape[2]
    chans = weight_ref.shape[1]

    def fetch(step):
        some = pl.ds(step * UNROLL, UNROLL)
        return pltpu.make_async_copy(in_hbm.at[some], in_ref.at[some], in_sems.at[step])

    for step in range(blocks // UNROLL):
        fetch(step).start()
    const_copies = load_consts(const_in, consts, const_sems)

    def prepare(step, carry):
        fetch(step).wait()
        for u in range(UNROLL):
            n1 = step * UNROLL + u
            at = row_of(n1, chans)
            mixed = []
            for b in range(2):
                mixed.append(mix(weight_ref, b + 1, lagged(in_ref, n1, b, chans, width)))
                mixed_ref[b, at, :] = mixed[b]
            src[0, at, :] = coded(in_ref, n1, 2, chans) * scale
            src[1, at, :] = mixed[0] * mixed[1]
        return carry

    lax.fori_loop(0, blocks // UNROLL, prepare, 0)
    mixed_copy = pltpu.make_async_copy(mixed_ref, mixed_out, out_sems.at[0])
    mixed_copy.start()

    row = lax.broadcasted_iota(jnp.int32, (8, width), 0)
    group = lax.broadcasted_iota(jnp.int32, (8, width), 1) // chans

    def edges(step, carry):
        for u in range(0, UNROLL, 2):
            n1 = step * UNROLL + u
            two = [in_ref[n1 + h, pl.ds(0, 2 * chans), :].astype(jnp.float32) for h in (0, 1)]
            turned = jnp.concatenate(two, axis=0).T
            ends = (turned[width - 8 :], turned[:8])
            for h in (0, 1):
                tile = jnp.zeros((8, width), jnp.float32)
                for i, (end, stream, down) in enumerate(
                    ((0, 0, 2), (0, 1, 4), (1, 0, 4), (1, 1, 6))
                ):
                    part = pltpu.roll(ends[end], down, 0)
                    shift = (3 - 2 * h - stream) % 4 * chans
                    part = pltpu.roll(part, shift, 1) if shift else part
                    tile = jnp.where((row // 2 == i) & (group == 3), part, tile)
                edge_ref[n1 + h] = tile
        return carry

    lax.fori_loop(0, blocks // UNROLL, edges, 0)
    edge_copy = pltpu.make_async_copy(edge_ref, edge_out, out_sems.at[4])
    edge_copy.start()
    for copy in const_copies:
        copy.wait()
    cos, sin = twiddle_ref[0], twiddle_ref[1]

    def convolve(step, carry):
        base = step * GROUP
        part = GROUP * blocks
        rows = []
        for s in range(2):
            rows += forward_rows(
                lambda g: src[s, pl.ds(base + g, blocks, stride=chans), :],
                first_ref,
                cos,
                sin,
                blocks,
                width,
            )
        spec = step_two(jnp.concatenate(rows, axis=0), forward_ref)
        at = row_of(step, part)
        filt_ref[at, :] = spec[:part]
        prod_ref[at, :] = spec[part:]
        pltpu.make_async_copy(filt_ref.at[at], filt_out.at[at], out_sems.at[1]).start()
        pltpu.make_async_copy(prod_ref.at[at], prod_out.at[at], out_sems.at[2]).start()
        back = step_two(times(spec[:part], spec[part:], width), backward_ref)

        def put(g, out):
            conv_ref[pl.ds(base + g, blocks, stride=chans), :] = out

        inverse_one(back, put, last_ref, cos, sin, blocks, width)
        return carry

    lax.fori_loop(0, chans // GROUP, convolve, 0)
    conv_copy = pltpu.make_async_copy(conv_ref, conv_out, out_sems.at[3])
    conv_copy.start()
    mixed_copy.wait()
    edge_copy.wait()
    pltpu.make_async_copy(filt_ref, filt_out, out_sems.at[1]).wait()
    pltpu.make_async_copy(prod_ref, prod_out, out_sems.at[2]).wait()
    conv_copy.wait()


def last_kernel(scale, grad_in, streams_in, mixed_in, filt_in, prod_in, conv_in, edge_in, weight_ref, *refs):
    const_in, out_hbm = refs[:5], refs[5]
    query_ref, in_ref, mixed_ref, filt_ref, prod_ref, conv_ref = refs[6:12]
    grad_ref, src, res, sums, peak, halo, lines, edge_ref, out_ref, tail_ref = refs[12:22]
    consts, const_sems, grad_sems, sems, spec_sems, out_sems = refs[22:27], *refs[27:32]
    first_ref, last_ref, forward_ref, backward_ref, twiddle_ref = consts
    blocks, width = in_ref.shape[0], in_ref.shape[2]
    chans = weight_ref.shape[1]
    lane = lax.broadcasted_iota(jnp.int32, (chans, width), 1)
    copies = [
        pltpu.make_async_copy(a, b, sems.at[i])
        for i, (a, b) in enumerate(
            (
                (mixed_in, mixed_ref),
                (conv_in, conv_ref),
                (streams_in, in_ref),
                (edge_in, edge_ref.at[pl.ds(1, blocks)]),
            )
        )
    ]

    def fetch_grad(step):
        some = pl.ds(step * UNROLL, UNROLL)
        return pltpu.make_async_copy(grad_in.at[some], query_ref.at[some], grad_sems.at[step])

    def fetch(step):
        at = row_of(step, GROUP * blocks)
        return [
            pltpu.make_async_copy(a.at[at], b.at[at], spec_sems.at[i, step])
            for i, (a, b) in enumerate(((filt_in, filt_ref), (prod_in, prod_ref)))
        ]

    for step in range(blocks // UNROLL):
        fetch_grad(step).start()
    const_copies = load_consts(const_in, consts, const_sems)
    for copy in fetch(0):
        copy.start()

    def prepare(step, carry):
        fetch_grad(step).wait()
        for u in range(UNROLL):
            n1 = step * UNROLL + u
            at = row_of(n1, chans)
            grad = coded(query_ref, n1, 1, chans)
            grad_ref[at, :] = grad
            src[at, :] = grad * mix(weight_ref, 0, lagged(query_ref, n1, 0, chans, width))
        return carry

    lax.fori_loop(0, blocks // UNROLL, prepare, 0)
    peak[...] = jnp.zeros_like(peak)
    halo[...] = jnp.zeros_like(halo)
    column = lax.broadcasted_iota(jnp.int32, (blocks, width), 1)
    for copy in const_copies:
        copy.wait()
    cos, sin = twiddle_ref[0], twiddle_ref[1]
    steps = chans // GROUP

    def convolve(step, carry):
        base = step * GROUP
        part = GROUP * blocks

        def dy(g):
            return src[pl.ds(base + g, blocks, stride=chans), :]

        @pl.when(step + 1 < steps)
        def _():
            for copy in fetch(step + 1):
                copy.start()

        @pl.when(step + 1 == steps)
        def _():
            for copy in copies:
                copy.start()

        rows = forward_rows(dy, first_ref, cos, sin, blocks, width)
        spec = step_two(jnp.concatenate(rows, axis=0), forward_ref)
        at = row_of(step, part)
        for copy in fetch(step):
            copy.wait()
        both = [conj_times(r[at, :], spec, width) for r in (filt_ref, prod_ref)]
        back = step_two(jnp.concatenate(both, axis=0), backward_ref)
        for s in range(2):

            def put(g, out):
                res[s, pl.ds(base + g, blocks, stride=chans), :] = out
                peak[s] = jnp.maximum(peak[s], jnp.abs(out))
                if s == 0:
                    for p in range(2):
                        halo[p] = jnp.where(column == base + g, out[:, p : p + 1], halo[p])

            inverse_one(
                back[s * part : (s + 1) * part], put, last_ref, cos, sin, blocks, width
            )
        return carry

    lax.fori_loop(0, steps, convolve, 0)
    for copy in copies:
        copy.wait()

    def query_grad(n1):
        at = row_of(n1, chans)
        return grad_ref[at, :] * conv_ref[at, :]

    sums[...] = jnp.zeros_like(sums)

    def most(i):
        peak_i = jnp.max(jnp.max(peak[i], axis=0, keepdims=True), axis=1, keepdims=True)
        peak_i = jnp.maximum(peak_i * (scale if i else 1.0) * (1.0 + 2.0**-7), 2.0**-100)
        peak_i = peak_i.astype(jnp.bfloat16).astype(jnp.float32)
        return jnp.broadcast_to(peak_i, (chans, width))

    bounds = [most(0), most(1)]

    def finish(step, cur):
        adds = [None] * 9
        for u in range(UNROLL):
            n1 = step * UNROLL + u
            at = row_of(n1, chans)
            follow = query_grad(jnp.minimum(n1 + 1, blocks - 1))
            if u == UNROLL - 1:
                follow = jnp.where(n1 + 1 < blocks, follow, 0.0)
            weights = [weight_ref[j] for j in range(3)]
            out = ahead(weights, cur, follow, chans, width)
            dz = res[0, at, :]
            out_ref[n1, pl.ds(0, chans), :] = out.astype(jnp.bfloat16)
            out_ref[n1, pl.ds(chans, chans), :] = encode(dz, bounds[0])
            out_ref[n1, pl.ds(2 * chans, chans), :] = encode(res[1, at, :] * scale, bounds[1])
            full = [cur, dz * mixed_ref[1, at, :], dz * mixed_ref[0, at, :]]
            for b in range(3):
                ref, place = (in_ref, b - 1) if b else (query_ref, 0)
                parts = lagged(ref, n1, place, chans, width)
                for j in range(3):
                    term = full[b] * parts[j]
                    old = adds[3 * b + j]
                    adds[3 * b + j] = term if old is None else old + term
            cur = follow
        for t in range(9):
            sums[t] += adds[t]
        some = pl.ds(step * UNROLL, UNROLL)
        pltpu.make_async_copy(
            out_ref.at[some], out_hbm.at[some, pl.ds(0, 3 * chans)], out_sems.at[0]
        ).start()
        return cur

    lax.fori_loop(0, blocks // UNROLL, finish, query_grad(0))

    edge_ref[0] = jnp.zeros(edge_ref.shape[1:], jnp.float32)
    edge_ref[blocks + 1] = jnp.zeros(edge_ref.shape[1:], jnp.float32)
    total = jnp.zeros((chans, width), jnp.float32)
    for t in range(9):
        column = jnp.sum(sums[t], axis=1, keepdims=True) * scale
        total = total + jnp.where(lane == t, column, 0.0)
    pad = [jnp.zeros_like(total)] * (width // chans - 1)
    total = jnp.concatenate([total] + pad, axis=0).T
    high, low = [p.astype(jnp.float32) for p in split(total)]
    row = lax.broadcasted_iota(jnp.int32, (8, width), 0)
    group = lax.broadcasted_iota(jnp.int32, (8, width), 1) // chans
    fixed = high[:8] + pltpu.roll(low[:8], chans, 1)
    extra = jnp.where(row == 0, high[8:9], 0.0) + jnp.where(row == 1, low[8:9], 0.0)
    extra = jnp.where(row == 6, bounds[1][:1], extra)
    extra = jnp.where(row == 7, bounds[0][:1], extra)
    extra = pltpu.roll(jnp.where(group == 0, extra, 0.0), 2 * chans, 1)
    fixed = fixed + extra
    for p in range(2):
        high, low = [x.astype(jnp.float32) for x in split(halo[p])]
        lines[p, pl.ds(0, blocks), :] = pltpu.roll(high, 2 * chans, 1)
        lines[2 + p, pl.ds(0, blocks), :] = pltpu.roll(low, 2 * chans, 1)
        lines[p, pl.ds(blocks, 8), :] = jnp.zeros((8, width), jnp.float32)
        lines[2 + p, pl.ds(blocks, 8), :] = jnp.zeros((8, width), jnp.float32)

    def attach(n1, carry):
        tile = fixed
        for i in range(4):
            tile = tile + jnp.where(row == 2 + i, lines[i, pl.ds(n1 + 1, 1), :], 0.0)
        tile = tile + jnp.where(row < 4, edge_ref[n1], edge_ref[n1 + 2])
        tail_ref[n1] = tile.astype(jnp.bfloat16)
        return carry

    lax.fori_loop(0, blocks, attach, 0)
    tail = pltpu.make_async_copy(
        tail_ref, out_hbm.at[:, pl.ds(3 * chans, 8)], out_sems.at[1]
    )
    tail.start()
    tail.wait()
    pltpu.make_async_copy(
        out_ref, out_hbm.at[:, pl.ds(0, 3 * chans)], out_sems.at[0]
    ).wait()


def f32(*shape):
    return jax.ShapeDtypeStruct(shape, jnp.float32)


def bf16(*shape):
    return jax.ShapeDtypeStruct(shape, jnp.bfloat16)


def estimate(us):
    return pl.CostEstimate(flops=int(us * 1e8), bytes_accessed=int(us * 3e6), transcendentals=0)


def params(mib):
    return pltpu.CompilerParams(vmem_limit_bytes=mib << 20)


def hbm():
    return pl.BlockSpec(memory_space=pltpu.HBM)


def vmem():
    return pl.BlockSpec(memory_space=pltpu.VMEM)


def hbm():
    return pl.BlockSpec(memory_space=pltpu.HBM)


def vmem():
    return pl.BlockSpec(memory_space=pltpu.VMEM)


def room(*arrays):
    return [pltpu.VMEM(a.shape, a.dtype) for a in arrays]


def stage_one(streams, weight, consts, scale):
    blocks, width = streams.shape[0], streams.shape[2]
    chans = weight.shape[1]
    rows = blocks * chans
    shapes = [f32(2, rows, width), f32(rows, 2 * width), f32(rows, 2 * width), f32(rows, width)]
    shapes.append(f32(blocks, 8, width))
    return pl.pallas_call(
        lambda *refs: first_kernel(scale, *refs),
        name="stage_one",
        out_shape=tuple(shapes),
        in_specs=[hbm(), vmem()] + [hbm()] * 5,
        out_specs=(hbm(),) * 5,
        scratch_shapes=room(streams, f32(2, rows, width), *shapes, *consts)
        + [
            pltpu.SemaphoreType.DMA((5,)),
            pltpu.SemaphoreType.DMA((blocks // UNROLL,)),
            pltpu.SemaphoreType.DMA((5,)),
        ],
        cost_estimate=estimate(14),
        compiler_params=params(60),
    )(streams, weight, *consts)


def stage_two(grad, streams, mixed, filt, prod, conv, edge, weight, consts, scale):
    blocks, width = streams.shape[0], streams.shape[2]
    chans = weight.shape[1]
    rows = blocks * chans
    return pl.pallas_call(
        lambda *refs: last_kernel(scale, *refs),
        name="stage_two",
        out_shape=bf16(blocks, 3 * chans + 8, width),
        in_specs=[hbm()] * 7 + [vmem()] + [hbm()] * 5,
        out_specs=hbm(),
        scratch_shapes=room(
            grad,
            streams,
            mixed,
            filt,
            prod,
            conv,
            f32(rows, width),
            f32(rows, width),
            f32(2, rows, width),
            f32(9, chans, width),
            f32(2, blocks, width),
            f32(2, blocks, width),
            f32(4, blocks + 8, width),
            f32(blocks + 2, 8, width),
            bf16(blocks, 3 * chans, width),
            bf16(blocks, 8, width),
            *consts,
        )
        + [
            pltpu.SemaphoreType.DMA((5,)),
            pltpu.SemaphoreType.DMA((blocks // UNROLL,)),
            pltpu.SemaphoreType.DMA((4,)),
            pltpu.SemaphoreType.DMA((2, chans // GROUP)),
            pltpu.SemaphoreType.DMA((2,)),
        ],
        cost_estimate=estimate(14),
        compiler_params=params(61),
    )(grad, streams, mixed, filt, prod, conv, edge, weight, *consts)


def spread_kernel(back_ref, in_hbm, weight_ref, ig_hbm, tg_hbm, sg_ref, in_ref, ig_ref, tg_ref, sems):
    count, _, width = back_ref.shape
    total = tg_ref.shape[1]
    chans = total // count
    some = width // chans
    wide = total // CHUNKS
    row = lax.broadcasted_iota(jnp.int32, (8, width), 0)
    group = lax.broadcasted_iota(jnp.int32, (8, width), 1) // chans

    def fetch(part):
        cols = pl.ds(part * wide, wide)
        return pltpu.make_async_copy(
            in_hbm.at[pl.ds(1, 2), :, cols], in_ref.at[..., cols], sems.at[2, part]
        )

    def copies(part):
        cols = pl.ds(part * wide, wide)
        return [
            pltpu.make_async_copy(a.at[..., cols], b.at[..., cols], sems.at[i, part])
            for i, (a, b) in enumerate(((ig_ref, ig_hbm), (tg_ref, tg_hbm)))
        ]

    for part in range(CHUNKS):
        fetch(part).start()
    for part in range(CHUNKS):
        fetch(part).wait()
        for m in range(part * wide // width, (part + 1) * wide // width):
            cols = pl.ds(m * width, width)
            owners = range(m * some, (m + 1) * some)
            parts = []
            for i in range(3):
                rows = [back_ref[d, pl.ds(i * chans, chans), :] for d in owners]
                parts.append(jnp.concatenate(rows, axis=0).astype(jnp.float32).T)
            ig_ref[0, :, cols] = parts[0].astype(jnp.bfloat16)
            sums = jnp.zeros((8, width), jnp.float32)
            extra = jnp.zeros((8, width), jnp.float32)
            edge = jnp.zeros((8, width), jnp.float32)
            for a, d in enumerate(owners):
                tile = back_ref[d, pl.ds(3 * chans, 8), :].astype(jnp.float32)
                turned = [pltpu.roll(tile, (a - i) % some * chans, 1) if a != i else tile for i in range(4)]
                sums = jnp.where(group == a, turned[0] + turned[1], sums)
                extra = jnp.where(group == a, turned[2], extra)
                edge = jnp.where(group == a, turned[3], edge)
            for t in range(9):
                line = sums[t : t + 1] if t < 8 else extra[:1] + extra[1:2]
                sg_ref[t // 3, pl.ds(t % 3, 1), cols] = line
            tg_ref[:, cols] = decode(parts[2], extra[6:7])
            dz = decode(parts[1], extra[7:8])
            after = pltpu.roll(extra, 6, 0) + pltpu.roll(extra, 4, 0)
            dz = jnp.concatenate([dz, jnp.where(row < 2, after, 0.0)], axis=0)
            weights = [[weight_ref[b, pl.ds(j, 1), cols] for j in range(3)] for b in range(3)]
            for b in (1, 2):
                other = 3 - b
                x = jnp.concatenate(
                    [
                        pltpu.roll(edge, 8 - 2 * other, 0),
                        in_ref[other - 1, :, cols].astype(jnp.float32),
                        pltpu.roll(edge, 6 - 2 * other, 0),
                    ],
                    axis=0,
                )
                mixed = weights[other][0] * x
                for j in (1, 2):
                    mixed = mixed + weights[other][j] * pltpu.roll(x, j, 0)
                dm = dz * mixed[8:]
                out = weights[b][0] * dm
                for j in (1, 2):
                    out = out + weights[b][j] * pltpu.roll(dm, dm.shape[0] - j, 0)
                ig_ref[b, :, cols] = out[:width].astype(jnp.bfloat16)
        for copy in copies(part):
            copy.start()
    for part in range(CHUNKS):
        for copy in copies(part):
            copy.wait()


def spread(back, inputs, weight):
    rows, total = inputs.shape[1:]
    outs = (bf16(3, rows, total), f32(rows, total))
    return pl.pallas_call(
        spread_kernel,
        name="spread",
        out_shape=outs + (f32(*weight.shape),),
        in_specs=[vmem(), hbm(), vmem()],
        out_specs=(hbm(), hbm(), vmem()),
        scratch_shapes=room(bf16(2, rows, total), *outs) + [pltpu.SemaphoreType.DMA((3, CHUNKS))],
        cost_estimate=estimate(5),
        compiler_params=params(24),
    )(back, inputs, weight)


def collect_kernel(in_hbm, taps_hbm, out_hbm, query_hbm, in_ref, taps_ref, out_ref, query_ref, sems):
    total = taps_ref.shape[1]
    count, chans, width = query_ref.shape
    some = width // chans
    wide = total // CHUNKS
    owners = count // CHUNKS
    taps_copy = pltpu.make_async_copy(taps_hbm, taps_ref, sems.at[3, 0])
    taps_copy.start()

    def fetch(part):
        cols = pl.ds(part * wide, wide)
        return pltpu.make_async_copy(in_hbm.at[..., cols], in_ref.at[..., cols], sems.at[0, part])

    def puts(part):
        these = pl.ds(part * owners, owners)
        return [
            pltpu.make_async_copy(a.at[these], b.at[these], sems.at[1 + i, part])
            for i, (a, b) in enumerate(((out_ref, out_hbm), (query_ref, query_hbm)))
        ]

    for part in range(CHUNKS):
        fetch(part).start()
    taps_copy.wait()
    most = jnp.max(jnp.abs(taps_ref[...]), axis=0, keepdims=True)
    most = jnp.max(most, axis=1, keepdims=True)
    most = jnp.maximum(most * (1.0 + 2.0**-7), 2.0**-100).astype(jnp.bfloat16)
    mark = jnp.broadcast_to(most, (8, width))
    bound = jnp.broadcast_to(most.astype(jnp.float32), (width, width))
    for part in range(CHUNKS):
        fetch(part).wait()
        for m in range(part * wide // width, (part + 1) * wide // width):
            cols = pl.ds(m * width, width)
            blocks = [in_ref[b, :, cols].astype(jnp.float32).T.astype(jnp.bfloat16) for b in range(3)]
            blocks.append(encode(taps_ref[:, cols].T, bound))
            for h in range(some):
                d = m * some + h
                at = slice(h * chans, (h + 1) * chans)
                query_ref[d] = blocks[0][at]
                for b in range(3):
                    out_ref[d, pl.ds(b * chans, chans), :] = blocks[b + 1][at]
                out_ref[d, pl.ds(3 * chans, 8), :] = mark
        for copy in puts(part):
            copy.start()
    for part in range(CHUNKS):
        for copy in puts(part):
            copy.wait()


def collect(inputs, taps, count):
    rows, total = taps.shape
    chans = total // count
    outs = (bf16(count, 3 * chans + 8, rows), bf16(count, chans, rows))
    return pl.pallas_call(
        collect_kernel,
        name="collect",
        out_shape=outs,
        in_specs=[hbm(), hbm()],
        out_specs=(hbm(), hbm()),
        scratch_shapes=room(inputs, taps, *outs) + [pltpu.SemaphoreType.DMA((4, CHUNKS))],
        cost_estimate=estimate(5),
        compiler_params=params(60),
    )(inputs, taps)


def project_kernel(which_ref, own_w, other_w, own_ref, other_ref, query_ref, out_ref, grad, peak):
    step = pl.program_id(0)
    rows, width = own_w.shape[0], own_ref.shape[0]
    count, chans, _ = query_ref.shape

    def part(a, b):
        return lax.dot_general(
            a[...], b[...], (((1,), (1,)), ((), ())), preferred_element_type=jnp.float32
        )

    block = part(own_w, own_ref) + part(other_w, other_ref)
    grad[pl.ds(pl.multiple_of(step * rows, rows), rows), :] = block
    most = jnp.max(jnp.abs(block), axis=0, keepdims=True)

    @pl.when(step == 0)
    def _():
        peak[...] = jnp.broadcast_to(most, peak.shape)

    @pl.when(step > 0)
    def _():
        peak[...] = jnp.maximum(peak[...], most)

    @pl.when(step == pl.num_programs(0) - 1)
    def _():
        most = jnp.max(peak[...], axis=1, keepdims=True)
        most = jnp.maximum(most * (1.0 + 2.0**-7), 2.0**-100).astype(jnp.bfloat16)
        mark = jnp.broadcast_to(most, (8, width))
        bound = jnp.broadcast_to(most[:1].astype(jnp.float32), (chans, width))

        def fill(i, carry):
            for u in range(UNROLL):
                d = i * UNROLL + u
                out_ref[d, pl.ds(0, chans), :] = query_ref[d]
                out_ref[d, pl.ds(chans, chans), :] = encode(grad[row_of(d, chans), :], bound)
                out_ref[d, pl.ds(2 * chans, 8), :] = mark
            return carry

        lax.fori_loop(0, count // UNROLL, fill, 0)


def project(which, w_out, own, other, query):
    count, chans, rows = query.shape
    depth = own.shape[1]
    tile = 256
    whole = lambda shape: pl.BlockSpec(shape, lambda i, which: (0,) * len(shape))
    return pl.pallas_call(
        project_kernel,
        name="project",
        grid_spec=pltpu.PrefetchScalarGridSpec(
            num_scalar_prefetch=1,
            grid=(w_out.shape[0] // tile,),
            in_specs=[
                pl.BlockSpec((tile, depth), lambda i, which: (i, which[0])),
                pl.BlockSpec((tile, depth), lambda i, which: (i, 1 - which[0])),
                whole(own.shape),
                whole(other.shape),
                whole(query.shape),
            ],
            out_specs=whole((count, 2 * chans + 8, rows)),
            scratch_shapes=[
                pltpu.VMEM((count * chans, rows), jnp.float32),
                pltpu.VMEM((8, rows), jnp.float32),
            ],
        ),
        out_shape=bf16(count, 2 * chans + 8, rows),
        cost_estimate=estimate(PROJECT_US),
        compiler_params=params(40),
    )(which, w_out, w_out, own, other, query)


def regroup(x):
    return lax.all_to_all(x, "ctx", split_axis=0, concat_axis=0, tiled=True)


def shards(inputs, short_weight, taps, w_out, grad_out):
    rows, local = inputs.shape[1], inputs.shape[2]
    count = lax.axis_size("ctx")
    where = lax.axis_index("ctx")
    chans = local // count
    scale = 1.0 / math.sqrt(count * rows)

    streams, query = collect(inputs, taps, count)
    other = lax.ppermute(grad_out, "tp", [(0, 1), (1, 0)])
    streams = regroup(streams)
    which = lax.axis_index("tp").astype(jnp.int32).reshape(1)
    gated = project(which, w_out, grad_out, other, query)
    gated = regroup(gated)

    weight = lax.dynamic_slice_in_dim(short_weight, where * chans, chans, axis=2)
    weight = jnp.broadcast_to(weight.reshape(9, chans, 1), (9, chans, rows))

    consts = [jnp.asarray(t) for t in tables(count, rows)]
    mixed, filt, prod, conv, edge = stage_one(streams, weight, consts, scale)
    back = stage_two(gated, streams, mixed, filt, prod, conv, edge, weight, consts, scale)

    back = regroup(back)
    return spread(back, inputs, short_weight)


def solution(mesh):
    return jax.shard_map(
        shards,
        mesh=mesh,
        in_specs=(
            P(None, "ctx", "tp"),
            P(None, None, "tp"),
            P("ctx", "tp"),
            P("tp", None),
            P("ctx", "tp"),
        ),
        out_specs=(P(None, "ctx", "tp"), P("ctx", "tp"), P(None, None, "tp")),
        check_vma=False,
    )
```

```python
import math

import jax
import jax.numpy as jnp
import numpy as np
from jax import lax
from jax.experimental import pallas as pl
from jax.experimental.pallas import tpu as pltpu
from jax.sharding import PartitionSpec as P

GROUP = 16
UNROLL = 8
STEPS = 240
CHUNKS = 4
ONE_MIB = 60
TWO_MIB = 62
PROJECT_US = 200


def split_np(x):
    high = x.astype(jnp.bfloat16)
    low = (x - high.astype(np.float64)).astype(jnp.bfloat16)
    return high, low


def tables(blocks, width):
    length = 2 * blocks * width
    n1 = np.arange(blocks)
    n2 = np.arange(width)
    angle = 2.0 * np.pi * np.outer(n1 + 0.5, n1) / (2 * blocks)
    first = np.concatenate([np.cos(angle), -np.sin(angle)], axis=0)
    high, low = split_np(first)
    first3 = np.concatenate([high, high, low], axis=1)
    last = first.T * (2.0 / length)
    high, low = split_np(last)
    last4 = np.concatenate(
        [
            np.concatenate([high, high], axis=1),
            np.concatenate([low, np.zeros_like(low)], axis=1),
        ],
        axis=0,
    )
    angle = 2.0 * np.pi * (np.outer(n2, n2) % width) / width
    cos, sin = np.cos(angle), np.sin(angle)
    forward = np.block([[cos, -sin], [sin, cos]])
    high, low = split_np(forward)
    forward2 = np.stack([high, low])
    backward = np.block([[cos, sin], [-sin, cos]])
    high, low = split_np(backward)
    backward2 = np.stack([high, low])
    angle = 2.0 * np.pi * np.outer(n1 + 0.5, n2) / length
    twiddle = np.stack([np.cos(angle), np.sin(angle)]).astype(np.float32)
    return first3, last4, forward2, backward2, twiddle


def split(x):
    high = x.astype(jnp.bfloat16)
    low = (x - high.astype(jnp.float32)).astype(jnp.bfloat16)
    return high, low


def encode(x, inverse):
    root = jnp.minimum(jnp.sqrt(jnp.abs(x) * inverse), 1.0)
    n = jnp.floor(root * (STEPS * 128.0) + 0.5)
    high = jnp.floor(n * (1.0 / 128.0))
    code = jnp.exp2(high - STEPS / 2) * (1.0 + (n - 128.0 * high) * (1.0 / 128.0))
    return jnp.where(x < 0, -code, code).astype(jnp.bfloat16)


def decode(code, bound):
    code = code.astype(jnp.float32)
    size = jnp.abs(code)
    high = jnp.floor(jnp.log2(size))
    root = (high + size * jnp.exp2(-high) + (STEPS / 2 - 1.0)) * (1.0 / STEPS)
    size = root * root * bound
    return jnp.where(code < 0, -size, size)


def mm(a, b):
    return jnp.dot(a, b, preferred_element_type=jnp.float32)


def forward_rows(x_of, first_ref, cos, sin, blocks, width):
    rows = []
    for g in range(0, GROUP, 2):
        cols = []
        for h in (0, 1):
            high, low = split(x_of(g + h))
            cols.append(jnp.concatenate([high, low, high], axis=0))
        out = mm(first_ref[...], jnp.concatenate(cols, axis=1))
        for h in (0, 1):
            re = out[:blocks, h * width : (h + 1) * width]
            im = out[blocks:, h * width : (h + 1) * width]
            rows.append(jnp.concatenate([re * cos + im * sin, im * cos - re * sin], axis=1))
    return rows


def step_two(rows, table_ref):
    high, low = split(rows)
    return mm(high, table_ref[0]) + mm(low, table_ref[0]) + mm(high, table_ref[1])


def inverse_one(back, put, last_ref, cos, sin, blocks, width):
    for g in range(0, GROUP, 2):
        cols = []
        for h in (0, 1):
            at = (g + h) * blocks
            re = back[at : at + blocks, :width]
            im = back[at : at + blocks, width:]
            both = jnp.concatenate([re * cos - im * sin, re * sin + im * cos], axis=0)
            high, low = split(both)
            cols.append(jnp.concatenate([high, low], axis=0))
        out = mm(last_ref[...], jnp.concatenate(cols, axis=1))
        out = out[:blocks] + out[blocks:]
        for h in (0, 1):
            put(g + h, out[:, h * width : (h + 1) * width])


def times(a, b, width):
    ar, ai, br, bi = a[:, :width], a[:, width:], b[:, :width], b[:, width:]
    return jnp.concatenate([ar * br - ai * bi, ar * bi + ai * br], axis=1)


def conj_times(a, b, width):
    ar, ai, br, bi = a[:, :width], a[:, width:], b[:, :width], b[:, width:]
    return jnp.concatenate([ar * br + ai * bi, ar * bi - ai * br], axis=1)


def row_of(n1, chans):
    return pl.ds(pl.multiple_of(n1 * chans, chans), chans)


def lagged(in_ref, n1, b, chans, width):
    lane = lax.broadcasted_iota(jnp.int32, (chans, width), 1)
    at = pl.ds(b * chans, chans)
    cur = in_ref[n1, at, :].astype(jnp.float32)
    before = in_ref[jnp.maximum(n1 - 1, 0), at, :].astype(jnp.float32)
    before = jnp.where(n1 > 0, before, 0.0)
    return [cur] + [
        pltpu.roll(jnp.where(lane >= width - j, before, cur), j, 1) for j in (1, 2)
    ]


def mix(weight_ref, b, parts):
    return (
        weight_ref[3 * b] * parts[0]
        + weight_ref[3 * b + 1] * parts[1]
        + weight_ref[3 * b + 2] * parts[2]
    )


def coded(in_ref, n1, b, chans):
    bound = in_ref[n1, pl.ds((b + 1) * chans, 8), :].astype(jnp.float32)
    bound = jnp.broadcast_to(bound[:, :1], bound.shape)
    bound = jnp.concatenate([bound] * (chans // 8), axis=0)
    return decode(in_ref[n1, pl.ds(b * chans, chans), :], bound)


def ahead(weights, cur, follow, chans, width):
    lane = lax.broadcasted_iota(jnp.int32, (chans, width), 1)
    out = weights[0] * cur
    for j in (1, 2):
        moved = pltpu.roll(jnp.where(lane < j, follow, cur), width - j, 1)
        out = out + weights[j] * moved
    return out


def load_consts(sources, targets, sems):
    copies = [pltpu.make_async_copy(a, b, sems.at[i]) for i, (a, b) in enumerate(zip(sources, targets))]
    for copy in copies:
        copy.start()
    return copies


def first_kernel(scale, in_hbm, weight_ref, *refs):
    const_in, (mixed_out, filt_out, prod_out, conv_out) = refs[:5], refs[5:9]
    in_ref, src, mixed_ref, filt_ref, prod_ref, conv_ref = refs[9:15]
    consts, const_sems, in_sems, out_sems = refs[15:20], refs[20], refs[21], refs[22]
    first_ref, last_ref, forward_ref, backward_ref, twiddle_ref = consts
    blocks, width = in_ref.shape[0], in_ref.shape[2]
    chans = weight_ref.shape[1]

    def fetch(step):
        some = pl.ds(step * UNROLL, UNROLL)
        return pltpu.make_async_copy(in_hbm.at[some], in_ref.at[some], in_sems.at[step])

    for step in range(blocks // UNROLL):
        fetch(step).start()
    const_copies = load_consts(const_in, consts, const_sems)

    def prepare(step, carry):
        fetch(step).wait()
        for u in range(UNROLL):
            n1 = step * UNROLL + u
            at = row_of(n1, chans)
            mixed = []
            for b in range(2):
                mixed.append(mix(weight_ref, b + 1, lagged(in_ref, n1, b, chans, width)))
                mixed_ref[b, at, :] = mixed[b]
            src[0, at, :] = coded(in_ref, n1, 2, chans) * scale
            src[1, at, :] = mixed[0] * mixed[1]
        return carry

    lax.fori_loop(0, blocks // UNROLL, prepare, 0)
    mixed_copy = pltpu.make_async_copy(mixed_ref, mixed_out, out_sems.at[0])
    mixed_copy.start()
    for copy in const_copies:
        copy.wait()
    cos, sin = twiddle_ref[0], twiddle_ref[1]

    def convolve(step, carry):
        base = step * GROUP
        part = GROUP * blocks
        rows = []
        for s in range(2):
            rows += forward_rows(
                lambda g: src[s, pl.ds(base + g, blocks, stride=chans), :],
                first_ref,
                cos,
                sin,
                blocks,
                width,
            )
        spec = step_two(jnp.concatenate(rows, axis=0), forward_ref)
        at = row_of(step, part)
        filt_ref[at, :] = spec[:part]
        prod_ref[at, :] = spec[part:]
        pltpu.make_async_copy(filt_ref.at[at], filt_out.at[at], out_sems.at[1]).start()
        pltpu.make_async_copy(prod_ref.at[at], prod_out.at[at], out_sems.at[2]).start()
        back = step_two(times(spec[:part], spec[part:], width), backward_ref)

        def put(g, out):
            conv_ref[pl.ds(base + g, blocks, stride=chans), :] = out

        inverse_one(back, put, last_ref, cos, sin, blocks, width)
        return carry

    lax.fori_loop(0, chans // GROUP, convolve, 0)
    conv_copy = pltpu.make_async_copy(conv_ref, conv_out, out_sems.at[3])
    conv_copy.start()
    mixed_copy.wait()
    pltpu.make_async_copy(filt_ref, filt_out, out_sems.at[1]).wait()
    pltpu.make_async_copy(prod_ref, prod_out, out_sems.at[2]).wait()
    conv_copy.wait()


def last_kernel(scale, grad_in, streams_in, mixed_in, filt_in, prod_in, conv_in, weight_ref, *refs):
    const_in, out_hbm = refs[:5], refs[5]
    query_ref, in_ref, mixed_ref, filt_ref, prod_ref, conv_ref = refs[6:12]
    grad_ref, src, res, sums, peak, halo, lines, out_ref, tail_ref = refs[12:21]
    consts, const_sems, grad_sems, sems, spec_sems, out_sems = refs[21:26], *refs[26:31]
    first_ref, last_ref, forward_ref, backward_ref, twiddle_ref = consts
    blocks, width = in_ref.shape[0], in_ref.shape[2]
    chans = weight_ref.shape[1]
    lane = lax.broadcasted_iota(jnp.int32, (chans, width), 1)
    copies = [
        pltpu.make_async_copy(a, b, sems.at[i])
        for i, (a, b) in enumerate(
            (
                (mixed_in, mixed_ref),
                (conv_in, conv_ref),
                (streams_in, in_ref),
            )
        )
    ]

    def fetch_grad(step):
        some = pl.ds(step * UNROLL, UNROLL)
        return pltpu.make_async_copy(grad_in.at[some], query_ref.at[some], grad_sems.at[step])

    def fetch(step):
        at = row_of(step, GROUP * blocks)
        return [
            pltpu.make_async_copy(a.at[at], b.at[at], spec_sems.at[i, step])
            for i, (a, b) in enumerate(((filt_in, filt_ref), (prod_in, prod_ref)))
        ]

    for step in range(blocks // UNROLL):
        fetch_grad(step).start()
    const_copies = load_consts(const_in, consts, const_sems)
    for copy in fetch(0):
        copy.start()

    def prepare(step, carry):
        fetch_grad(step).wait()
        for u in range(UNROLL):
            n1 = step * UNROLL + u
            at = row_of(n1, chans)
            grad = coded(query_ref, n1, 1, chans)
            grad_ref[at, :] = grad
            src[at, :] = grad * mix(weight_ref, 0, lagged(query_ref, n1, 0, chans, width))
        return carry

    lax.fori_loop(0, blocks // UNROLL, prepare, 0)
    peak[...] = jnp.zeros_like(peak)
    halo[...] = jnp.zeros_like(halo)
    column = lax.broadcasted_iota(jnp.int32, (blocks, width), 1)
    for copy in const_copies:
        copy.wait()
    cos, sin = twiddle_ref[0], twiddle_ref[1]
    steps = chans // GROUP

    def convolve(step, carry):
        base = step * GROUP
        part = GROUP * blocks

        def dy(g):
            return src[pl.ds(base + g, blocks, stride=chans), :]

        @pl.when(step + 1 < steps)
        def _():
            for copy in fetch(step + 1):
                copy.start()

        @pl.when(step + 1 == steps)
        def _():
            for copy in copies:
                copy.start()

        rows = forward_rows(dy, first_ref, cos, sin, blocks, width)
        spec = step_two(jnp.concatenate(rows, axis=0), forward_ref)
        at = row_of(step, part)
        for copy in fetch(step):
            copy.wait()
        both = [conj_times(r[at, :], spec, width) for r in (filt_ref, prod_ref)]
        back = step_two(jnp.concatenate(both, axis=0), backward_ref)
        for s in range(2):

            def put(g, out):
                res[s, pl.ds(base + g, blocks, stride=chans), :] = out
                peak[s] = jnp.maximum(peak[s], jnp.abs(out))
                if s == 0:
                    for p in range(2):
                        halo[p] = jnp.where(column == base + g, out[:, p : p + 1], halo[p])

            inverse_one(
                back[s * part : (s + 1) * part], put, last_ref, cos, sin, blocks, width
            )
        return carry

    lax.fori_loop(0, steps, convolve, 0)
    for copy in copies:
        copy.wait()

    def query_grad(n1):
        at = row_of(n1, chans)
        return grad_ref[at, :] * conv_ref[at, :]

    sums[...] = jnp.zeros_like(sums)

    def most(i):
        peak_i = jnp.max(jnp.max(peak[i], axis=0, keepdims=True), axis=1, keepdims=True)
        peak_i = jnp.maximum(peak_i * (scale if i else 1.0) * (1.0 + 2.0**-7), 2.0**-100)
        peak_i = peak_i.astype(jnp.bfloat16).astype(jnp.float32)
        return jnp.broadcast_to(peak_i, (chans, width))

    bounds = [most(0), most(1)]
    inverses = [1.0 / bound for bound in bounds]

    def finish(step, cur):
        adds = [None] * 9
        for u in range(UNROLL):
            n1 = step * UNROLL + u
            at = row_of(n1, chans)
            follow = query_grad(jnp.minimum(n1 + 1, blocks - 1))
            if u == UNROLL - 1:
                follow = jnp.where(n1 + 1 < blocks, follow, 0.0)
            weights = [weight_ref[j] for j in range(3)]
            out = ahead(weights, cur, follow, chans, width)
            dz = res[0, at, :]
            out_ref[n1, pl.ds(0, chans), :] = out.astype(jnp.bfloat16)
            out_ref[n1, pl.ds(chans, chans), :] = encode(dz, inverses[0])
            out_ref[n1, pl.ds(2 * chans, chans), :] = encode(res[1, at, :] * scale, inverses[1])
            full = [cur, dz * mixed_ref[1, at, :], dz * mixed_ref[0, at, :]]
            for b in range(3):
                ref, place = (in_ref, b - 1) if b else (query_ref, 0)
                parts = lagged(ref, n1, place, chans, width)
                for j in range(3):
                    term = full[b] * parts[j]
                    old = adds[3 * b + j]
                    adds[3 * b + j] = term if old is None else old + term
            cur = follow
        for t in range(9):
            sums[t] += adds[t]
        some = pl.ds(step * UNROLL, UNROLL)
        pltpu.make_async_copy(
            out_ref.at[some], out_hbm.at[some, pl.ds(0, 3 * chans)], out_sems.at[0]
        ).start()
        return cur

    lax.fori_loop(0, blocks // UNROLL, finish, query_grad(0))

    total = jnp.zeros((chans, width), jnp.float32)
    for t in range(9):
        column = jnp.sum(sums[t], axis=1, keepdims=True) * scale
        total = total + jnp.where(lane == t, column, 0.0)
    pad = [jnp.zeros_like(total)] * (width // chans - 1)
    total = jnp.concatenate([total] + pad, axis=0).T
    high, low = [p.astype(jnp.float32) for p in split(total)]
    row = lax.broadcasted_iota(jnp.int32, (8, width), 0)
    group = lax.broadcasted_iota(jnp.int32, (8, width), 1) // chans
    fixed = high[:8] + pltpu.roll(low[:8], chans, 1)
    extra = jnp.where(row == 0, high[8:9], 0.0) + jnp.where(row == 1, low[8:9], 0.0)
    extra = jnp.where(row == 6, bounds[1][:1], extra)
    extra = jnp.where(row == 7, bounds[0][:1], extra)
    extra = pltpu.roll(jnp.where(group == 0, extra, 0.0), 2 * chans, 1)
    fixed = fixed + extra
    for p in range(2):
        high, low = [x.astype(jnp.float32) for x in split(halo[p])]
        lines[p, pl.ds(0, blocks), :] = pltpu.roll(high, 2 * chans, 1)
        lines[2 + p, pl.ds(0, blocks), :] = pltpu.roll(low, 2 * chans, 1)
        lines[p, pl.ds(blocks, 8), :] = jnp.zeros((8, width), jnp.float32)
        lines[2 + p, pl.ds(blocks, 8), :] = jnp.zeros((8, width), jnp.float32)

    def attach(n1, carry):
        tile = fixed
        for i in range(4):
            tile = tile + jnp.where(row == 2 + i, lines[i, pl.ds(n1 + 1, 1), :], 0.0)
        near = [
            in_ref[i, pl.ds(3 * chans, 8), :].astype(jnp.float32)
            for i in (jnp.maximum(n1 - 1, 0), jnp.minimum(n1 + 1, blocks - 1))
        ]
        keep = ((row < 4) & (n1 > 0)) | ((row >= 4) & (n1 + 1 < blocks))
        edge = jnp.where(row < 4, near[0], near[1])
        tile = jnp.where(group == 3, jnp.where(keep, edge, 0.0), tile)
        tail_ref[n1] = tile.astype(jnp.bfloat16)
        return carry

    lax.fori_loop(0, blocks, attach, 0)
    tail = pltpu.make_async_copy(
        tail_ref, out_hbm.at[:, pl.ds(3 * chans, 8)], out_sems.at[1]
    )
    tail.start()
    tail.wait()
    pltpu.make_async_copy(
        out_ref, out_hbm.at[:, pl.ds(0, 3 * chans)], out_sems.at[0]
    ).wait()


def f32(*shape):
    return jax.ShapeDtypeStruct(shape, jnp.float32)


def bf16(*shape):
    return jax.ShapeDtypeStruct(shape, jnp.bfloat16)


def estimate(us):
    return pl.CostEstimate(flops=int(us * 1e8), bytes_accessed=int(us * 3e6), transcendentals=0)


def params(mib):
    return pltpu.CompilerParams(vmem_limit_bytes=mib << 20)


def hbm():
    return pl.BlockSpec(memory_space=pltpu.HBM)


def vmem():
    return pl.BlockSpec(memory_space=pltpu.VMEM)


def hbm():
    return pl.BlockSpec(memory_space=pltpu.HBM)


def vmem():
    return pl.BlockSpec(memory_space=pltpu.VMEM)


def room(*arrays):
    return [pltpu.VMEM(a.shape, a.dtype) for a in arrays]


def stage_one(streams, weight, consts, scale):
    blocks, width = streams.shape[0], streams.shape[2]
    chans = weight.shape[1]
    rows = blocks * chans
    shapes = [f32(2, rows, width), f32(rows, 2 * width), f32(rows, 2 * width), f32(rows, width)]
    return pl.pallas_call(
        lambda *refs: first_kernel(scale, *refs),
        name="stage_one",
        out_shape=tuple(shapes),
        in_specs=[hbm(), vmem()] + [hbm()] * 5,
        out_specs=(hbm(),) * 4,
        scratch_shapes=room(streams, f32(2, rows, width), *shapes, *consts)
        + [
            pltpu.SemaphoreType.DMA((5,)),
            pltpu.SemaphoreType.DMA((blocks // UNROLL,)),
            pltpu.SemaphoreType.DMA((4,)),
        ],
        cost_estimate=estimate(14),
        compiler_params=params(ONE_MIB),
    )(streams, weight, *consts)


def stage_two(grad, streams, mixed, filt, prod, conv, weight, consts, scale):
    blocks, width = streams.shape[0], streams.shape[2]
    chans = weight.shape[1]
    rows = blocks * chans
    return pl.pallas_call(
        lambda *refs: last_kernel(scale, *refs),
        name="stage_two",
        out_shape=bf16(blocks, 3 * chans + 8, width),
        in_specs=[hbm()] * 6 + [vmem()] + [hbm()] * 5,
        out_specs=hbm(),
        scratch_shapes=room(
            grad,
            streams,
            mixed,
            filt,
            prod,
            conv,
            f32(rows, width),
            f32(rows, width),
            f32(2, rows, width),
            f32(9, chans, width),
            f32(2, blocks, width),
            f32(2, blocks, width),
            f32(4, blocks + 8, width),
            bf16(blocks, 3 * chans, width),
            bf16(blocks, 8, width),
            *consts,
        )
        + [
            pltpu.SemaphoreType.DMA((5,)),
            pltpu.SemaphoreType.DMA((blocks // UNROLL,)),
            pltpu.SemaphoreType.DMA((3,)),
            pltpu.SemaphoreType.DMA((2, chans // GROUP)),
            pltpu.SemaphoreType.DMA((2,)),
        ],
        cost_estimate=estimate(14),
        compiler_params=params(TWO_MIB),
    )(grad, streams, mixed, filt, prod, conv, weight, *consts)


def spread_kernel(back_ref, in_hbm, weight_ref, ig_hbm, tg_hbm, sg_ref, in_ref, ig_ref, tg_ref, sems):
    count, _, width = back_ref.shape
    total = tg_ref.shape[1]
    chans = total // count
    some = width // chans
    wide = total // CHUNKS
    row = lax.broadcasted_iota(jnp.int32, (8, width), 0)
    group = lax.broadcasted_iota(jnp.int32, (8, width), 1) // chans

    def fetch(part):
        cols = pl.ds(part * wide, wide)
        return pltpu.make_async_copy(
            in_hbm.at[pl.ds(1, 2), :, cols], in_ref.at[..., cols], sems.at[2, part]
        )

    def copies(part):
        cols = pl.ds(part * wide, wide)
        return [
            pltpu.make_async_copy(a.at[..., cols], b.at[..., cols], sems.at[i, part])
            for i, (a, b) in enumerate(((ig_ref, ig_hbm), (tg_ref, tg_hbm)))
        ]

    for part in range(CHUNKS):
        fetch(part).start()
    for part in range(CHUNKS):
        fetch(part).wait()
        for m in range(part * wide // width, (part + 1) * wide // width):
            cols = pl.ds(m * width, width)
            owners = range(m * some, (m + 1) * some)
            parts = []
            for i in range(3):
                rows = [back_ref[d, pl.ds(i * chans, chans), :] for d in owners]
                parts.append(jnp.concatenate(rows, axis=0).astype(jnp.float32).T)
            ig_ref[0, :, cols] = parts[0].astype(jnp.bfloat16)
            sums = jnp.zeros((8, width), jnp.float32)
            extra = jnp.zeros((8, width), jnp.float32)
            edge = jnp.zeros((8, width), jnp.float32)
            for a, d in enumerate(owners):
                tile = back_ref[d, pl.ds(3 * chans, 8), :].astype(jnp.float32)
                turned = [pltpu.roll(tile, (a - i) % some * chans, 1) if a != i else tile for i in range(4)]
                sums = jnp.where(group == a, turned[0] + turned[1], sums)
                extra = jnp.where(group == a, turned[2], extra)
                edge = jnp.where(group == a, turned[3], edge)
            for t in range(9):
                line = sums[t : t + 1] if t < 8 else extra[:1] + extra[1:2]
                sg_ref[t // 3, pl.ds(t % 3, 1), cols] = line
            tg_ref[:, cols] = decode(parts[2], extra[6:7])
            dz = decode(parts[1], extra[7:8])
            after = pltpu.roll(extra, 6, 0) + pltpu.roll(extra, 4, 0)
            dz = jnp.concatenate([dz, jnp.where(row < 2, after, 0.0)], axis=0)
            weights = [[weight_ref[b, pl.ds(j, 1), cols] for j in range(3)] for b in range(3)]
            for b in (1, 2):
                other = 3 - b
                x = jnp.concatenate(
                    [
                        pltpu.roll(edge, 8 - 2 * other, 0),
                        in_ref[other - 1, :, cols].astype(jnp.float32),
                        pltpu.roll(edge, 6 - 2 * other, 0),
                    ],
                    axis=0,
                )
                mixed = weights[other][0] * x
                for j in (1, 2):
                    mixed = mixed + weights[other][j] * pltpu.roll(x, j, 0)
                dm = dz * mixed[8:]
                out = weights[b][0] * dm
                for j in (1, 2):
                    out = out + weights[b][j] * pltpu.roll(dm, dm.shape[0] - j, 0)
                ig_ref[b, :, cols] = out[:width].astype(jnp.bfloat16)
        for copy in copies(part):
            copy.start()
    for part in range(CHUNKS):
        for copy in copies(part):
            copy.wait()


def spread(back, inputs, weight):
    rows, total = inputs.shape[1:]
    outs = (bf16(3, rows, total), f32(rows, total))
    return pl.pallas_call(
        spread_kernel,
        name="spread",
        out_shape=outs + (f32(*weight.shape),),
        in_specs=[vmem(), hbm(), vmem()],
        out_specs=(hbm(), hbm(), vmem()),
        scratch_shapes=room(bf16(2, rows, total), *outs) + [pltpu.SemaphoreType.DMA((3, CHUNKS))],
        cost_estimate=estimate(5),
        compiler_params=params(24),
    )(back, inputs, weight)


def collect_kernel(in_hbm, taps_hbm, out_hbm, query_hbm, in_ref, taps_ref, out_ref, query_ref, sems):
    total = taps_ref.shape[1]
    count, chans, width = query_ref.shape
    some = width // chans
    wide = total // CHUNKS
    owners = count // CHUNKS
    taps_copy = pltpu.make_async_copy(taps_hbm, taps_ref, sems.at[3, 0])
    taps_copy.start()

    def fetch(part):
        cols = pl.ds(part * wide, wide)
        return pltpu.make_async_copy(in_hbm.at[..., cols], in_ref.at[..., cols], sems.at[0, part])

    def puts(part):
        these = pl.ds(part * owners, owners)
        return [
            pltpu.make_async_copy(a.at[these], b.at[these], sems.at[1 + i, part])
            for i, (a, b) in enumerate(((out_ref, out_hbm), (query_ref, query_hbm)))
        ]

    for part in range(CHUNKS):
        fetch(part).start()
    taps_copy.wait()
    most = jnp.max(jnp.abs(taps_ref[...]), axis=0, keepdims=True)
    most = jnp.max(most, axis=1, keepdims=True)
    most = jnp.maximum(most * (1.0 + 2.0**-7), 2.0**-100).astype(jnp.bfloat16)
    mark = jnp.broadcast_to(most.astype(jnp.float32), (8, width))
    row = lax.broadcasted_iota(jnp.int32, (8, width), 0)
    group = lax.broadcasted_iota(jnp.int32, (8, width), 1) // chans
    inverse = jnp.broadcast_to(1.0 / most.astype(jnp.float32), (width, width))
    for part in range(CHUNKS):
        fetch(part).wait()
        for m in range(part * wide // width, (part + 1) * wide // width):
            cols = pl.ds(m * width, width)
            blocks = [in_ref[b, :, cols].astype(jnp.float32).T.astype(jnp.bfloat16) for b in range(3)]
            blocks.append(encode(taps_ref[:, cols].T, inverse))
            edge = jnp.zeros((8, width), jnp.float32)
            for i, (at, stream, down) in enumerate(
                ((width - 16, 1, 2), (width - 16, 2, 4), (0, 1, 4), (0, 2, 6))
            ):
                end = in_ref[stream, pl.ds(at, 16), cols].astype(jnp.float32)
                end = pltpu.roll(end[8:] if at else end[:8], down, 0)
                edge = jnp.where(row // 2 == i, end, edge)
            for h in range(some):
                d = m * some + h
                at = slice(h * chans, (h + 1) * chans)
                query_ref[d] = blocks[0][at]
                for b in range(3):
                    out_ref[d, pl.ds(b * chans, chans), :] = blocks[b + 1][at]
                turned = pltpu.roll(edge, (some - 1 - h) * chans, 1) if h < some - 1 else edge
                tile = jnp.where(group == some - 1, turned, mark)
                out_ref[d, pl.ds(3 * chans, 8), :] = tile.astype(jnp.bfloat16)
        for copy in puts(part):
            copy.start()
    for part in range(CHUNKS):
        for copy in puts(part):
            copy.wait()


def collect(inputs, taps, count):
    rows, total = taps.shape
    chans = total // count
    outs = (bf16(count, 3 * chans + 8, rows), bf16(count, chans, rows))
    return pl.pallas_call(
        collect_kernel,
        name="collect",
        out_shape=outs,
        in_specs=[hbm(), hbm()],
        out_specs=(hbm(), hbm()),
        scratch_shapes=room(inputs, taps, *outs) + [pltpu.SemaphoreType.DMA((4, CHUNKS))],
        cost_estimate=estimate(5),
        compiler_params=params(60),
    )(inputs, taps)


def project_kernel(which_ref, own_w, other_w, own_ref, other_ref, query_ref, out_ref, grad, peak):
    step = pl.program_id(0)
    rows, width = own_w.shape[0], own_ref.shape[0]
    count, chans, _ = query_ref.shape

    def part(a, b):
        return lax.dot_general(
            a[...], b[...], (((1,), (1,)), ((), ())), preferred_element_type=jnp.float32
        )

    block = part(own_w, own_ref) + part(other_w, other_ref)
    grad[pl.ds(pl.multiple_of(step * rows, rows), rows), :] = block
    most = jnp.max(jnp.abs(block), axis=0, keepdims=True)

    @pl.when(step == 0)
    def _():
        peak[...] = jnp.broadcast_to(most, peak.shape)

    @pl.when(step > 0)
    def _():
        peak[...] = jnp.maximum(peak[...], most)

    @pl.when(step == pl.num_programs(0) - 1)
    def _():
        most = jnp.max(peak[...], axis=1, keepdims=True)
        most = jnp.maximum(most * (1.0 + 2.0**-7), 2.0**-100).astype(jnp.bfloat16)
        mark = jnp.broadcast_to(most, (8, width))
        inverse = jnp.broadcast_to(1.0 / most[:1].astype(jnp.float32), (chans, width))

        def fill(i, carry):
            for u in range(UNROLL):
                d = i * UNROLL + u
                out_ref[d, pl.ds(0, chans), :] = query_ref[d]
                out_ref[d, pl.ds(chans, chans), :] = encode(grad[row_of(d, chans), :], inverse)
                out_ref[d, pl.ds(2 * chans, 8), :] = mark
            return carry

        lax.fori_loop(0, count // UNROLL, fill, 0)


def project(which, w_out, own, other, query):
    count, chans, rows = query.shape
    depth = own.shape[1]
    tile = 256
    whole = lambda shape: pl.BlockSpec(shape, lambda i, which: (0,) * len(shape))
    return pl.pallas_call(
        project_kernel,
        name="project",
        grid_spec=pltpu.PrefetchScalarGridSpec(
            num_scalar_prefetch=1,
            grid=(w_out.shape[0] // tile,),
            in_specs=[
                pl.BlockSpec((tile, depth), lambda i, which: (i, which[0])),
                pl.BlockSpec((tile, depth), lambda i, which: (i, 1 - which[0])),
                whole(own.shape),
                whole(other.shape),
                whole(query.shape),
            ],
            out_specs=whole((count, 2 * chans + 8, rows)),
            scratch_shapes=[
                pltpu.VMEM((count * chans, rows), jnp.float32),
                pltpu.VMEM((8, rows), jnp.float32),
            ],
        ),
        out_shape=bf16(count, 2 * chans + 8, rows),
        cost_estimate=estimate(PROJECT_US),
        compiler_params=params(40),
    )(which, w_out, w_out, own, other, query)


def regroup(x):
    return lax.all_to_all(x, "ctx", split_axis=0, concat_axis=0, tiled=True)


def shards(inputs, short_weight, taps, w_out, grad_out):
    rows, local = inputs.shape[1], inputs.shape[2]
    count = lax.axis_size("ctx")
    where = lax.axis_index("ctx")
    chans = local // count
    scale = 1.0 / math.sqrt(count * rows)

    streams, query = collect(inputs, taps, count)
    other = lax.ppermute(grad_out, "tp", [(0, 1), (1, 0)])
    streams = regroup(streams)
    which = lax.axis_index("tp").astype(jnp.int32).reshape(1)
    gated = project(which, w_out, grad_out, other, query)
    gated = regroup(gated)

    weight = lax.dynamic_slice_in_dim(short_weight, where * chans, chans, axis=2)
    weight = jnp.broadcast_to(weight.reshape(9, chans, 1), (9, chans, rows))

    consts = [jnp.asarray(t) for t in tables(count, rows)]
    mixed, filt, prod, conv = stage_one(streams, weight, consts, scale)
    back = stage_two(gated, streams, mixed, filt, prod, conv, weight, consts, scale)

    back = regroup(back)
    return spread(back, inputs, short_weight)


def solution(mesh):
    return jax.shard_map(
        shards,
        mesh=mesh,
        in_specs=(
            P(None, "ctx", "tp"),
            P(None, None, "tp"),
            P("ctx", "tp"),
            P("tp", None),
            P("ctx", "tp"),
        ),
        out_specs=(P(None, "ctx", "tp"), P("ctx", "tp"), P(None, None, "tp")),
        check_vma=False,
    )
```

```python
import math

import jax
import jax.numpy as jnp
import numpy as np
from jax import lax
from jax.experimental import pallas as pl
from jax.experimental.pallas import tpu as pltpu
from jax.sharding import PartitionSpec as P

GROUP = 16
UNROLL = 8
STEPS = 240
CHUNKS = 4
ONE_MIB = 60
TWO_MIB = 62
PROJECT_US = 200


def split_np(x):
    high = x.astype(jnp.bfloat16)
    low = (x - high.astype(np.float64)).astype(jnp.bfloat16)
    return high, low


def tables(blocks, width):
    length = 2 * blocks * width
    n1 = np.arange(blocks)
    n2 = np.arange(width)
    angle = 2.0 * np.pi * np.outer(n1 + 0.5, n1) / (2 * blocks)
    first = np.concatenate([np.cos(angle), -np.sin(angle)], axis=0)
    high, low = split_np(first)
    first3 = np.concatenate([high, high, low], axis=1)
    last = first.T * (2.0 / length)
    high, low = split_np(last)
    last4 = np.concatenate(
        [
            np.concatenate([high, high], axis=1),
            np.concatenate([low, np.zeros_like(low)], axis=1),
        ],
        axis=0,
    )
    angle = 2.0 * np.pi * (np.outer(n2, n2) % width) / width
    cos, sin = np.cos(angle), np.sin(angle)
    forward = np.block([[cos, -sin], [sin, cos]])
    high, low = split_np(forward)
    forward2 = np.stack([high, low])
    backward = np.block([[cos, sin], [-sin, cos]])
    high, low = split_np(backward)
    backward2 = np.stack([high, low])
    angle = 2.0 * np.pi * np.outer(n1 + 0.5, n2) / length
    twiddle = np.stack([np.cos(angle), np.sin(angle)]).astype(np.float32)
    return first3, last4, forward2, backward2, twiddle


def split(x):
    high = x.astype(jnp.bfloat16)
    low = (x - high.astype(jnp.float32)).astype(jnp.bfloat16)
    return high, low


def encode(x, inverse):
    root = jnp.minimum(jnp.sqrt(jnp.abs(x) * inverse), 1.0)
    n = jnp.floor(root * (STEPS * 128.0) + 0.5)
    high = jnp.floor(n * (1.0 / 128.0))
    code = jnp.exp2(high - STEPS / 2) * (1.0 + (n - 128.0 * high) * (1.0 / 128.0))
    return jnp.where(x < 0, -code, code).astype(jnp.bfloat16)


def decode(code, bound):
    code = code.astype(jnp.float32)
    size = jnp.abs(code)
    high = jnp.floor(jnp.log2(size))
    root = (high + size * jnp.exp2(-high) + (STEPS / 2 - 1.0)) * (1.0 / STEPS)
    size = root * root * bound
    return jnp.where(code < 0, -size, size)


def mm(a, b):
    return jnp.dot(a, b, preferred_element_type=jnp.float32)


def forward_rows(x_of, first_ref, cos, sin, blocks, width):
    rows = []
    for g in range(0, GROUP, 2):
        cols = []
        for h in (0, 1):
            high, low = split(x_of(g + h))
            cols.append(jnp.concatenate([high, low, high], axis=0))
        out = mm(first_ref[...], jnp.concatenate(cols, axis=1))
        for h in (0, 1):
            re = out[:blocks, h * width : (h + 1) * width]
            im = out[blocks:, h * width : (h + 1) * width]
            rows.append(jnp.concatenate([re * cos + im * sin, im * cos - re * sin], axis=1))
    return rows


def step_two(rows, table_ref):
    high, low = split(rows)
    return mm(high, table_ref[0]) + mm(low, table_ref[0]) + mm(high, table_ref[1])


def inverse_one(back, put, last_ref, cos, sin, blocks, width):
    for g in range(0, GROUP, 2):
        cols = []
        for h in (0, 1):
            at = (g + h) * blocks
            re = back[at : at + blocks, :width]
            im = back[at : at + blocks, width:]
            both = jnp.concatenate([re * cos - im * sin, re * sin + im * cos], axis=0)
            high, low = split(both)
            cols.append(jnp.concatenate([high, low], axis=0))
        out = mm(last_ref[...], jnp.concatenate(cols, axis=1))
        out = out[:blocks] + out[blocks:]
        for h in (0, 1):
            put(g + h, out[:, h * width : (h + 1) * width])


def times(a, b, width):
    ar, ai, br, bi = a[:, :width], a[:, width:], b[:, :width], b[:, width:]
    return jnp.concatenate([ar * br - ai * bi, ar * bi + ai * br], axis=1)


def conj_times(a, b, width):
    ar, ai, br, bi = a[:, :width], a[:, width:], b[:, :width], b[:, width:]
    return jnp.concatenate([ar * br + ai * bi, ar * bi - ai * br], axis=1)


def row_of(n1, chans):
    return pl.ds(pl.multiple_of(n1 * chans, chans), chans)


def lagged(in_ref, n1, b, chans, width):
    lane = lax.broadcasted_iota(jnp.int32, (chans, width), 1)
    at = pl.ds(b * chans, chans)
    cur = in_ref[n1, at, :].astype(jnp.float32)
    before = in_ref[jnp.maximum(n1 - 1, 0), at, :].astype(jnp.float32)
    before = jnp.where(n1 > 0, before, 0.0)
    return [cur] + [
        pltpu.roll(jnp.where(lane >= width - j, before, cur), j, 1) for j in (1, 2)
    ]


def mix(weight_ref, b, parts):
    return (
        weight_ref[3 * b] * parts[0]
        + weight_ref[3 * b + 1] * parts[1]
        + weight_ref[3 * b + 2] * parts[2]
    )


def coded(in_ref, n1, b, chans):
    bound = in_ref[n1, pl.ds((b + 1) * chans, 8), :].astype(jnp.float32)
    bound = jnp.broadcast_to(bound[:, :1], bound.shape)
    bound = jnp.concatenate([bound] * (chans // 8), axis=0)
    return decode(in_ref[n1, pl.ds(b * chans, chans), :], bound)


def ahead(weights, cur, follow, chans, width):
    lane = lax.broadcasted_iota(jnp.int32, (chans, width), 1)
    out = weights[0] * cur
    for j in (1, 2):
        moved = pltpu.roll(jnp.where(lane < j, follow, cur), width - j, 1)
        out = out + weights[j] * moved
    return out


def load_consts(sources, targets, sems):
    copies = [pltpu.make_async_copy(a, b, sems.at[i]) for i, (a, b) in enumerate(zip(sources, targets))]
    for copy in copies:
        copy.start()
    return copies


def first_kernel(scale, in_hbm, weight_ref, *refs):
    const_in, (mixed_out, filt_out, prod_out, conv_out, lag_out) = refs[:5], refs[5:10]
    in_ref, src, mixed_ref, filt_ref, prod_ref, conv_ref, lag_ref = refs[10:17]
    consts, const_sems, in_sems, out_sems = refs[17:22], refs[22], refs[23], refs[24]
    first_ref, last_ref, forward_ref, backward_ref, twiddle_ref = consts
    blocks, width = in_ref.shape[0], in_ref.shape[2]
    chans = weight_ref.shape[1]

    def fetch(step):
        some = pl.ds(step * UNROLL, UNROLL)
        return pltpu.make_async_copy(in_hbm.at[some], in_ref.at[some], in_sems.at[step])

    for step in range(blocks // UNROLL):
        fetch(step).start()
    const_copies = load_consts(const_in, consts, const_sems)

    def prepare(step, carry):
        fetch(step).wait()
        for u in range(UNROLL):
            n1 = step * UNROLL + u
            at = row_of(n1, chans)
            mixed = []
            for b in range(2):
                parts = lagged(in_ref, n1, b, chans, width)
                for j in (1, 2):
                    at_lag = pl.ds((2 * b + j - 1) * chans, chans)
                    lag_ref[n1, at_lag, :] = parts[j].astype(jnp.bfloat16)
                mixed.append(mix(weight_ref, b + 1, parts))
                mixed_ref[b, at, :] = mixed[b]
            src[0, at, :] = coded(in_ref, n1, 2, chans) * scale
            src[1, at, :] = mixed[0] * mixed[1]
        return carry

    lax.fori_loop(0, blocks // UNROLL, prepare, 0)
    mixed_copy = pltpu.make_async_copy(mixed_ref, mixed_out, out_sems.at[0])
    mixed_copy.start()
    lag_copy = pltpu.make_async_copy(lag_ref, lag_out, out_sems.at[4])
    lag_copy.start()
    for copy in const_copies:
        copy.wait()
    cos, sin = twiddle_ref[0], twiddle_ref[1]

    def convolve(step, carry):
        base = step * GROUP
        part = GROUP * blocks
        rows = []
        for s in range(2):
            rows += forward_rows(
                lambda g: src[s, pl.ds(base + g, blocks, stride=chans), :],
                first_ref,
                cos,
                sin,
                blocks,
                width,
            )
        spec = step_two(jnp.concatenate(rows, axis=0), forward_ref)
        at = row_of(step, part)
        filt_ref[at, :] = spec[:part]
        prod_ref[at, :] = spec[part:]
        pltpu.make_async_copy(filt_ref.at[at], filt_out.at[at], out_sems.at[1]).start()
        pltpu.make_async_copy(prod_ref.at[at], prod_out.at[at], out_sems.at[2]).start()
        back = step_two(times(spec[:part], spec[part:], width), backward_ref)

        def put(g, out):
            conv_ref[pl.ds(base + g, blocks, stride=chans), :] = out

        inverse_one(back, put, last_ref, cos, sin, blocks, width)
        return carry

    lax.fori_loop(0, chans // GROUP, convolve, 0)
    conv_copy = pltpu.make_async_copy(conv_ref, conv_out, out_sems.at[3])
    conv_copy.start()
    mixed_copy.wait()
    lag_copy.wait()
    pltpu.make_async_copy(filt_ref, filt_out, out_sems.at[1]).wait()
    pltpu.make_async_copy(prod_ref, prod_out, out_sems.at[2]).wait()
    conv_copy.wait()


def last_kernel(scale, grad_in, streams_in, mixed_in, filt_in, prod_in, conv_in, lag_in, weight_ref, *refs):
    const_in, out_hbm = refs[:5], refs[5]
    query_ref, in_ref, mixed_ref, filt_ref, prod_ref, conv_ref = refs[6:12]
    grad_ref, src, res, sums, peak, halo, lines, lag_ref, out_ref, tail_ref = refs[12:22]
    consts, const_sems, grad_sems, sems, spec_sems, out_sems = refs[22:27], *refs[27:32]
    first_ref, last_ref, forward_ref, backward_ref, twiddle_ref = consts
    blocks, width = in_ref.shape[0], in_ref.shape[2]
    chans = weight_ref.shape[1]
    lane = lax.broadcasted_iota(jnp.int32, (chans, width), 1)
    copies = [
        pltpu.make_async_copy(a, b, sems.at[i])
        for i, (a, b) in enumerate(
            (
                (mixed_in, mixed_ref),
                (conv_in, conv_ref),
                (streams_in, in_ref),
                (lag_in, lag_ref),
            )
        )
    ]

    def fetch_grad(step):
        some = pl.ds(step * UNROLL, UNROLL)
        return pltpu.make_async_copy(grad_in.at[some], query_ref.at[some], grad_sems.at[step])

    def fetch(step):
        at = row_of(step, GROUP * blocks)
        return [
            pltpu.make_async_copy(a.at[at], b.at[at], spec_sems.at[i, step])
            for i, (a, b) in enumerate(((filt_in, filt_ref), (prod_in, prod_ref)))
        ]

    for step in range(blocks // UNROLL):
        fetch_grad(step).start()
    const_copies = load_consts(const_in, consts, const_sems)
    for copy in fetch(0):
        copy.start()

    def prepare(step, carry):
        fetch_grad(step).wait()
        for u in range(UNROLL):
            n1 = step * UNROLL + u
            at = row_of(n1, chans)
            grad = coded(query_ref, n1, 1, chans)
            grad_ref[at, :] = grad
            src[at, :] = grad * mix(weight_ref, 0, lagged(query_ref, n1, 0, chans, width))
        return carry

    lax.fori_loop(0, blocks // UNROLL, prepare, 0)
    peak[...] = jnp.zeros_like(peak)
    halo[...] = jnp.zeros_like(halo)
    column = lax.broadcasted_iota(jnp.int32, (blocks, width), 1)
    for copy in const_copies:
        copy.wait()
    cos, sin = twiddle_ref[0], twiddle_ref[1]
    steps = chans // GROUP

    def convolve(step, carry):
        base = step * GROUP
        part = GROUP * blocks

        def dy(g):
            return src[pl.ds(base + g, blocks, stride=chans), :]

        @pl.when(step + 1 < steps)
        def _():
            for copy in fetch(step + 1):
                copy.start()

        @pl.when(step == 0)
        def _():
            for copy in copies:
                copy.start()

        rows = forward_rows(dy, first_ref, cos, sin, blocks, width)
        spec = step_two(jnp.concatenate(rows, axis=0), forward_ref)
        at = row_of(step, part)
        for copy in fetch(step):
            copy.wait()
        both = [conj_times(r[at, :], spec, width) for r in (filt_ref, prod_ref)]
        back = step_two(jnp.concatenate(both, axis=0), backward_ref)
        for s in range(2):

            def put(g, out):
                res[s, pl.ds(base + g, blocks, stride=chans), :] = out
                peak[s] = jnp.maximum(peak[s], jnp.abs(out))
                if s == 0:
                    for p in range(2):
                        halo[p] = jnp.where(column == base + g, out[:, p : p + 1], halo[p])

            inverse_one(
                back[s * part : (s + 1) * part], put, last_ref, cos, sin, blocks, width
            )
        return carry

    lax.fori_loop(0, steps, convolve, 0)
    for copy in copies:
        copy.wait()

    def query_grad(n1):
        at = row_of(n1, chans)
        return grad_ref[at, :] * conv_ref[at, :]

    sums[...] = jnp.zeros_like(sums)

    def most(i):
        peak_i = jnp.max(jnp.max(peak[i], axis=0, keepdims=True), axis=1, keepdims=True)
        peak_i = jnp.maximum(peak_i * (scale if i else 1.0) * (1.0 + 2.0**-7), 2.0**-100)
        peak_i = peak_i.astype(jnp.bfloat16).astype(jnp.float32)
        return jnp.broadcast_to(peak_i, (chans, width))

    bounds = [most(0), most(1)]
    inverses = [1.0 / bound for bound in bounds]

    def finish(step, cur):
        adds = [None] * 9
        for u in range(UNROLL):
            n1 = step * UNROLL + u
            at = row_of(n1, chans)
            follow = query_grad(jnp.minimum(n1 + 1, blocks - 1))
            if u == UNROLL - 1:
                follow = jnp.where(n1 + 1 < blocks, follow, 0.0)
            weights = [weight_ref[j] for j in range(3)]
            out = ahead(weights, cur, follow, chans, width)
            dz = res[0, at, :]
            out_ref[n1, pl.ds(0, chans), :] = out.astype(jnp.bfloat16)
            out_ref[n1, pl.ds(chans, chans), :] = encode(dz, inverses[0])
            out_ref[n1, pl.ds(2 * chans, chans), :] = encode(res[1, at, :] * scale, inverses[1])
            full = [cur, dz * mixed_ref[1, at, :], dz * mixed_ref[0, at, :]]
            for b in range(3):
                if b:
                    parts = [in_ref[n1, pl.ds((b - 1) * chans, chans), :]]
                    for j in (0, 1):
                        parts.append(lag_ref[n1, pl.ds((2 * b - 2 + j) * chans, chans), :])
                    parts = [part.astype(jnp.float32) for part in parts]
                else:
                    parts = lagged(query_ref, n1, 0, chans, width)
                for j in range(3):
                    term = full[b] * parts[j]
                    old = adds[3 * b + j]
                    adds[3 * b + j] = term if old is None else old + term
            cur = follow
        for t in range(9):
            sums[t] += adds[t]
        some = pl.ds(step * UNROLL, UNROLL)
        pltpu.make_async_copy(
            out_ref.at[some], out_hbm.at[some, pl.ds(0, 3 * chans)], out_sems.at[0]
        ).start()
        return cur

    lax.fori_loop(0, blocks // UNROLL, finish, query_grad(0))

    total = jnp.zeros((chans, width), jnp.float32)
    for t in range(9):
        column = jnp.sum(sums[t], axis=1, keepdims=True) * scale
        total = total + jnp.where(lane == t, column, 0.0)
    pad = [jnp.zeros_like(total)] * (width // chans - 1)
    total = jnp.concatenate([total] + pad, axis=0).T
    high, low = [p.astype(jnp.float32) for p in split(total)]
    row = lax.broadcasted_iota(jnp.int32, (8, width), 0)
    group = lax.broadcasted_iota(jnp.int32, (8, width), 1) // chans
    fixed = high[:8] + pltpu.roll(low[:8], chans, 1)
    extra = jnp.where(row == 0, high[8:9], 0.0) + jnp.where(row == 1, low[8:9], 0.0)
    extra = jnp.where(row == 6, bounds[1][:1], extra)
    extra = jnp.where(row == 7, bounds[0][:1], extra)
    extra = pltpu.roll(jnp.where(group == 0, extra, 0.0), 2 * chans, 1)
    fixed = fixed + extra
    for p in range(2):
        high, low = [x.astype(jnp.float32) for x in split(halo[p])]
        lines[p, pl.ds(0, blocks), :] = pltpu.roll(high, 2 * chans, 1)
        lines[2 + p, pl.ds(0, blocks), :] = pltpu.roll(low, 2 * chans, 1)
        lines[p, pl.ds(blocks, 8), :] = jnp.zeros((8, width), jnp.float32)
        lines[2 + p, pl.ds(blocks, 8), :] = jnp.zeros((8, width), jnp.float32)

    def attach(n1, carry):
        tile = fixed
        for i in range(4):
            tile = tile + jnp.where(row == 2 + i, lines[i, pl.ds(n1 + 1, 1), :], 0.0)
        near = [
            in_ref[i, pl.ds(3 * chans, 8), :].astype(jnp.float32)
            for i in (jnp.maximum(n1 - 1, 0), jnp.minimum(n1 + 1, blocks - 1))
        ]
        keep = ((row < 4) & (n1 > 0)) | ((row >= 4) & (n1 + 1 < blocks))
        edge = jnp.where(row < 4, near[0], near[1])
        tile = jnp.where(group == 3, jnp.where(keep, edge, 0.0), tile)
        tail_ref[n1] = tile.astype(jnp.bfloat16)
        return carry

    lax.fori_loop(0, blocks, attach, 0)
    tail = pltpu.make_async_copy(
        tail_ref, out_hbm.at[:, pl.ds(3 * chans, 8)], out_sems.at[1]
    )
    tail.start()
    tail.wait()
    pltpu.make_async_copy(
        out_ref, out_hbm.at[:, pl.ds(0, 3 * chans)], out_sems.at[0]
    ).wait()


def f32(*shape):
    return jax.ShapeDtypeStruct(shape, jnp.float32)


def bf16(*shape):
    return jax.ShapeDtypeStruct(shape, jnp.bfloat16)


def estimate(us):
    return pl.CostEstimate(flops=int(us * 1e8), bytes_accessed=int(us * 3e6), transcendentals=0)


def params(mib):
    return pltpu.CompilerParams(vmem_limit_bytes=mib << 20)


def hbm():
    return pl.BlockSpec(memory_space=pltpu.HBM)


def vmem():
    return pl.BlockSpec(memory_space=pltpu.VMEM)


def hbm():
    return pl.BlockSpec(memory_space=pltpu.HBM)


def vmem():
    return pl.BlockSpec(memory_space=pltpu.VMEM)


def room(*arrays):
    return [pltpu.VMEM(a.shape, a.dtype) for a in arrays]


def stage_one(streams, weight, consts, scale):
    blocks, width = streams.shape[0], streams.shape[2]
    chans = weight.shape[1]
    rows = blocks * chans
    shapes = [f32(2, rows, width), f32(rows, 2 * width), f32(rows, 2 * width), f32(rows, width)]
    shapes.append(bf16(blocks, 4 * chans, width))
    return pl.pallas_call(
        lambda *refs: first_kernel(scale, *refs),
        name="stage_one",
        out_shape=tuple(shapes),
        in_specs=[hbm(), vmem()] + [hbm()] * 5,
        out_specs=(hbm(),) * 5,
        scratch_shapes=room(streams, f32(2, rows, width), *shapes, *consts)
        + [
            pltpu.SemaphoreType.DMA((5,)),
            pltpu.SemaphoreType.DMA((blocks // UNROLL,)),
            pltpu.SemaphoreType.DMA((5,)),
        ],
        cost_estimate=estimate(14),
        compiler_params=params(ONE_MIB),
    )(streams, weight, *consts)


def stage_two(grad, streams, mixed, filt, prod, conv, lag, weight, consts, scale):
    blocks, width = streams.shape[0], streams.shape[2]
    chans = weight.shape[1]
    rows = blocks * chans
    return pl.pallas_call(
        lambda *refs: last_kernel(scale, *refs),
        name="stage_two",
        out_shape=bf16(blocks, 3 * chans + 8, width),
        in_specs=[hbm()] * 7 + [vmem()] + [hbm()] * 5,
        out_specs=hbm(),
        scratch_shapes=room(
            grad,
            streams,
            mixed,
            filt,
            prod,
            conv,
            f32(rows, width),
            f32(rows, width),
            f32(2, rows, width),
            f32(9, chans, width),
            f32(2, blocks, width),
            f32(2, blocks, width),
            f32(4, blocks + 8, width),
            bf16(blocks, 4 * chans, width),
            bf16(blocks, 3 * chans, width),
            bf16(blocks, 8, width),
            *consts,
        )
        + [
            pltpu.SemaphoreType.DMA((5,)),
            pltpu.SemaphoreType.DMA((blocks // UNROLL,)),
            pltpu.SemaphoreType.DMA((4,)),
            pltpu.SemaphoreType.DMA((2, chans // GROUP)),
            pltpu.SemaphoreType.DMA((2,)),
        ],
        cost_estimate=estimate(14),
        compiler_params=params(TWO_MIB),
    )(grad, streams, mixed, filt, prod, conv, lag, weight, *consts)


def spread_kernel(back_ref, in_hbm, weight_ref, ig_hbm, tg_hbm, sg_ref, in_ref, ig_ref, tg_ref, sems):
    count, _, width = back_ref.shape
    total = tg_ref.shape[1]
    chans = total // count
    some = width // chans
    wide = total // CHUNKS
    row = lax.broadcasted_iota(jnp.int32, (8, width), 0)
    group = lax.broadcasted_iota(jnp.int32, (8, width), 1) // chans

    def fetch(part):
        cols = pl.ds(part * wide, wide)
        return pltpu.make_async_copy(
            in_hbm.at[pl.ds(1, 2), :, cols], in_ref.at[..., cols], sems.at[2, part]
        )

    def copies(part):
        cols = pl.ds(part * wide, wide)
        return [
            pltpu.make_async_copy(a.at[..., cols], b.at[..., cols], sems.at[i, part])
            for i, (a, b) in enumerate(((ig_ref, ig_hbm), (tg_ref, tg_hbm)))
        ]

    for part in range(CHUNKS):
        fetch(part).start()
    for part in range(CHUNKS):
        fetch(part).wait()
        for m in range(part * wide // width, (part + 1) * wide // width):
            cols = pl.ds(m * width, width)
            owners = range(m * some, (m + 1) * some)
            parts = []
            for i in range(3):
                rows = [back_ref[d, pl.ds(i * chans, chans), :] for d in owners]
                parts.append(jnp.concatenate(rows, axis=0).astype(jnp.float32).T)
            ig_ref[0, :, cols] = parts[0].astype(jnp.bfloat16)
            sums = jnp.zeros((8, width), jnp.float32)
            extra = jnp.zeros((8, width), jnp.float32)
            edge = jnp.zeros((8, width), jnp.float32)
            for a, d in enumerate(owners):
                tile = back_ref[d, pl.ds(3 * chans, 8), :].astype(jnp.float32)
                turned = [pltpu.roll(tile, (a - i) % some * chans, 1) if a != i else tile for i in range(4)]
                sums = jnp.where(group == a, turned[0] + turned[1], sums)
                extra = jnp.where(group == a, turned[2], extra)
                edge = jnp.where(group == a, turned[3], edge)
            for t in range(9):
                line = sums[t : t + 1] if t < 8 else extra[:1] + extra[1:2]
                sg_ref[t // 3, pl.ds(t % 3, 1), cols] = line
            tg_ref[:, cols] = decode(parts[2], extra[6:7])
            dz = decode(parts[1], extra[7:8])
            after = pltpu.roll(extra, 6, 0) + pltpu.roll(extra, 4, 0)
            dz = jnp.concatenate([dz, jnp.where(row < 2, after, 0.0)], axis=0)
            weights = [[weight_ref[b, pl.ds(j, 1), cols] for j in range(3)] for b in range(3)]
            for b in (1, 2):
                other = 3 - b
                x = jnp.concatenate(
                    [
                        pltpu.roll(edge, 8 - 2 * other, 0),
                        in_ref[other - 1, :, cols].astype(jnp.float32),
                        pltpu.roll(edge, 6 - 2 * other, 0),
                    ],
                    axis=0,
                )
                mixed = weights[other][0] * x
                for j in (1, 2):
                    mixed = mixed + weights[other][j] * pltpu.roll(x, j, 0)
                dm = dz * mixed[8:]
                out = weights[b][0] * dm
                for j in (1, 2):
                    out = out + weights[b][j] * pltpu.roll(dm, dm.shape[0] - j, 0)
                ig_ref[b, :, cols] = out[:width].astype(jnp.bfloat16)
        for copy in copies(part):
            copy.start()
    for part in range(CHUNKS):
        for copy in copies(part):
            copy.wait()


def spread(back, inputs, weight):
    rows, total = inputs.shape[1:]
    outs = (bf16(3, rows, total), f32(rows, total))
    return pl.pallas_call(
        spread_kernel,
        name="spread",
        out_shape=outs + (f32(*weight.shape),),
        in_specs=[vmem(), hbm(), vmem()],
        out_specs=(hbm(), hbm(), vmem()),
        scratch_shapes=room(bf16(2, rows, total), *outs) + [pltpu.SemaphoreType.DMA((3, CHUNKS))],
        cost_estimate=estimate(5),
        compiler_params=params(24),
    )(back, inputs, weight)


def collect_kernel(in_hbm, taps_hbm, out_hbm, query_hbm, in_ref, taps_ref, out_ref, query_ref, sems):
    total = taps_ref.shape[1]
    count, chans, width = query_ref.shape
    some = width // chans
    wide = total // CHUNKS
    owners = count // CHUNKS
    taps_copy = pltpu.make_async_copy(taps_hbm, taps_ref, sems.at[3, 0])
    taps_copy.start()

    def fetch(part):
        cols = pl.ds(part * wide, wide)
        return pltpu.make_async_copy(in_hbm.at[..., cols], in_ref.at[..., cols], sems.at[0, part])

    def puts(part):
        these = pl.ds(part * owners, owners)
        return [
            pltpu.make_async_copy(a.at[these], b.at[these], sems.at[1 + i, part])
            for i, (a, b) in enumerate(((out_ref, out_hbm), (query_ref, query_hbm)))
        ]

    for part in range(CHUNKS):
        fetch(part).start()
    taps_copy.wait()
    most = jnp.max(jnp.abs(taps_ref[...]), axis=0, keepdims=True)
    most = jnp.max(most, axis=1, keepdims=True)
    most = jnp.maximum(most * (1.0 + 2.0**-7), 2.0**-100).astype(jnp.bfloat16)
    mark = jnp.broadcast_to(most.astype(jnp.float32), (8, width))
    row = lax.broadcasted_iota(jnp.int32, (8, width), 0)
    group = lax.broadcasted_iota(jnp.int32, (8, width), 1) // chans
    inverse = jnp.broadcast_to(1.0 / most.astype(jnp.float32), (width, width))
    for part in range(CHUNKS):
        fetch(part).wait()
        for m in range(part * wide // width, (part + 1) * wide // width):
            cols = pl.ds(m * width, width)
            blocks = [in_ref[b, :, cols].astype(jnp.float32).T.astype(jnp.bfloat16) for b in range(3)]
            blocks.append(encode(taps_ref[:, cols].T, inverse))
            edge = jnp.zeros((8, width), jnp.float32)
            for i, (at, stream, down) in enumerate(
                ((width - 16, 1, 2), (width - 16, 2, 4), (0, 1, 4), (0, 2, 6))
            ):
                end = in_ref[stream, pl.ds(at, 16), cols].astype(jnp.float32)
                end = pltpu.roll(end[8:] if at else end[:8], down, 0)
                edge = jnp.where(row // 2 == i, end, edge)
            for h in range(some):
                d = m * some + h
                at = slice(h * chans, (h + 1) * chans)
                query_ref[d] = blocks[0][at]
                for b in range(3):
                    out_ref[d, pl.ds(b * chans, chans), :] = blocks[b + 1][at]
                turned = pltpu.roll(edge, (some - 1 - h) * chans, 1) if h < some - 1 else edge
                tile = jnp.where(group == some - 1, turned, mark)
                out_ref[d, pl.ds(3 * chans, 8), :] = tile.astype(jnp.bfloat16)
        for copy in puts(part):
            copy.start()
    for part in range(CHUNKS):
        for copy in puts(part):
            copy.wait()


def collect(inputs, taps, count):
    rows, total = taps.shape
    chans = total // count
    outs = (bf16(count, 3 * chans + 8, rows), bf16(count, chans, rows))
    return pl.pallas_call(
        collect_kernel,
        name="collect",
        out_shape=outs,
        in_specs=[hbm(), hbm()],
        out_specs=(hbm(), hbm()),
        scratch_shapes=room(inputs, taps, *outs) + [pltpu.SemaphoreType.DMA((4, CHUNKS))],
        cost_estimate=estimate(5),
        compiler_params=params(60),
    )(inputs, taps)


def project_kernel(which_ref, own_w, other_w, own_ref, other_ref, query_ref, out_ref, grad, peak):
    step = pl.program_id(0)
    rows, width = own_w.shape[0], own_ref.shape[0]
    count, chans, _ = query_ref.shape

    def part(a, b):
        return lax.dot_general(
            a[...], b[...], (((1,), (1,)), ((), ())), preferred_element_type=jnp.float32
        )

    block = part(own_w, own_ref) + part(other_w, other_ref)
    grad[pl.ds(pl.multiple_of(step * rows, rows), rows), :] = block
    most = jnp.max(jnp.abs(block), axis=0, keepdims=True)

    @pl.when(step == 0)
    def _():
        peak[...] = jnp.broadcast_to(most, peak.shape)

    @pl.when(step > 0)
    def _():
        peak[...] = jnp.maximum(peak[...], most)

    @pl.when(step == pl.num_programs(0) - 1)
    def _():
        most = jnp.max(peak[...], axis=1, keepdims=True)
        most = jnp.maximum(most * (1.0 + 2.0**-7), 2.0**-100).astype(jnp.bfloat16)
        mark = jnp.broadcast_to(most, (8, width))
        inverse = jnp.broadcast_to(1.0 / most[:1].astype(jnp.float32), (chans, width))

        def fill(i, carry):
            for u in range(UNROLL):
                d = i * UNROLL + u
                out_ref[d, pl.ds(0, chans), :] = query_ref[d]
                out_ref[d, pl.ds(chans, chans), :] = encode(grad[row_of(d, chans), :], inverse)
                out_ref[d, pl.ds(2 * chans, 8), :] = mark
            return carry

        lax.fori_loop(0, count // UNROLL, fill, 0)


def project(which, w_out, own, other, query):
    count, chans, rows = query.shape
    depth = own.shape[1]
    tile = 256
    whole = lambda shape: pl.BlockSpec(shape, lambda i, which: (0,) * len(shape))
    return pl.pallas_call(
        project_kernel,
        name="project",
        grid_spec=pltpu.PrefetchScalarGridSpec(
            num_scalar_prefetch=1,
            grid=(w_out.shape[0] // tile,),
            in_specs=[
                pl.BlockSpec((tile, depth), lambda i, which: (i, which[0])),
                pl.BlockSpec((tile, depth), lambda i, which: (i, 1 - which[0])),
                whole(own.shape),
                whole(other.shape),
                whole(query.shape),
            ],
            out_specs=whole((count, 2 * chans + 8, rows)),
            scratch_shapes=[
                pltpu.VMEM((count * chans, rows), jnp.float32),
                pltpu.VMEM((8, rows), jnp.float32),
            ],
        ),
        out_shape=bf16(count, 2 * chans + 8, rows),
        cost_estimate=estimate(PROJECT_US),
        compiler_params=params(40),
    )(which, w_out, w_out, own, other, query)


def regroup(x):
    return lax.all_to_all(x, "ctx", split_axis=0, concat_axis=0, tiled=True)


def shards(inputs, short_weight, taps, w_out, grad_out):
    rows, local = inputs.shape[1], inputs.shape[2]
    count = lax.axis_size("ctx")
    where = lax.axis_index("ctx")
    chans = local // count
    scale = 1.0 / math.sqrt(count * rows)

    streams, query = collect(inputs, taps, count)
    other = lax.ppermute(grad_out, "tp", [(0, 1), (1, 0)])
    streams = regroup(streams)
    which = lax.axis_index("tp").astype(jnp.int32).reshape(1)
    gated = project(which, w_out, grad_out, other, query)
    gated = regroup(gated)

    weight = lax.dynamic_slice_in_dim(short_weight, where * chans, chans, axis=2)
    weight = jnp.broadcast_to(weight.reshape(9, chans, 1), (9, chans, rows))

    consts = [jnp.asarray(t) for t in tables(count, rows)]
    mixed, filt, prod, conv, lag = stage_one(streams, weight, consts, scale)
    back = stage_two(gated, streams, mixed, filt, prod, conv, lag, weight, consts, scale)

    back = regroup(back)
    return spread(back, inputs, short_weight)


def solution(mesh):
    return jax.shard_map(
        shards,
        mesh=mesh,
        in_specs=(
            P(None, "ctx", "tp"),
            P(None, None, "tp"),
            P("ctx", "tp"),
            P("tp", None),
            P("ctx", "tp"),
        ),
        out_specs=(P(None, "ctx", "tp"), P("ctx", "tp"), P(None, None, "tp")),
        check_vma=False,
    )
```
